128 devices in a mesh: lat: 8 (over y_lo, x), lon: 16 (over z, y_hi, core).
Axes of the slice: x: 4, y: 4 (y_hi: 2, y_lo: 2; y = y_hi * 2 + y_lo), z: 4, core: 2. Of those that a mesh axis runs over, the one named last changes fastest.
Arguments:
- block_input: float32 [192, 384, 384], P('lat', 'lon'), may hold values from -90 to 90, as said below
- cotangent: float32 [192, 384, 384], P('lat', 'lon'), may hold values from -6 to 6
- weights: float32 [1769472], replicated, may hold values from -4 to 4, as said below
- first_moment: float32 [1769472], P(('lat', 'lon')), may hold values from -3 to 3
- second_moment: float32 [1769472], P(('lat', 'lon')), may hold values from 0.05 to 2
- bias_table: float32 [12, 529], replicated, may hold values from -5 to 5
- bias_index: int32 [144, 144], replicated, may hold values from 0 to 528
- region_ids: int32 [192, 384], P('lat', 'lon'), may hold values from 0 to 2
Outputs:
- grad_input: float32 [192, 384, 384], P('lat', 'lon')
- weights_new: float32 [1769472], replicated
- first_new: float32 [1769472], P(('lat', 'lon'))
- second_new: float32 [1769472], P(('lat', 'lon'))
- table_grad: float32 [12, 529], replicated
The draws below stay inside these ranges and needn't reach their ends.
Inputs may be any that keep to these rules, and one draw needn't show every extreme that they name: `block_input`: Tokens' features; real values. `weights`: real values. `region_ids`: entry (r, c) is the region of the token at ((r + 6) mod 192, (c + 6) mod 384) of the input grid.
All inputs are finite; a program needn't handle non-finite values.
Results may differ from the reference program's by a relative error of at most 0.0003.
Values sent between devices are 32-bit elements; how exact they have to be, the bound alone decides.
No kernel may reach another device: no remote copies, remote signals or barrier semaphores. Data moves between devices by JAX's collectives and lax.ppermute only.
A program may use at most 128 MiB of HBM per device.

```python
import math
import jax
import jax.numpy as jnp
from jax import lax

D = 384
HEADS = 12
FF = 1536
WIN = 12
HEAD_DIM = 32
SHIFT = 6
BIAS = 529
NPARAM = 1769472
LAT = 192
LON = 384
TOKENS = 73728


def draw_block_input(key, part):
    streams = jax.random.split(jax.random.fold_in(key, 7), 1)
    sample = jax.random.normal(streams[0], (LAT, LON, D), jnp.float32)
    return jnp.clip(sample, -90.0, 90.0)


def draw_weights(key, part):
    streams = jax.random.split(jax.random.fold_in(key, 13), 6)
    query = jax.random.normal(streams[0], (D, D), jnp.float32) * D ** (-0.5)
    keyed = jax.random.normal(streams[1], (D, D), jnp.float32) * D ** (-0.5)
    valued = jax.random.normal(streams[2], (D, D), jnp.float32) * D ** (-0.5)
    w_proj = jax.random.normal(streams[3], (D, D), jnp.float32) * D ** (-0.5)
    w_up = jax.random.normal(streams[4], (D, FF), jnp.float32) * D ** (-0.5)
    w_down = jax.random.normal(streams[5], (FF, D), jnp.float32) * FF ** (-0.5)
    w_qkv = jnp.concatenate([query, keyed, valued], axis=1)
    packed = jnp.concatenate([w_qkv.reshape(-1), w_proj.reshape(-1), w_up.reshape(-1), w_down.reshape(-1)])
    return jnp.clip(packed, -4.0, 4.0)


def place_ends(drawn, own_key, smallest, largest):
    extent = drawn.shape
    index_at = [jax.random.randint(jax.random.fold_in(own_key, axis), (), 0, extent[axis]) for axis in range(len(extent))]
    drawn = drawn.at[tuple(index_at)].set(smallest)
    longest = extent.index(max(extent))
    index_at[longest] = (index_at[longest] + 1) % extent[longest]
    return drawn.at[tuple(index_at)].set(largest)


def levels(own_key, extent, shards, smallest, largest):
    gain = 1.0
    for axis_at, parts in shards:
        heights = jax.random.uniform(jax.random.fold_in(jax.random.fold_in(own_key, 6), axis_at), (parts,), jnp.float32, smallest / len(shards), largest / len(shards))
        gain = gain * jnp.repeat(jnp.exp(heights), extent[axis_at] // parts).reshape((-1,) + (1,) * (len(extent) - 1 - axis_at))
    return gain


def bell_draw(key, extent, scale, limit, cuts=(), dtype=jnp.bfloat16):
    gain = levels(key, extent, cuts, -0.22, 0.18) if cuts else 1.0
    values = jax.random.normal(key, extent, jnp.float32) * scale * gain
    return jnp.minimum(jnp.maximum(values, -limit), limit).astype(dtype)


def setup_inputs(seed: int = 0) -> dict:
    arg_keys = jax.random.split(jax.random.key(seed), 9)
    block_input = draw_block_input(jax.random.fold_in(arg_keys[8], 71), 0)
    cotangent = bell_draw(arg_keys[1], (LAT, LON, D), 1.0, 6.0, ((0, 8), (1, 16)), jnp.float32)
    weights = draw_weights(jax.random.fold_in(arg_keys[8], 71), 0)
    first_moment = bell_draw(arg_keys[3], (NPARAM,), 0.5, 3.0, ((0, 128),), jnp.float32)
    second_moment = jnp.clip(jnp.exp(math.log(2.0) - 3.6888794 * jax.random.uniform(arg_keys[4], (NPARAM,), jnp.float32) ** levels(arg_keys[4], (NPARAM,), ((0, 128),), -0.2, 0.2)), 0.05, 2.0)
    bias_table = bell_draw(arg_keys[5], (HEADS, BIAS), 1.0, 5.0, (), jnp.float32)
    bias_index = place_ends(jax.random.randint(arg_keys[6], (WIN * WIN, WIN * WIN), 0, BIAS), jax.random.fold_in(arg_keys[6], 1), 0, BIAS - 1).astype(jnp.int32)
    region_ids = place_ends(jax.random.randint(arg_keys[7], (LAT, LON), 0, 3), jax.random.fold_in(arg_keys[7], 1), 0, 2).astype(jnp.int32)
    return dict(block_input=block_input, cotangent=cotangent, weights=weights, first_moment=first_moment, second_moment=second_moment, bias_table=bias_table, bias_index=bias_index, region_ids=region_ids)


precise = lax.Precision.HIGHEST

def normalize(values):
    center = values - lax.optimization_barrier(jnp.mean(values, axis=-1, keepdims=True))
    spread = lax.optimization_barrier(jnp.mean(center * center, axis=-1, keepdims=True))
    return center / jnp.sqrt(spread + 1e-05)

def windows(tensor):
    height, breadth, features = tensor.shape
    blocks = tensor.reshape(height // WIN, WIN, breadth // WIN, WIN, features)
    return blocks.transpose(0, 2, 1, 3, 4).reshape(-1, WIN * WIN, features)

def unwindow(blocks, height, breadth):
    features = blocks.shape[-1]
    tensor = blocks.reshape(height // WIN, breadth // WIN, WIN, WIN, features)
    return tensor.transpose(0, 2, 1, 3, 4).reshape(height, breadth, features)

def unpack(packed):
    first_cut = D * 3 * D
    second_cut = first_cut + D * D
    third_cut = second_cut + D * FF
    return (packed[:first_cut].reshape(D, 3 * D), packed[first_cut:second_cut].reshape(D, D), packed[second_cut:third_cut].reshape(D, FF), packed[third_cut:].reshape(FF, D))

def attend(tensor, w_all, bias_table, bias_index, region_ids, wrapped):
    w_qkv, w_proj, _, _ = unpack(w_all)
    height, breadth, _ = tensor.shape
    flat_rows = normalize(tensor).reshape(-1, D)
    mixed = jnp.dot(flat_rows, w_qkv, precision=precise, preferred_element_type=jnp.float32)
    mixed = windows(mixed.reshape(height, breadth, 3 * D))
    window_count = mixed.shape[0]
    query = mixed[:, :, :D].reshape(window_count, WIN * WIN, HEADS, HEAD_DIM)
    keyed = mixed[:, :, D:2 * D].reshape(window_count, WIN * WIN, HEADS, HEAD_DIM)
    valued = mixed[:, :, 2 * D:].reshape(window_count, WIN * WIN, HEADS, HEAD_DIM)
    scores = jnp.einsum('wihd,wjhd->whij', query, keyed, precision=precise) / math.sqrt(HEAD_DIM)
    scores = scores + jnp.take(bias_table, bias_index, axis=1)[None]
    labels = windows(region_ids[:, :, None])[:, :, 0]
    halves = windows(jnp.broadcast_to(wrapped[:, None, None], (height, breadth, 1)).astype(jnp.int32))[:, :, 0]
    allowed = (labels[:, :, None] == labels[:, None, :]) & (halves[:, :, None] == halves[:, None, :])
    allowed = allowed[:, None]
    masked = jnp.where(allowed, scores, -jnp.inf)
    summit = lax.stop_gradient(lax.optimization_barrier(jnp.max(masked, axis=-1, keepdims=True)))
    raised = jnp.exp(masked - summit)
    probability = raised / lax.optimization_barrier(jnp.sum(raised, axis=-1, keepdims=True))
    context = jnp.einsum('whij,wjhd->wihd', probability, valued, precision=precise)
    context = unwindow(context.reshape(window_count, WIN * WIN, D), height, breadth).reshape(-1, D)
    return jnp.dot(context, w_proj, precision=precise, preferred_element_type=jnp.float32).reshape(height, breadth, D)

def feed(tensor, w_all):
    _, _, w_up, w_down = unpack(w_all)
    flat_rows = normalize(tensor).reshape(-1, D)
    hidden = jax.nn.gelu(jnp.dot(flat_rows, w_up, precision=precise, preferred_element_type=jnp.float32), approximate=True)
    return jnp.dot(hidden, w_down, precision=precise, preferred_element_type=jnp.float32).reshape(tensor.shape)

def reference(block_input, cotangent, weights, first_moment, second_moment, bias_table, bias_index, region_ids):
    wrapped = jnp.arange(LAT) >= LAT - SHIFT

    def forward(tensor, w_all, table):
        moved = jnp.roll(tensor, (-SHIFT, -SHIFT), (0, 1))
        mixed = moved + attend(moved, w_all, table, bias_index, region_ids, wrapped)
        output = mixed + feed(mixed, w_all)
        return jnp.roll(output, (SHIFT, SHIFT), (0, 1))
    _, pullback = jax.vjp(forward, block_input, weights, bias_table)
    grad_input, grad_weights, grad_table = pullback(cotangent)
    factor = 1.0 / math.sqrt(TOKENS)
    grad_weights = grad_weights * factor
    first_new = 0.9 * first_moment + 0.1 * grad_weights
    second_new = 0.95 * second_moment + 0.05 * grad_weights * grad_weights
    weights_new = weights - 0.01 * first_new / (jnp.sqrt(second_new) + 1e-08)
    return (grad_input, weights_new, first_new, second_new, grad_table * factor)
```

```python
import functools
import math

import jax
import jax.numpy as jnp
from jax import lax
from jax.experimental import pallas as pl
from jax.experimental.pallas import tpu as pltpu
from jax.sharding import PartitionSpec as P

D = 384
HEADS = 12
FF = 1536
WIN = 12
SHIFT = 6
WT = WIN * WIN
TILE = 24
TOK = TILE * TILE
WINS = TOK // WT
GROUPS = 3
PER = 4
QKV_ROWS = D * 3 * D // 128
PROJ_ROWS = D * D // 128
MLP_ROWS = D * FF // 128
PROJ_AT = QKV_ROWS
UP_AT = QKV_ROWS + PROJ_ROWS
DOWN_AT = UP_AT + MLP_ROWS
ROWS = DOWN_AT + MLP_ROWS
CHUNK = 256
CHUNKS = FF // CHUNK
HALF = ROWS // 2
OWN = ROWS // 128
BLOCK = OWN + 1
HALF_X = HALF + 64
TABLE_ROWS = 50
BIAS = 529
BOTH = ("lat", "lon")
F32 = jnp.float32
BF16 = jnp.bfloat16
VMEM = pl.BlockSpec(memory_space=pltpu.VMEM)
PARAMS = pltpu.CompilerParams(vmem_limit_bytes=58 * 1024 * 1024)

NN = (((1,), (0,)), ((), ()))
NT = (((1,), (1,)), ((), ()))
TN = (((0,), (0,)), ((), ()))


def split(value):
    high = value.astype(BF16)
    return high, (value - high.astype(F32)).astype(BF16)


def dot(a, b, dims):
    return lax.dot_general(a, b, dims, preferred_element_type=F32)


def dot3(a, b, dims):
    return dot(a[0], b[0], dims) + dot(a[0], b[1], dims) + dot(a[1], b[0], dims)


def unit(value):
    center = value - jnp.mean(value, axis=-1, keepdims=True)
    scale = lax.rsqrt(jnp.mean(center * center, axis=-1, keepdims=True) + 1e-05)
    return center * scale, scale


def unit_back(grad, normed, scale):
    mean = jnp.mean(grad, axis=-1, keepdims=True)
    along = jnp.mean(grad * normed, axis=-1, keepdims=True)
    return scale * (grad - mean - normed * along)


def prepare(flat, table, index, wq_h, wq_l, wp_h, wp_l, wu_h, wu_l, wd_h, wd_l, bias):
    for at, rows, blocks, high, low in (
        (0, D, 9, wq_h, wq_l),
        (PROJ_AT, D, 3, wp_h, wp_l),
    ):
        for b in range(blocks):
            h, l = split(flat[pl.ds(at + b, rows, stride=blocks), :])
            high[:, 128 * b : 128 * b + 128] = h
            low[:, 128 * b : 128 * b + 128] = l
    for f in range(CHUNKS):
        for b in range(2):
            h, l = split(flat[pl.ds(UP_AT + 2 * f + b, D, stride=12), :])
            wu_h[f, :, 128 * b : 128 * b + 128] = h
            wu_l[f, :, 128 * b : 128 * b + 128] = l
        for b in range(3):
            h, l = split(flat[pl.ds(DOWN_AT + 3 * CHUNK * f + b, CHUNK, stride=3), :])
            wd_h[f, :, 128 * b : 128 * b + 128] = h
            wd_l[f, :, 128 * b : 128 * b + 128] = l

    def rows_of(step, carry):
        at = pl.multiple_of(step * 8, 8)
        columns = index[pl.ds(at, 8), :]
        low = columns & 127
        part = columns >> 7
        for h in range(HEADS):
            found = jnp.zeros((8, 256), F32)
            for p in range(5):
                line = jnp.broadcast_to(table[h : h + 1, 128 * p : 128 * p + 128], (8, 128))
                taken = jnp.concatenate(
                    [
                        jnp.take_along_axis(line, low[:, :128], axis=1),
                        jnp.take_along_axis(line, low[:, 128:], axis=1),
                    ],
                    axis=1,
                )
                found = jnp.where(part == p, taken, found)
            bias[h // PER, pl.ds(pl.multiple_of((h % PER) * WT + at, 8), 8), :] = found[:, :WT]
        return carry

    lax.fori_loop(0, WT // 8, rows_of, 0)


def prepared(flat, table, index):
    table = jnp.pad(table, ((0, 4), (0, 640 - BIAS)))
    index = jnp.pad(index, ((0, 0), (0, 256 - WT)))
    shapes = [(D, 3 * D)] * 2 + [(D, D)] * 2 + [(CHUNKS, D, CHUNK)] * 2 + [(CHUNKS, CHUNK, D)] * 2
    return pl.pallas_call(
        prepare,
        out_shape=[jax.ShapeDtypeStruct(s, BF16) for s in shapes]
        + [jax.ShapeDtypeStruct((GROUPS, PER * WT, WT), F32)],
        in_specs=[VMEM] * 3,
        out_specs=[VMEM] * 9,
        compiler_params=PARAMS,
        name="prepare",
    )(flat, table, index)


def gather_windows(target, local, east, south, corner):
    for wr in range(2):
        for wc in range(2):
            for r in range(WIN):
                row = wr * WIN + r
                at = (wr * 2 + wc) * WT + r * WIN
                if row < TILE - SHIFT:
                    near, far, k = local, east, row + SHIFT
                else:
                    near, far, k = south, corner, row - (TILE - SHIFT)
                if wc == 0:
                    target[at : at + WIN, :] = near[k, SHIFT : SHIFT + WIN, :]
                else:
                    target[at : at + SHIFT, :] = near[k, SHIFT + WIN : TILE, :]
                    target[at + SHIFT : at + WIN, :] = far[k, 0:SHIFT, :]


def scatter_windows(source, local, east, south, corner):
    for wr in range(2):
        for wc in range(2):
            for r in range(WIN):
                row = wr * WIN + r
                at = (wr * 2 + wc) * WT + r * WIN
                if row < TILE - SHIFT:
                    near, far, k = local, east, row + SHIFT
                else:
                    near, far, k = south, corner, row - (TILE - SHIFT)
                if wc == 0:
                    near[k, SHIFT : SHIFT + WIN, :] = source[at : at + WIN, :]
                else:
                    near[k, SHIFT + WIN : TILE, :] = source[at : at + SHIFT, :]
                    far[k, 0:SHIFT, :] = source[at + SHIFT : at + WIN, :]


def head_lane():
    return lax.broadcasted_iota(jnp.int32, (WT, 128), 1) >> 5


def stacked(value):
    lane = head_lane()
    return jnp.concatenate([jnp.where(lane == h, value, 0.0) for h in range(PER)], axis=0)


def unstacked(value):
    lane = head_lane()
    total = jnp.where(lane == 0, value[:WT], 0.0)
    for h in range(1, PER):
        total = jnp.where(lane == h, value[h * WT : h * WT + WT], total)
    return total


SCALE = 1.0 / math.sqrt(32.0)


def block_pass(
    x_l, x_e, x_s, x_c, c_l, c_e, c_s, c_c, wq_h, wq_l, wp_h, wp_l, wu_h, wu_l, wd_h, wd_l,
    bias, label_col, label_row,
    grads, dscore, o_l, o_e, o_s, o_c,
    x, cot, qkv, ctx, prob, n2h, n2l, ch, cl, grad, dqkv, dctx,
):
    gather_windows(x, x_l, x_e, x_s, x_c)
    gather_windows(cot, c_l, c_e, c_s, c_c)
    n1 = split(unit(x[...])[0])
    qkv[...] = dot3(n1, (wq_h[...], wq_l[...]), NN)

    def attend(step, carry):
        w, g = step // GROUPS, step % GROUPS
        rows = pl.ds(pl.multiple_of(w * WT, 16), WT)
        lanes = pl.ds(pl.multiple_of(g * 128, 128), 128)
        q = split(stacked(qkv[rows, pl.ds(pl.multiple_of(g * 128, 128), 128)] * SCALE))
        k = split(qkv[rows, pl.ds(pl.multiple_of(D + g * 128, 128), 128)])
        v = split(qkv[rows, pl.ds(pl.multiple_of(2 * D + g * 128, 128), 128)])
        allowed = label_col[w] == label_row[w]
        score = dot3(q, k, NT) + bias[g]
        score = jnp.where(jnp.concatenate([allowed] * PER, axis=0), score, -jnp.inf)
        raised = jnp.exp(score - jnp.max(score, axis=-1, keepdims=True))
        p = raised * (1.0 / jnp.sum(raised, axis=-1, keepdims=True))
        prob[step] = p
        ctx[rows, lanes] = unstacked(dot3(split(p), v, NN))
        return carry

    lax.fori_loop(0, WINS * GROUPS, attend, 0)

    mixed = x[...] + dot3(split(ctx[...]), (wp_h[...], wp_l[...]), NN)
    n2, scale2 = unit(mixed)
    n2h[...], n2l[...] = split(n2)
    ch[...], cl[...] = split(cot[...])
    grad[...] = jnp.zeros_like(grad)

    def feed(f, carry):
        n = (n2h[...], n2l[...])
        c = (ch[...], cl[...])
        up = (wu_h[f], wu_l[f])
        u = dot3(n, up, NN)
        back = dot3(c, (wd_h[f], wd_l[f]), NT)
        inner = 0.7978845608028654 * (u + 0.044715 * u * u * u)
        t = jnp.tanh(inner)
        hidden = split(0.5 * u * (1.0 + t))
        slope = 0.5 * (1.0 + t) + 0.5 * u * (1.0 - t * t) * (
            0.7978845608028654 * (1.0 + 3.0 * 0.044715 * u * u)
        )
        du = split(back * slope)
        gdown = dot3(hidden, c, TN)
        for b in range(3):
            grads[pl.ds(DOWN_AT + 3 * CHUNK * f + b, CHUNK, stride=3), :] = gdown[:, 128 * b : 128 * b + 128]
        gup = dot3(n, du, TN)
        for b in range(2):
            grads[pl.ds(UP_AT + 2 * f + b, D, stride=12), :] = gup[:, 128 * b : 128 * b + 128]
        grad[...] += dot3(du, up, NT)
        return carry

    lax.fori_loop(0, CHUNKS, feed, 0)

    mixed = x[...] + dot3(split(ctx[...]), (wp_h[...], wp_l[...]), NN)
    n2, scale2 = unit(mixed)
    grad[...] = cot[...] + unit_back(grad[...], n2, scale2)
    gm = split(grad[...])
    dctx[...] = dot3(gm, (wp_h[...], wp_l[...]), NT)
    gproj = dot3(split(ctx[...]), gm, TN)
    for b in range(3):
        grads[pl.ds(PROJ_AT + b, D, stride=3), :] = gproj[:, 128 * b : 128 * b + 128]
    dscore[...] = jnp.zeros_like(dscore)

    def attend_back(step, carry):
        w, g = step // GROUPS, step % GROUPS
        rows = pl.ds(pl.multiple_of(w * WT, 16), WT)
        q_at = pl.ds(pl.multiple_of(g * 128, 128), 128)
        k_at = pl.ds(pl.multiple_of(D + g * 128, 128), 128)
        v_at = pl.ds(pl.multiple_of(2 * D + g * 128, 128), 128)
        q = split(stacked(qkv[rows, q_at] * SCALE))
        k = split(qkv[rows, k_at])
        v = split(qkv[rows, v_at])
        d = split(stacked(dctx[rows, q_at]))
        p = prob[step]
        dp = dot3(d, v, NT)
        ds = p * (dp - jnp.sum(dp * p, axis=-1, keepdims=True))
        dscore[g] += ds
        ps, dss = split(p), split(ds)
        dqkv[rows, v_at] = dot3(ps, d, TN)
        dqkv[rows, q_at] = unstacked(dot3(dss, k, NN)) * SCALE
        dqkv[rows, k_at] = dot3(dss, q, TN)
        return carry

    lax.fori_loop(0, WINS * GROUPS, attend_back, 0)

    n1, scale1 = unit(x[...])
    dq = split(dqkv[...])
    gqkv = dot3(split(n1), dq, TN)
    for b in range(9):
        grads[pl.ds(b, D, stride=9), :] = gqkv[:, 128 * b : 128 * b + 128]
    back = dot3(dq, (wq_h[...], wq_l[...]), NT)
    grad[...] += unit_back(back, n1, scale1)
    scatter_windows(grad, o_l, o_e, o_s, o_c)


def run_block(x_parts, c_parts, weights, bias, label_col, label_row):
    halo = [(TILE, TILE, D), (TILE, 8, D), (SHIFT, TILE, D), (SHIFT, 8, D)]
    outs = [(ROWS, 128), (GROUPS, PER * WT, WT)] + halo
    scratch = [
        pltpu.VMEM((TOK, D), F32),
        pltpu.VMEM((TOK, D), F32),
        pltpu.VMEM((TOK, 3 * D), F32),
        pltpu.VMEM((TOK, D), F32),
        pltpu.VMEM((WINS * GROUPS, PER * WT, WT), F32),
        pltpu.VMEM((TOK, D), BF16),
        pltpu.VMEM((TOK, D), BF16),
        pltpu.VMEM((TOK, D), BF16),
        pltpu.VMEM((TOK, D), BF16),
        pltpu.VMEM((TOK, D), F32),
        pltpu.VMEM((TOK, 3 * D), F32),
        pltpu.VMEM((TOK, D), F32),
    ]
    args = (*x_parts, *c_parts, *weights, bias, label_col, label_row)
    return pl.pallas_call(
        block_pass,
        out_shape=[jax.ShapeDtypeStruct(s, F32) for s in outs],
        in_specs=[VMEM] * len(args),
        out_specs=[VMEM] * len(outs),
        scratch_shapes=scratch,
        compiler_params=PARAMS,
        name="block_pass",
    )(*args)


def table_sum(scores, index, out):
    out[...] = jnp.zeros_like(out)
    column = lax.broadcasted_iota(jnp.int32, (128, WT), 0)

    def step(i, carry):
        line = index[i]
        part = line >> 7
        hot = (column == jnp.broadcast_to(line & 127, (128, WT))).astype(F32).astype(BF16)
        high, low = split(scores[i])
        pair = jnp.concatenate([high.astype(F32), low.astype(F32)], axis=0)
        rows = jnp.concatenate([jnp.where(part == p, pair, 0.0) for p in range(5)], axis=0).astype(BF16)
        out[...] += dot(rows, hot, NT)
        return carry

    lax.fori_loop(0, WT, step, 0)


def table_gradient(dscore, index):
    scores = dscore.reshape(HEADS, WT, WT).transpose(1, 0, 2)
    scores = jnp.pad(scores, ((0, 0), (0, 4), (0, 0)))
    sums = pl.pallas_call(
        table_sum,
        out_shape=jax.ShapeDtypeStruct((160, 128), F32),
        in_specs=[VMEM] * 2,
        out_specs=VMEM,
        compiler_params=PARAMS,
        name="table_sum",
    )(scores, index.reshape(WT, 1, WT))
    sums = sums.reshape(5, 2, 16, 128).sum(axis=1)[:, :HEADS]
    return sums.transpose(1, 0, 2).reshape(HEADS, 640)[:, :BIAS]


def chip_order():
    return [(y_lo * 4 + x) * 16 + zy * 2 for y_lo in range(2) for x in range(4) for zy in range(8)]


def chip_groups():
    return [[d + core for d in chip_order()] for core in range(2)]


def core_groups():
    return [[d, d + 1] for d in chip_order()]


def worker_pairs():
    return [(core * 64 + q, d + core) for core in range(2) for q, d in enumerate(chip_order())]


def exchanged(value, groups):
    return lax.all_to_all(value, BOTH, 0, 0, axis_index_groups=groups, tiled=True)


def around(value, axis, by):
    size = lax.axis_size(axis)
    return lax.ppermute(value, axis, [(i, (i + by) % size) for i in range(size)])


def diagonal(value, by):
    lat, lon = lax.axis_size("lat"), lax.axis_size("lon")
    return lax.ppermute(
        value,
        BOTH,
        [
            (a * lon + o, ((a + by) % lat) * lon + (o + by) % lon)
            for a in range(lat)
            for o in range(lon)
        ],
    )


def halo(tile):
    return (
        tile,
        around(tile[:, :8], "lon", -1),
        around(tile[:SHIFT], "lat", -1),
        diagonal(tile[:SHIFT, :8], -1),
    )


def adam(parts, weights, first, second, new, first_new, second_new, factor):
    total = parts[0:BLOCK, :]
    for q in range(1, 64):
        total = total + parts[q * BLOCK : (q + 1) * BLOCK, :]
    total = total * factor
    grad = total[:OWN]
    m = 0.9 * first[...] + 0.1 * grad
    s = 0.95 * second[...] + 0.05 * grad * grad
    first_new[...] = m
    second_new[...] = s
    new[0:OWN, :] = weights[...] - 0.01 * m / (jnp.sqrt(s) + 1e-08)
    new[OWN:BLOCK, :] = total[OWN:BLOCK]


def per_device(
    block_input, cotangent, weights, first_moment, second_moment, bias_table, bias_index, region_ids
):
    lat_at, lon_at = lax.axis_index("lat"), lax.axis_index("lon")
    factor = 1.0 / math.sqrt(TOK * 128)
    flat = weights.reshape(ROWS, 128)
    *pairs, bias = prepared(flat, bias_table, bias_index)
    x_parts = halo(block_input)
    c_parts = halo(cotangent)

    wrapped = (lat_at * TILE + jnp.arange(TILE)) >= TILE * 8 - SHIFT
    labels = region_ids * 2 + wrapped[:, None].astype(jnp.int32)
    labels = labels.reshape(2, WIN, 2, WIN).transpose(0, 2, 1, 3).reshape(WINS, WT)
    grads, dscore, o_l, o_e, o_s, o_c = run_block(
        x_parts, c_parts, pairs, bias, labels[:, :, None], labels[:, None, :]
    )

    from_west = around(o_e, "lon", 1)
    from_north = around(o_s, "lat", 1)
    from_corner = diagonal(o_c, 1)
    top = jnp.concatenate([from_corner[:, :SHIFT], from_north[:, SHIFT:]], axis=1)
    rest = jnp.concatenate([from_west[SHIFT:, :SHIFT], o_l[SHIFT:, SHIFT:]], axis=1)
    grad_input = jnp.concatenate([top, rest], axis=0)

    table = table_gradient(dscore, bias_index).reshape(-1)
    table = jnp.pad(table, (0, 128 * 128 - table.shape[0])).reshape(2, 64, 1, 128)
    sent = jnp.concatenate([grads.reshape(2, 64, OWN, 128), table], axis=2)
    halves = exchanged(sent.reshape(2, 64 * BLOCK, 128), core_groups())
    summed = halves[0] + halves[1]
    parts = exchanged(summed.reshape(64, 1, BLOCK * 128), chip_groups())

    pairs_of = worker_pairs()
    back = [(b, a) for a, b in pairs_of]
    moments = jnp.stack([first_moment.reshape(OWN, 128), second_moment.reshape(OWN, 128)])
    moments = lax.ppermute(moments, BOTH, pairs_of)
    core = lon_at % 2
    shard = core * 64 + lat_at * 8 + lon_at // 2
    own = lax.dynamic_slice_in_dim(flat, shard * OWN, OWN, 0)
    new, first_new, second_new = pl.pallas_call(
        functools.partial(adam, factor=factor),
        out_shape=[jax.ShapeDtypeStruct((n, 128), F32) for n in (BLOCK, OWN, OWN)],
        in_specs=[VMEM] * 4,
        out_specs=[VMEM] * 3,
        compiler_params=PARAMS,
        name="adam",
    )(parts.reshape(64 * BLOCK, 128), own, moments[0], moments[1])
    moments = lax.ppermute(jnp.stack([first_new, second_new]), BOTH, back)
    copies = jnp.broadcast_to(new.reshape(1, 1, BLOCK * 128), (64, 1, BLOCK * 128))
    mine = exchanged(copies, chip_groups()).reshape(1, 64 * BLOCK, 128)
    everything = exchanged(jnp.concatenate([mine, mine]), core_groups())
    everything = everything.reshape(128, BLOCK, 128)
    weights_new = everything[:, :OWN].reshape(-1)
    table_new = everything[:, OWN].reshape(-1)[: HEADS * BIAS].reshape(HEADS, BIAS)
    return (
        grad_input,
        weights_new,
        moments[0].reshape(-1),
        moments[1].reshape(-1),
        table_new,
    )


def solution(mesh):
    placed = (
        P("lat", "lon", None),
        P("lat", "lon", None),
        P(),
        P(BOTH),
        P(BOTH),
        P(),
        P(),
        P("lat", "lon"),
    )
    return jax.shard_map(
        per_device,
        mesh=mesh,
        in_specs=placed,
        out_specs=(P("lat", "lon", None), P(), P(BOTH), P(BOTH), P()),
        check_vma=False,
    )
```

```python
import functools
import math

import jax
import jax.numpy as jnp
from jax import lax
from jax.experimental import pallas as pl
from jax.experimental.pallas import tpu as pltpu
from jax.sharding import PartitionSpec as P

D = 384
HEADS = 12
FF = 1536
WIN = 12
SHIFT = 6
WT = WIN * WIN
TILE = 24
TOK = TILE * TILE
WINS = TOK // WT
GROUPS = 3
PER = 4
QKV_ROWS = D * 3 * D // 128
PROJ_ROWS = D * D // 128
MLP_ROWS = D * FF // 128
PROJ_AT = QKV_ROWS
UP_AT = QKV_ROWS + PROJ_ROWS
DOWN_AT = UP_AT + MLP_ROWS
ROWS = DOWN_AT + MLP_ROWS
CHUNK = 256
CHUNKS = FF // CHUNK
HALF = ROWS // 2
OWN = ROWS // 128
BLOCK = OWN + 1
BIAS = 529
BOTH = ("lat", "lon")
F32 = jnp.float32
BF16 = jnp.bfloat16
VMEM = pl.BlockSpec(memory_space=pltpu.VMEM)
PARAMS = pltpu.CompilerParams(vmem_limit_bytes=58 * 1024 * 1024)

NN = (((1,), (0,)), ((), ()))
NT = (((1,), (1,)), ((), ()))
TN = (((0,), (0,)), ((), ()))


def split(value):
    high = value.astype(BF16)
    return high, (value - high.astype(F32)).astype(BF16)


def dot(a, b, dims):
    return lax.dot_general(a, b, dims, preferred_element_type=F32)


def dot3(a, b, dims):
    return dot(a[0], b[0], dims) + dot(a[0], b[1], dims) + dot(a[1], b[0], dims)


def unit(value):
    center = value - jnp.mean(value, axis=-1, keepdims=True)
    scale = lax.rsqrt(jnp.mean(center * center, axis=-1, keepdims=True) + 1e-05)
    return center * scale, scale


def unit_back(grad, normed, scale):
    mean = jnp.mean(grad, axis=-1, keepdims=True)
    along = jnp.mean(grad * normed, axis=-1, keepdims=True)
    return scale * (grad - mean - normed * along)


def prepare(flat, table, index, wq_h, wq_l, wp_h, wp_l, wu_h, wu_l, wd_h, wd_l, bias):
    for at, rows, blocks, high, low in (
        (0, D, 9, wq_h, wq_l),
        (PROJ_AT, D, 3, wp_h, wp_l),
    ):
        for b in range(blocks):
            h, l = split(flat[pl.ds(at + b, rows, stride=blocks), :])
            high[:, 128 * b : 128 * b + 128] = h
            low[:, 128 * b : 128 * b + 128] = l
    for f in range(CHUNKS):
        for b in range(2):
            h, l = split(flat[pl.ds(UP_AT + 2 * f + b, D, stride=12), :])
            wu_h[f, :, 128 * b : 128 * b + 128] = h
            wu_l[f, :, 128 * b : 128 * b + 128] = l
        for b in range(3):
            h, l = split(flat[pl.ds(DOWN_AT + 3 * CHUNK * f + b, CHUNK, stride=3), :])
            wd_h[f, :, 128 * b : 128 * b + 128] = h
            wd_l[f, :, 128 * b : 128 * b + 128] = l

    lines = jnp.concatenate([table[...], jnp.zeros((HEADS, 640 - BIAS), F32)], axis=1)

    def rows_of(step, carry):
        at = pl.multiple_of(step * 8, 8)
        columns = index[pl.ds(at, 8), :]
        columns = jnp.concatenate([columns, jnp.zeros((8, 256 - WT), jnp.int32)], axis=1)
        low = columns & 127
        part = columns >> 7
        for h in range(HEADS):
            found = jnp.zeros((8, 256), F32)
            for p in range(5):
                line = jnp.broadcast_to(lines[h : h + 1, 128 * p : 128 * p + 128], (8, 128))
                taken = jnp.concatenate(
                    [
                        jnp.take_along_axis(line, low[:, :128], axis=1),
                        jnp.take_along_axis(line, low[:, 128:], axis=1),
                    ],
                    axis=1,
                )
                found = jnp.where(part == p, taken, found)
            bias[h // PER, pl.ds(pl.multiple_of((h % PER) * WT + at, 8), 8), :] = found[:, :WT]
        return carry

    lax.fori_loop(0, WT // 8, rows_of, 0)


def prepared(flat, table, index):
    shapes = [(D, 3 * D)] * 2 + [(D, D)] * 2 + [(CHUNKS, D, CHUNK)] * 2 + [(CHUNKS, CHUNK, D)] * 2
    return pl.pallas_call(
        prepare,
        out_shape=[jax.ShapeDtypeStruct(s, BF16) for s in shapes]
        + [jax.ShapeDtypeStruct((GROUPS, PER * WT, WT), F32)],
        in_specs=[VMEM] * 3,
        out_specs=[VMEM] * 9,
        compiler_params=PARAMS,
        name="prepare",
    )(flat, table, index)


def gather_windows(target, local, east, south, corner):
    for wr in range(2):
        for wc in range(2):
            for r in range(WIN):
                row = wr * WIN + r
                at = (wr * 2 + wc) * WT + r * WIN
                if row < TILE - SHIFT:
                    near, far, k = local, east, row + SHIFT
                else:
                    near, far, k = south, corner, row - (TILE - SHIFT)
                if wc == 0:
                    target[at : at + WIN, :] = near[k, SHIFT : SHIFT + WIN, :]
                else:
                    target[at : at + SHIFT, :] = near[k, SHIFT + WIN : TILE, :]
                    target[at + SHIFT : at + WIN, :] = far[k, 0:SHIFT, :]


def scatter_windows(source, local, east, south, corner):
    for wr in range(2):
        for wc in range(2):
            for r in range(WIN):
                row = wr * WIN + r
                at = (wr * 2 + wc) * WT + r * WIN
                if row < TILE - SHIFT:
                    near, far, k = local, east, row + SHIFT
                else:
                    near, far, k = south, corner, row - (TILE - SHIFT)
                if wc == 0:
                    near[k, SHIFT : SHIFT + WIN, :] = source[at : at + WIN, :]
                else:
                    near[k, SHIFT + WIN : TILE, :] = source[at : at + SHIFT, :]
                    far[k, 0:SHIFT, :] = source[at + SHIFT : at + WIN, :]


def head_lane():
    return lax.broadcasted_iota(jnp.int32, (WT, 128), 1) >> 5


def stacked(value):
    lane = head_lane()
    return jnp.concatenate([jnp.where(lane == h, value, 0.0) for h in range(PER)], axis=0)


def unstacked(value):
    lane = head_lane()
    total = jnp.where(lane == 0, value[:WT], 0.0)
    for h in range(1, PER):
        total = jnp.where(lane == h, value[h * WT : h * WT + WT], total)
    return total


def find_labels(region, last, label_row, label_col):
    eye = lax.broadcasted_iota(jnp.int32, (WT, WT), 0) == lax.broadcasted_iota(jnp.int32, (WT, WT), 1)
    for wr in range(2):
        for wc in range(2):
            w = wr * 2 + wc
            pieces = []
            for r in range(WIN):
                row = wr * WIN + r
                ids = region[row : row + 1, wc * WIN : wc * WIN + WIN]
                pieces.append(ids + (4 * last if row >= TILE - SHIFT else 0))
            line = jnp.concatenate(pieces, axis=1).astype(F32)
            label_row[w] = line
            wide = jnp.where(eye, jnp.broadcast_to(line, (WT, WT)), 0.0)
            label_col[w] = jnp.sum(wide, axis=1, keepdims=True)


SCALE = 1.0 / math.sqrt(32.0)


def block_pass(
    x_l, x_e, x_s, x_c, c_l, c_e, c_s, c_c, wq_h, wq_l, wp_h, wp_l, wu_h, wu_l, wd_h, wd_l,
    bias, region, place,
    keep, send, dscore, o_l, o_e, o_s, o_c,
    x, cot, qkv, ctx, prob, n2h, n2l, ch, cl, grad, dqkv, dctx, grads, label_row, label_col, sems,
):
    find_labels(region, place[1], label_row, label_col)
    gather_windows(x, x_l, x_e, x_s, x_c)
    gather_windows(cot, c_l, c_e, c_s, c_c)
    n1 = split(unit(x[...])[0])
    qkv[...] = dot3(n1, (wq_h[...], wq_l[...]), NN)

    def attend(step, carry):
        w, g = step // GROUPS, step % GROUPS
        rows = pl.ds(pl.multiple_of(w * WT, 16), WT)
        lanes = pl.ds(pl.multiple_of(g * 128, 128), 128)
        q = split(stacked(qkv[rows, pl.ds(pl.multiple_of(g * 128, 128), 128)] * SCALE))
        k = split(qkv[rows, pl.ds(pl.multiple_of(D + g * 128, 128), 128)])
        v = split(qkv[rows, pl.ds(pl.multiple_of(2 * D + g * 128, 128), 128)])
        allowed = label_col[w] == label_row[w]
        score = dot3(q, k, NT) + bias[g]
        score = jnp.where(jnp.concatenate([allowed] * PER, axis=0), score, -jnp.inf)
        raised = jnp.exp(score - jnp.max(score, axis=-1, keepdims=True))
        p = raised * (1.0 / jnp.sum(raised, axis=-1, keepdims=True))
        prob[step] = p
        ctx[rows, lanes] = unstacked(dot3(split(p), v, NN))
        return carry

    lax.fori_loop(0, WINS * GROUPS, attend, 0)

    mixed = x[...] + dot3(split(ctx[...]), (wp_h[...], wp_l[...]), NN)
    n2, scale2 = unit(mixed)
    n2h[...], n2l[...] = split(n2)
    ch[...], cl[...] = split(cot[...])
    grad[...] = jnp.zeros_like(grad)

    def feed(f, carry):
        n = (n2h[...], n2l[...])
        c = (ch[...], cl[...])
        up = (wu_h[f], wu_l[f])
        u = dot3(n, up, NN)
        back = dot3(c, (wd_h[f], wd_l[f]), NT)
        inner = 0.7978845608028654 * (u + 0.044715 * u * u * u)
        t = jnp.tanh(inner)
        hidden = split(0.5 * u * (1.0 + t))
        slope = 0.5 * (1.0 + t) + 0.5 * u * (1.0 - t * t) * (
            0.7978845608028654 * (1.0 + 3.0 * 0.044715 * u * u)
        )
        du = split(back * slope)
        gdown = dot3(hidden, c, TN)
        for b in range(3):
            grads[pl.ds(DOWN_AT + 3 * CHUNK * f + b, CHUNK, stride=3), :] = gdown[:, 128 * b : 128 * b + 128]
        gup = dot3(n, du, TN)
        for b in range(2):
            grads[pl.ds(UP_AT + 2 * f + b, D, stride=12), :] = gup[:, 128 * b : 128 * b + 128]
        grad[...] += dot3(du, up, NT)
        return carry

    lax.fori_loop(0, CHUNKS, feed, 0)

    mixed = x[...] + dot3(split(ctx[...]), (wp_h[...], wp_l[...]), NN)
    n2, scale2 = unit(mixed)
    grad[...] = cot[...] + unit_back(grad[...], n2, scale2)
    gm = split(grad[...])
    dctx[...] = dot3(gm, (wp_h[...], wp_l[...]), NT)
    gproj = dot3(split(ctx[...]), gm, TN)
    for b in range(3):
        grads[pl.ds(PROJ_AT + b, D, stride=3), :] = gproj[:, 128 * b : 128 * b + 128]
    dscore[...] = jnp.zeros_like(dscore)

    def attend_back(step, carry):
        w, g = step // GROUPS, step % GROUPS
        rows = pl.ds(pl.multiple_of(w * WT, 16), WT)
        q_at = pl.ds(pl.multiple_of(g * 128, 128), 128)
        k_at = pl.ds(pl.multiple_of(D + g * 128, 128), 128)
        v_at = pl.ds(pl.multiple_of(2 * D + g * 128, 128), 128)
        q = split(stacked(qkv[rows, q_at] * SCALE))
        k = split(qkv[rows, k_at])
        v = split(qkv[rows, v_at])
        d = split(stacked(dctx[rows, q_at]))
        p = prob[step]
        dp = dot3(d, v, NT)
        ds = p * (dp - jnp.sum(dp * p, axis=-1, keepdims=True))
        dscore[g] += ds
        ps, dss = split(p), split(ds)
        dqkv[rows, v_at] = dot3(ps, d, TN)
        dqkv[rows, q_at] = unstacked(dot3(dss, k, NN)) * SCALE
        dqkv[rows, k_at] = dot3(dss, q, TN)
        return carry

    lax.fori_loop(0, WINS * GROUPS, attend_back, 0)

    n1, scale1 = unit(x[...])
    dq = split(dqkv[...])
    gqkv = dot3(split(n1), dq, TN)
    for b in range(9):
        grads[pl.ds(b, D, stride=9), :] = gqkv[:, 128 * b : 128 * b + 128]
    back = dot3(dq, (wq_h[...], wq_l[...]), NT)
    grad[...] += unit_back(back, n1, scale1)
    core = place[0]
    out = pltpu.make_async_copy(
        grads.at[pl.ds(pl.multiple_of((1 - core) * HALF, 8), HALF)], send, sems.at[0]
    )
    stay = pltpu.make_async_copy(
        grads.at[pl.ds(pl.multiple_of(core * HALF, 8), HALF)], keep, sems.at[1]
    )
    out.start()
    stay.start()
    scatter_windows(grad, o_l, o_e, o_s, o_c)
    out.wait()
    stay.wait()


def run_block(x_parts, c_parts, weights, bias, region, place):
    halo = [(TILE, TILE, D), (TILE, 8, D), (SHIFT, TILE, D), (SHIFT, 8, D)]
    outs = [(HALF, 128), (HALF, 128), (GROUPS, PER * WT, WT)] + halo
    whole = pl.BlockSpec(memory_space=pl.ANY)
    scratch = [
        pltpu.VMEM((TOK, D), F32),
        pltpu.VMEM((TOK, D), F32),
        pltpu.VMEM((TOK, 3 * D), F32),
        pltpu.VMEM((TOK, D), F32),
        pltpu.VMEM((WINS * GROUPS, PER * WT, WT), F32),
        pltpu.VMEM((TOK, D), BF16),
        pltpu.VMEM((TOK, D), BF16),
        pltpu.VMEM((TOK, D), BF16),
        pltpu.VMEM((TOK, D), BF16),
        pltpu.VMEM((TOK, D), F32),
        pltpu.VMEM((TOK, 3 * D), F32),
        pltpu.VMEM((TOK, D), F32),
        pltpu.VMEM((ROWS, 128), F32),
        pltpu.VMEM((WINS, 1, WT), F32),
        pltpu.VMEM((WINS, WT, 1), F32),
        pltpu.SemaphoreType.DMA((2,)),
    ]
    args = (*x_parts, *c_parts, *weights, bias, region, place)
    return pl.pallas_call(
        block_pass,
        out_shape=[jax.ShapeDtypeStruct(s, F32) for s in outs],
        in_specs=[VMEM] * (len(args) - 1) + [pl.BlockSpec(memory_space=pltpu.SMEM)],
        out_specs=[whole] * 2 + [VMEM] * (len(outs) - 2),
        scratch_shapes=scratch,
        compiler_params=PARAMS,
        name="block_pass",
    )(*args)


def table_sum(scores, index, out, sums):
    sums[...] = jnp.zeros_like(sums)
    column = lax.broadcasted_iota(jnp.int32, (128, WT), 0)

    def one(i):
        line = index[pl.ds(i, 1), :]
        part = jnp.broadcast_to(line >> 7, (16, WT))
        hot = (column == jnp.broadcast_to(line & 127, (128, WT))).astype(F32).astype(BF16)
        high, low = split(scores[i])
        pieces = []
        for p in range(5):
            here = part == p
            pieces.append(jnp.where(here, high, jnp.zeros_like(high)))
            pieces.append(jnp.where(here, low, jnp.zeros_like(low)))
        return dot(jnp.concatenate(pieces, axis=0), hot, NT)

    def step(k, carry):
        sums[...] += (one(4 * k) + one(4 * k + 1)) + (one(4 * k + 2) + one(4 * k + 3))
        return carry

    lax.fori_loop(0, WT // 4, step, 0)
    out[...] = jnp.zeros_like(out)
    for p in range(5):
        both = sums[32 * p : 32 * p + 16, :] + sums[32 * p + 16 : 32 * p + 32, :]
        out[HEADS * p : HEADS * p + HEADS, :] = both[:HEADS]


def table_gradient(dscore, index):
    scores = dscore.reshape(HEADS, WT, WT).transpose(1, 0, 2)
    scores = jnp.pad(scores, ((0, 0), (0, 4), (0, 0)))
    return pl.pallas_call(
        table_sum,
        out_shape=jax.ShapeDtypeStruct((64, 128), F32),
        in_specs=[VMEM] * 2,
        out_specs=VMEM,
        scratch_shapes=[pltpu.VMEM((160, 128), F32)],
        compiler_params=PARAMS,
        name="table_sum",
    )(scores, index)


def chip_order():
    return [(y_lo * 4 + x) * 16 + zy * 2 for y_lo in range(2) for x in range(4) for zy in range(8)]


def chip_groups():
    return [[d + core for d in chip_order()] for core in range(2)]


def core_swap():
    return [(d, d ^ 1) for d in range(128)]


def worker_pairs():
    return [(core * 64 + q, d + core) for core in range(2) for q, d in enumerate(chip_order())]


def exchanged(value, groups):
    return lax.all_to_all(value, BOTH, 0, 0, axis_index_groups=groups, tiled=True)


def around(value, axis, by):
    size = lax.axis_size(axis)
    return lax.ppermute(value, axis, [(i, (i + by) % size) for i in range(size)])


def diagonal(value, by):
    lat, lon = lax.axis_size("lat"), lax.axis_size("lon")
    return lax.ppermute(
        value,
        BOTH,
        [
            (a * lon + o, ((a + by) % lat) * lon + (o + by) % lon)
            for a in range(lat)
            for o in range(lon)
        ],
    )


def halo(tile):
    return (
        tile,
        around(tile[:, :8], "lon", -1),
        around(tile[:SHIFT], "lat", -1),
        diagonal(tile[:SHIFT, :8], -1),
    )


def merge(keep, came, line, line_came, out):
    for q in range(64):
        rows = slice(q * OWN, q * OWN + OWN)
        out[q, 0:OWN, :] = keep[rows, :] + came[rows, :]
        out[q, OWN:BLOCK, :] = line[q : q + 1, :] + line_came[q : q + 1, :]


def adam(parts, weights, first, second, new, first_new, second_new, factor):
    total = parts[0]
    for q in range(1, 64):
        total = total + parts[q]
    total = total * factor
    grad, line = total[:OWN], total[OWN:]
    m = 0.9 * first[...] + 0.1 * grad
    s = 0.95 * second[...] + 0.05 * grad * grad
    first_new[...] = m
    second_new[...] = s
    fresh = weights[...] - 0.01 * m / (jnp.sqrt(s) + 1e-08)
    for q in range(64):
        new[q, 0:OWN, :] = fresh
        new[q, OWN:BLOCK, :] = line


def lay_out(place, blocks, *refs):
    out = refs[-1]
    for q in range(8):
        out[q * OWN : q * OWN + OWN, :] = blocks[q, 0:OWN, :]


def half_weights(place, blocks, so_far, other):
    def out_at(step, spot):
        half = (1 - spot[0]) if other else spot[0]
        return half * 8 + step, 0

    spec = pl.BlockSpec((8, BLOCK, 128), lambda step, spot: (step, 0, 0))
    more = [] if so_far is None else [so_far]
    return pl.pallas_call(
        lay_out,
        out_shape=jax.ShapeDtypeStruct((ROWS, 128), F32),
        grid_spec=pltpu.PrefetchScalarGridSpec(
            num_scalar_prefetch=1,
            grid=(8,),
            in_specs=[spec] + [pl.BlockSpec(memory_space=pl.ANY)] * len(more),
            out_specs=pl.BlockSpec((8 * OWN, 128), out_at),
        ),
        input_output_aliases={2: 0} if more else {},
        compiler_params=PARAMS,
        name="lay_out_other" if other else "lay_out_own",
    )(place, blocks, *more)


def per_device(
    block_input, cotangent, weights, first_moment, second_moment, bias_table, bias_index, region_ids
):
    lat_at, lon_at = lax.axis_index("lat"), lax.axis_index("lon")
    factor = 1.0 / math.sqrt(TOK * 128)
    flat = weights.reshape(ROWS, 128)
    *pairs, bias = prepared(flat, bias_table, bias_index)
    x_parts = halo(block_input)
    c_parts = halo(cotangent)

    core = lon_at % 2
    place = jnp.stack([core, (lat_at == 7).astype(jnp.int32)]).astype(jnp.int32)
    keep, send, dscore, o_l, o_e, o_s, o_c = run_block(
        x_parts, c_parts, pairs, bias, region_ids, place
    )
    came = lax.ppermute(send, BOTH, core_swap())
    line = table_gradient(dscore, bias_index)
    line_came = lax.ppermute(line, BOTH, core_swap())
    summed = pl.pallas_call(
        merge,
        out_shape=jax.ShapeDtypeStruct((64, BLOCK, 128), F32),
        in_specs=[VMEM] * 4,
        out_specs=VMEM,
        compiler_params=PARAMS,
        name="merge",
    )(keep, came, line, line_came)
    parts = exchanged(summed, chip_groups())

    _, o_e, o_s, o_c, first_moment, second_moment = lax.optimization_barrier(
        (summed, o_e, o_s, o_c, first_moment, second_moment)
    )
    from_west = around(o_e, "lon", 1)
    from_north = around(o_s, "lat", 1)
    from_corner = diagonal(o_c, 1)
    pairs_of = worker_pairs()
    moments = jnp.stack([first_moment.reshape(OWN, 128), second_moment.reshape(OWN, 128)])
    moments = lax.ppermute(moments, BOTH, pairs_of)
    parts, from_west, from_north, from_corner, moments = lax.optimization_barrier(
        (parts, from_west, from_north, from_corner, moments)
    )

    shard = core * 64 + lat_at * 8 + lon_at // 2
    own = lax.dynamic_slice_in_dim(flat, shard * OWN, OWN, 0)
    new, first_new, second_new = pl.pallas_call(
        functools.partial(adam, factor=factor),
        out_shape=[jax.ShapeDtypeStruct(n, F32) for n in ((64, BLOCK, 128), (OWN, 128), (OWN, 128))],
        in_specs=[VMEM] * 4,
        out_specs=[VMEM] * 3,
        compiler_params=PARAMS,
        name="adam",
    )(parts, own, moments[0], moments[1])
    mine = exchanged(new, chip_groups())
    back = [(b, a) for a, b in pairs_of]
    moments = lax.ppermute(jnp.stack([first_new, second_new]), BOTH, back)
    top = jnp.concatenate([from_corner[:, :SHIFT], from_north[:, SHIFT:]], axis=1)
    rest = jnp.concatenate([from_west[SHIFT:, :SHIFT], o_l[SHIFT:, SHIFT:]], axis=1)
    grad_input = jnp.concatenate([top, rest], axis=0)
    mine, moments = lax.optimization_barrier((mine, moments))

    theirs = lax.ppermute(mine, BOTH, core_swap())
    weights_new = half_weights(place, mine, None, False)
    table_new = mine[: HEADS * 5, OWN].reshape(5, HEADS, 128).transpose(1, 0, 2)
    table_new = table_new.reshape(HEADS, 640)[:, :BIAS]
    weights_new = half_weights(place, theirs, weights_new, True)
    return (
        grad_input,
        weights_new.reshape(-1),
        moments[0].reshape(-1),
        moments[1].reshape(-1),
        table_new,
    )


def solution(mesh):
    placed = (
        P("lat", "lon", None),
        P("lat", "lon", None),
        P(),
        P(BOTH),
        P(BOTH),
        P(),
        P(),
        P("lat", "lon"),
    )
    return jax.shard_map(
        per_device,
        mesh=mesh,
        in_specs=placed,
        out_specs=(P("lat", "lon", None), P(), P(BOTH), P(BOTH), P()),
        check_vma=False,
    )
```

```python
import functools
import math

import jax
import jax.numpy as jnp
from jax import lax
from jax.experimental import pallas as pl
from jax.experimental.pallas import tpu as pltpu
from jax.sharding import PartitionSpec as P

D = 384
HEADS = 12
FF = 1536
WIN = 12
SHIFT = 6
WT = WIN * WIN
TILE = 24
TOK = TILE * TILE
WINS = TOK // WT
GROUPS = 3
PER = 4
QKV_ROWS = D * 3 * D // 128
PROJ_ROWS = D * D // 128
MLP_ROWS = D * FF // 128
PROJ_AT = QKV_ROWS
UP_AT = QKV_ROWS + PROJ_ROWS
DOWN_AT = UP_AT + MLP_ROWS
ROWS = DOWN_AT + MLP_ROWS
CHUNK = 256
CHUNKS = FF // CHUNK
HALF = ROWS // 2
OWN = ROWS // 128
BIAS = 529
BOTH = ("lat", "lon")
F32 = jnp.float32
BF16 = jnp.bfloat16
VMEM = pl.BlockSpec(memory_space=pltpu.VMEM)
PARAMS = pltpu.CompilerParams(vmem_limit_bytes=58 * 1024 * 1024)

NN = (((1,), (0,)), ((), ()))
NT = (((1,), (1,)), ((), ()))
TN = (((0,), (0,)), ((), ()))


def split(value):
    high = value.astype(BF16)
    return high, (value - high.astype(F32)).astype(BF16)


def dot(a, b, dims):
    return lax.dot_general(a, b, dims, preferred_element_type=F32)


def dot3(a, b, dims):
    return dot(a[0], b[0], dims) + dot(a[0], b[1], dims) + dot(a[1], b[0], dims)


def unit(value):
    center = value - jnp.mean(value, axis=-1, keepdims=True)
    scale = lax.rsqrt(jnp.mean(center * center, axis=-1, keepdims=True) + 1e-05)
    return center * scale, scale


def unit_back(grad, normed, scale):
    mean = jnp.mean(grad, axis=-1, keepdims=True)
    along = jnp.mean(grad * normed, axis=-1, keepdims=True)
    return scale * (grad - mean - normed * along)


STEPS = 6


def prepare(qkv, proj, up, down, table, index, wq_h, wq_l, wp_h, wp_l, wu_h, wu_l, wd_h, wd_l, bias):
    for flat, rows, blocks, high, low in (
        (qkv, D // STEPS, 9, wq_h, wq_l),
        (proj, D // STEPS, 3, wp_h, wp_l),
        (down, FF // STEPS, 3, wd_h.at[0], wd_l.at[0]),
    ):
        for b in range(blocks):
            h, l = split(flat[pl.ds(b, rows, stride=blocks), :])
            high[:, 128 * b : 128 * b + 128] = h
            low[:, 128 * b : 128 * b + 128] = l
    for f in range(CHUNKS):
        for b in range(2):
            h, l = split(up[pl.ds(2 * f + b, D // STEPS, stride=12), :])
            wu_h[f, :, 128 * b : 128 * b + 128] = h
            wu_l[f, :, 128 * b : 128 * b + 128] = l
    lines = jnp.concatenate([table[...], jnp.zeros((HEADS, 640 - BIAS), F32)], axis=1)
    for k in range(WT // 8 // STEPS):
        at = pl.multiple_of((pl.program_id(0) * (WT // 8 // STEPS) + k) * 8, 8)
        columns = index[pl.ds(at, 8), :]
        columns = jnp.concatenate([columns, jnp.zeros((8, 256 - WT), jnp.int32)], axis=1)
        low = columns & 127
        part = columns >> 7
        for h in range(HEADS):
            found = jnp.zeros((8, 256), F32)
            for p in range(5):
                line = jnp.broadcast_to(lines[h : h + 1, 128 * p : 128 * p + 128], (8, 128))
                taken = jnp.concatenate(
                    [
                        jnp.take_along_axis(line, low[:, :128], axis=1),
                        jnp.take_along_axis(line, low[:, 128:], axis=1),
                    ],
                    axis=1,
                )
                found = jnp.where(part == p, taken, found)
            bias[h // PER, pl.ds(pl.multiple_of((h % PER) * WT + at, 8), 8), :] = found[:, :WT]


def prepared(flat, table, index):
    shapes = [(D, 3 * D)] * 2 + [(D, D)] * 2 + [(CHUNKS, D, CHUNK)] * 2 + [(CHUNKS, CHUNK, D)] * 2
    piece = D // STEPS
    outs = [
        *[pl.BlockSpec((piece, 3 * D), lambda i: (i, 0))] * 2,
        *[pl.BlockSpec((piece, D), lambda i: (i, 0))] * 2,
        *[pl.BlockSpec((CHUNKS, piece, CHUNK), lambda i: (0, i, 0))] * 2,
        *[pl.BlockSpec((1, CHUNK, D), lambda i: (i, 0, 0))] * 2,
        pl.BlockSpec((GROUPS, PER * WT, WT), lambda i: (0, 0, 0)),
    ]

    def part(at, rows):
        return pl.BlockSpec((rows // STEPS, 128), lambda i: (at * STEPS // rows + i, 0))

    return pl.pallas_call(
        prepare,
        out_shape=[jax.ShapeDtypeStruct(s, BF16) for s in shapes]
        + [jax.ShapeDtypeStruct((GROUPS, PER * WT, WT), F32)],
        grid=(STEPS,),
        in_specs=[
            part(0, QKV_ROWS),
            part(PROJ_AT, PROJ_ROWS),
            part(UP_AT, MLP_ROWS),
            part(DOWN_AT, MLP_ROWS),
            pl.BlockSpec((HEADS, BIAS), lambda i: (0, 0)),
            pl.BlockSpec((WT, WT), lambda i: (0, 0)),
        ],
        out_specs=outs,
        compiler_params=PARAMS,
        name="prepare",
    )(flat, flat, flat, flat, table, index)


def gather_windows(target, local, east, south, corner):
    for wr in range(2):
        for wc in range(2):
            for r in range(WIN):
                row = wr * WIN + r
                at = (wr * 2 + wc) * WT + r * WIN
                if row < TILE - SHIFT:
                    near, far, k = local, east, row + SHIFT
                else:
                    near, far, k = south, corner, row - (TILE - SHIFT)
                if wc == 0:
                    target[at : at + WIN, :] = near[k, SHIFT : SHIFT + WIN, :]
                else:
                    target[at : at + SHIFT, :] = near[k, SHIFT + WIN : TILE, :]
                    target[at + SHIFT : at + WIN, :] = far[k, 0:SHIFT, :]


def scatter_windows(source, local, east, south, corner):
    for wr in range(2):
        for wc in range(2):
            for r in range(WIN):
                row = wr * WIN + r
                at = (wr * 2 + wc) * WT + r * WIN
                if row < TILE - SHIFT:
                    near, far, k = local, east, row + SHIFT
                else:
                    near, far, k = south, corner, row - (TILE - SHIFT)
                if wc == 0:
                    near[k, SHIFT : SHIFT + WIN, :] = source[at : at + WIN, :]
                else:
                    near[k, SHIFT + WIN : TILE, :] = source[at : at + SHIFT, :]
                    far[k, 0:SHIFT, :] = source[at + SHIFT : at + WIN, :]


def head_lane():
    return lax.broadcasted_iota(jnp.int32, (WT, 128), 1) >> 5


def stacked(value):
    lane = head_lane()
    return jnp.concatenate([jnp.where(lane == h, value, 0.0) for h in range(PER)], axis=0)


def unstacked(value):
    lane = head_lane()
    total = jnp.where(lane == 0, value[:WT], 0.0)
    for h in range(1, PER):
        total = jnp.where(lane == h, value[h * WT : h * WT + WT], total)
    return total


def find_labels(region, last, label_row, label_col):
    eye = lax.broadcasted_iota(jnp.int32, (WT, WT), 0) == lax.broadcasted_iota(jnp.int32, (WT, WT), 1)
    for wr in range(2):
        for wc in range(2):
            w = wr * 2 + wc
            pieces = []
            for r in range(WIN):
                row = wr * WIN + r
                ids = region[row : row + 1, wc * WIN : wc * WIN + WIN]
                pieces.append(ids + (4 * last if row >= TILE - SHIFT else 0))
            line = jnp.concatenate(pieces, axis=1).astype(F32)
            label_row[w] = line
            wide = jnp.where(eye, jnp.broadcast_to(line, (WT, WT)), 0.0)
            label_col[w] = jnp.sum(wide, axis=1, keepdims=True)


SCALE = 1.0 / math.sqrt(32.0)


def block_pass(
    x_l, c_l, east, south, corner, wq_h, wq_l, wp_h, wp_l, wu_h, wu_l, wd_h, wd_l,
    bias, region, place,
    keep, send, dscore, o_l, o_e, o_s, o_c,
    x, cot, qkv, ctx, prob, n2h, n2l, ch, cl, grad, dqkv, dctx, grads, label_row, label_col, sems,
):
    find_labels(region, place[1], label_row, label_col)
    gather_windows(x, x_l, east.at[0], south.at[0], corner.at[0])
    gather_windows(cot, c_l, east.at[1], south.at[1], corner.at[1])
    n1 = split(unit(x[...])[0])
    qkv[...] = dot3(n1, (wq_h[...], wq_l[...]), NN)

    def attend(step, carry):
        w, g = step // GROUPS, step % GROUPS
        rows = pl.ds(pl.multiple_of(w * WT, 16), WT)
        lanes = pl.ds(pl.multiple_of(g * 128, 128), 128)
        q = split(stacked(qkv[rows, pl.ds(pl.multiple_of(g * 128, 128), 128)] * SCALE))
        k = split(qkv[rows, pl.ds(pl.multiple_of(D + g * 128, 128), 128)])
        v = split(qkv[rows, pl.ds(pl.multiple_of(2 * D + g * 128, 128), 128)])
        allowed = label_col[w] == label_row[w]
        score = dot3(q, k, NT) + bias[g]
        score = jnp.where(jnp.concatenate([allowed] * PER, axis=0), score, -jnp.inf)
        raised = jnp.exp(score - jnp.max(score, axis=-1, keepdims=True))
        p = raised * (1.0 / jnp.sum(raised, axis=-1, keepdims=True))
        prob[step] = p
        ctx[rows, lanes] = unstacked(dot3(split(p), v, NN))
        return carry

    lax.fori_loop(0, WINS * GROUPS, attend, 0)

    mixed = x[...] + dot3(split(ctx[...]), (wp_h[...], wp_l[...]), NN)
    n2, scale2 = unit(mixed)
    n2h[...], n2l[...] = split(n2)
    ch[...], cl[...] = split(cot[...])
    grad[...] = jnp.zeros_like(grad)

    def feed(f, carry):
        n = (n2h[...], n2l[...])
        c = (ch[...], cl[...])
        up = (wu_h[f], wu_l[f])
        u = dot3(n, up, NN)
        back = dot3(c, (wd_h[f], wd_l[f]), NT)
        inner = 0.7978845608028654 * (u + 0.044715 * u * u * u)
        t = jnp.tanh(inner)
        hidden = split(0.5 * u * (1.0 + t))
        slope = 0.5 * (1.0 + t) + 0.5 * u * (1.0 - t * t) * (
            0.7978845608028654 * (1.0 + 3.0 * 0.044715 * u * u)
        )
        du = split(back * slope)
        gdown = dot3(hidden, c, TN)
        for b in range(3):
            grads[pl.ds(DOWN_AT + 3 * CHUNK * f + b, CHUNK, stride=3), :] = gdown[:, 128 * b : 128 * b + 128]
        gup = dot3(n, du, TN)
        for b in range(2):
            grads[pl.ds(UP_AT + 2 * f + b, D, stride=12), :] = gup[:, 128 * b : 128 * b + 128]
        grad[...] += dot3(du, up, NT)
        return carry

    lax.fori_loop(0, CHUNKS, feed, 0)

    mixed = x[...] + dot3(split(ctx[...]), (wp_h[...], wp_l[...]), NN)
    n2, scale2 = unit(mixed)
    grad[...] = cot[...] + unit_back(grad[...], n2, scale2)
    gm = split(grad[...])
    dctx[...] = dot3(gm, (wp_h[...], wp_l[...]), NT)
    gproj = dot3(split(ctx[...]), gm, TN)
    for b in range(3):
        grads[pl.ds(PROJ_AT + b, D, stride=3), :] = gproj[:, 128 * b : 128 * b + 128]
    dscore[...] = jnp.zeros_like(dscore)

    def attend_back(step, carry):
        w, g = step // GROUPS, step % GROUPS
        rows = pl.ds(pl.multiple_of(w * WT, 16), WT)
        q_at = pl.ds(pl.multiple_of(g * 128, 128), 128)
        k_at = pl.ds(pl.multiple_of(D + g * 128, 128), 128)
        v_at = pl.ds(pl.multiple_of(2 * D + g * 128, 128), 128)
        q = split(stacked(qkv[rows, q_at] * SCALE))
        k = split(qkv[rows, k_at])
        v = split(qkv[rows, v_at])
        d = split(stacked(dctx[rows, q_at]))
        p = prob[step]
        dp = dot3(d, v, NT)
        ds = p * (dp - jnp.sum(dp * p, axis=-1, keepdims=True))
        dscore[g] += ds
        ps, dss = split(p), split(ds)
        dqkv[rows, v_at] = dot3(ps, d, TN)
        dqkv[rows, q_at] = unstacked(dot3(dss, k, NN)) * SCALE
        dqkv[rows, k_at] = dot3(dss, q, TN)
        return carry

    lax.fori_loop(0, WINS * GROUPS, attend_back, 0)

    n1, scale1 = unit(x[...])
    dq = split(dqkv[...])
    gqkv = dot3(split(n1), dq, TN)
    for b in range(9):
        grads[pl.ds(b, D, stride=9), :] = gqkv[:, 128 * b : 128 * b + 128]
    back = dot3(dq, (wq_h[...], wq_l[...]), NT)
    grad[...] += unit_back(back, n1, scale1)
    core = place[0]
    out = pltpu.make_async_copy(
        grads.at[pl.ds(pl.multiple_of((1 - core) * HALF, 8), HALF)], send, sems.at[0]
    )
    stay = pltpu.make_async_copy(
        grads.at[pl.ds(pl.multiple_of(core * HALF, 8), HALF)], keep, sems.at[1]
    )
    out.start()
    stay.start()
    scatter_windows(grad, o_l, o_e, o_s, o_c)
    out.wait()
    stay.wait()


def run_block(tiles, edges, weights, bias, region, place):
    halo = [(TILE, TILE, D), (TILE, 8, D), (SHIFT, TILE, D), (SHIFT, 8, D)]
    outs = [(HALF, 128), (HALF, 128), (GROUPS, PER * WT, WT)] + halo
    whole = pl.BlockSpec(memory_space=pl.ANY)
    scratch = [
        pltpu.VMEM((TOK, D), F32),
        pltpu.VMEM((TOK, D), F32),
        pltpu.VMEM((TOK, 3 * D), F32),
        pltpu.VMEM((TOK, D), F32),
        pltpu.VMEM((WINS * GROUPS, PER * WT, WT), F32),
        pltpu.VMEM((TOK, D), BF16),
        pltpu.VMEM((TOK, D), BF16),
        pltpu.VMEM((TOK, D), BF16),
        pltpu.VMEM((TOK, D), BF16),
        pltpu.VMEM((TOK, D), F32),
        pltpu.VMEM((TOK, 3 * D), F32),
        pltpu.VMEM((TOK, D), F32),
        pltpu.VMEM((ROWS, 128), F32),
        pltpu.VMEM((WINS, 1, WT), F32),
        pltpu.VMEM((WINS, WT, 1), F32),
        pltpu.SemaphoreType.DMA((2,)),
    ]
    args = (*tiles, *edges, *weights, bias, region, place)
    return pl.pallas_call(
        block_pass,
        out_shape=[jax.ShapeDtypeStruct(s, F32) for s in outs],
        in_specs=[VMEM] * (len(args) - 1) + [pl.BlockSpec(memory_space=pltpu.SMEM)],
        out_specs=[whole] * 2 + [VMEM] * (len(outs) - 2),
        scratch_shapes=scratch,
        compiler_params=PARAMS,
        name="block_pass",
    )(*args)


def table_sum(scores, index, out, sums):
    sums[...] = jnp.zeros_like(sums)
    column = lax.broadcasted_iota(jnp.int32, (128, WT), 0)

    def one(i):
        line = index[pl.ds(i, 1), :]
        part = jnp.broadcast_to(line >> 7, (16, WT))
        hot = (column == jnp.broadcast_to(line & 127, (128, WT))).astype(F32).astype(BF16)
        high, low = split(scores[i])
        pieces = []
        for p in range(5):
            here = part == p
            pieces.append(jnp.where(here, high, jnp.zeros_like(high)))
            pieces.append(jnp.where(here, low, jnp.zeros_like(low)))
        return dot(jnp.concatenate(pieces, axis=0), hot, NT)

    def step(k, carry):
        sums[...] += (one(4 * k) + one(4 * k + 1)) + (one(4 * k + 2) + one(4 * k + 3))
        return carry

    lax.fori_loop(0, WT // 4, step, 0)
    out[...] = jnp.zeros_like(out)
    for p in range(5):
        both = sums[32 * p : 32 * p + 16, :] + sums[32 * p + 16 : 32 * p + 32, :]
        out[HEADS * p : HEADS * p + HEADS, :] = both[:HEADS]


def table_gradient(dscore, index):
    scores = dscore.reshape(HEADS, WT, WT).transpose(1, 0, 2)
    scores = jnp.pad(scores, ((0, 0), (0, 4), (0, 0)))
    return pl.pallas_call(
        table_sum,
        out_shape=jax.ShapeDtypeStruct((64, 128), F32),
        in_specs=[VMEM] * 2,
        out_specs=VMEM,
        scratch_shapes=[pltpu.VMEM((160, 128), F32)],
        compiler_params=PARAMS,
        name="table_sum",
    )(scores, index)


def chip_order():
    return [(y_lo * 4 + x) * 16 + zy * 2 for y_lo in range(2) for x in range(4) for zy in range(8)]


def chip_groups():
    return [[d + core for d in chip_order()] for core in range(2)]


def core_swap():
    return [(d, d ^ 1) for d in range(128)]


def worker_pairs():
    return [(core * 64 + q, d + core) for core in range(2) for q, d in enumerate(chip_order())]


def exchanged(value, groups):
    return lax.all_to_all(value, BOTH, 0, 0, axis_index_groups=groups, tiled=True)


def around(value, axis, by):
    size = lax.axis_size(axis)
    return lax.ppermute(value, axis, [(i, (i + by) % size) for i in range(size)])


def diagonal(value, by):
    lat, lon = lax.axis_size("lat"), lax.axis_size("lon")
    return lax.ppermute(
        value,
        BOTH,
        [
            (a * lon + o, ((a + by) % lat) * lon + (o + by) % lon)
            for a in range(lat)
            for o in range(lon)
        ],
    )


def pack(x, c, east, south, corner, sems):
    copies = []
    for i, tile in enumerate((x, c)):
        for j, (rows, cols, out) in enumerate(
            ((TILE, 8, east), (SHIFT, TILE, south), (SHIFT, 8, corner))
        ):
            source = tile.at[pl.ds(0, rows), pl.ds(0, cols)]
            copies.append(pltpu.make_async_copy(source, out.at[i], sems.at[3 * i + j]))
    for copy in copies:
        copy.start()
    for copy in copies:
        copy.wait()


def edges_of(x, c):
    whole = pl.BlockSpec(memory_space=pl.ANY)
    shapes = [(2, TILE, 8, D), (2, SHIFT, TILE, D), (2, SHIFT, 8, D)]
    east, south, corner = pl.pallas_call(
        pack,
        out_shape=[jax.ShapeDtypeStruct(s, F32) for s in shapes],
        in_specs=[whole] * 2,
        out_specs=[whole] * 3,
        scratch_shapes=[pltpu.SemaphoreType.DMA((6,))],
        compiler_params=PARAMS,
        name="pack",
    )(x, c)
    return around(east, "lon", -1), around(south, "lat", -1), diagonal(corner, -1)


def butterfly(value, bit):
    return value + lax.ppermute(value, BOTH, [(d, d ^ bit) for d in range(128)])


def merge(keep, came, out):
    out[...] = keep[...] + came[...]


def adam(parts, weights, first, second, new, first_new, second_new, factor):
    grad = parts[0:OWN, :]
    for q in range(1, 64):
        grad = grad + parts[q * OWN : q * OWN + OWN, :]
    grad = grad * factor
    m = 0.9 * first[...] + 0.1 * grad
    s = 0.95 * second[...] + 0.05 * grad * grad
    first_new[...] = m
    second_new[...] = s
    fresh = weights[...] - 0.01 * m / (jnp.sqrt(s) + 1e-08)
    for q in range(64):
        new[q * OWN : q * OWN + OWN, :] = fresh


def put(other, place, half, *refs):
    out, sem = refs[-2:]
    at = (1 - place[0]) if other else place[0]
    copy = pltpu.make_async_copy(half, out.at[pl.ds(pl.multiple_of(at * HALF, 8), HALF)], sem)
    copy.start()
    copy.wait()


def half_weights(place, half, so_far, other):
    more = [] if so_far is None else [so_far]
    whole = pl.BlockSpec(memory_space=pl.ANY)
    return pl.pallas_call(
        functools.partial(put, other),
        out_shape=jax.ShapeDtypeStruct((ROWS, 128), F32),
        in_specs=[pl.BlockSpec(memory_space=pltpu.SMEM)] + [whole] * (1 + len(more)),
        out_specs=whole,
        scratch_shapes=[pltpu.SemaphoreType.DMA(())],
        input_output_aliases={2: 0} if more else {},
        compiler_params=PARAMS,
        name="put_other" if other else "put_own",
    )(place, half, *more)


def per_device(
    block_input, cotangent, weights, first_moment, second_moment, bias_table, bias_index, region_ids
):
    lat_at, lon_at = lax.axis_index("lat"), lax.axis_index("lon")
    factor = 1.0 / math.sqrt(TOK * 128)
    flat = weights.reshape(ROWS, 128)
    *pairs, bias = prepared(flat, bias_table, bias_index)
    edges = edges_of(block_input, cotangent)
    core = lon_at % 2
    place = jnp.stack([core, (lat_at == 7).astype(jnp.int32)]).astype(jnp.int32)
    keep, send, dscore, o_l, o_e, o_s, o_c = run_block(
        (block_input, cotangent), edges, pairs, bias, region_ids, place
    )
    came = lax.ppermute(send, BOTH, core_swap())
    piece = pl.BlockSpec((HALF // 4, 128), lambda i: (i, 0))
    summed = pl.pallas_call(
        merge,
        out_shape=jax.ShapeDtypeStruct((HALF, 128), F32),
        grid=(4,),
        in_specs=[piece] * 2,
        out_specs=piece,
        compiler_params=PARAMS,
        name="merge",
    )(keep, came)
    parts = exchanged(summed.reshape(64, 1, OWN * 128), chip_groups())

    _, o_e, o_s, o_c, dscore, first_moment, second_moment = lax.optimization_barrier(
        (summed, o_e, o_s, o_c, dscore, first_moment, second_moment)
    )
    from_west = around(o_e, "lon", 1)
    from_north = around(o_s, "lat", 1)
    from_corner = diagonal(o_c, 1)
    pairs_of = worker_pairs()
    moments = jnp.stack([first_moment.reshape(OWN, 128), second_moment.reshape(OWN, 128)])
    moments = lax.ppermute(moments, BOTH, pairs_of)
    table = butterfly(table_gradient(dscore, bias_index), 1)
    parts, from_west, from_north, from_corner, moments, table = lax.optimization_barrier(
        (parts, from_west, from_north, from_corner, moments, table)
    )

    shard = core * 64 + lat_at * 8 + lon_at // 2
    own = lax.dynamic_slice_in_dim(flat, shard * OWN, OWN, 0)
    new, first_new, second_new = pl.pallas_call(
        functools.partial(adam, factor=factor),
        out_shape=[jax.ShapeDtypeStruct((n, 128), F32) for n in (HALF, OWN, OWN)],
        in_specs=[VMEM] * 4,
        out_specs=[VMEM] * 3,
        compiler_params=PARAMS,
        name="adam",
    )(parts.reshape(HALF, 128), own, moments[0], moments[1])
    mine = exchanged(new.reshape(64, 1, OWN * 128), chip_groups())
    back = [(b, a) for a, b in pairs_of]
    _, table, first_new, second_new = lax.optimization_barrier((new, table, first_new, second_new))
    moments = lax.ppermute(jnp.stack([first_new, second_new]), BOTH, back)
    for bit in (2, 4, 8, 16, 32, 64):
        table = butterfly(table, bit)
    top = jnp.concatenate([from_corner[:, :SHIFT], from_north[:, SHIFT:]], axis=1)
    rest = jnp.concatenate([from_west[SHIFT:, :SHIFT], o_l[SHIFT:, SHIFT:]], axis=1)
    grad_input = jnp.concatenate([top, rest], axis=0)
    table_new = (table[: HEADS * 5] * factor).reshape(5, HEADS, 128).transpose(1, 0, 2)
    table_new = table_new.reshape(HEADS, 640)[:, :BIAS]
    mine, moments, table_new = lax.optimization_barrier((mine, moments, table_new))

    mine = mine.reshape(HALF, 128)
    theirs = lax.ppermute(mine, BOTH, core_swap())
    weights_new = half_weights(place, mine, None, False)
    weights_new = half_weights(place, theirs, weights_new, True)
    return (
        grad_input,
        weights_new.reshape(-1),
        moments[0].reshape(-1),
        moments[1].reshape(-1),
        table_new,
    )


def solution(mesh):
    placed = (
        P("lat", "lon", None),
        P("lat", "lon", None),
        P(),
        P(BOTH),
        P(BOTH),
        P(),
        P(),
        P("lat", "lon"),
    )
    return jax.shard_map(
        per_device,
        mesh=mesh,
        in_specs=placed,
        out_specs=(P("lat", "lon", None), P(), P(BOTH), P(BOTH), P()),
        check_vma=False,
    )
```

```python
import functools
import math

import jax
import jax.numpy as jnp
from jax import lax
from jax.experimental import pallas as pl
from jax.experimental.pallas import tpu as pltpu
from jax.sharding import PartitionSpec as P

D = 384
HEADS = 12
FF = 1536
WIN = 12
SHIFT = 6
WT = WIN * WIN
TILE = 24
TOK = TILE * TILE
WINS = TOK // WT
GROUPS = 3
PER = 4
QKV_ROWS = D * 3 * D // 128
PROJ_ROWS = D * D // 128
MLP_ROWS = D * FF // 128
PROJ_AT = QKV_ROWS
UP_AT = QKV_ROWS + PROJ_ROWS
DOWN_AT = UP_AT + MLP_ROWS
ROWS = DOWN_AT + MLP_ROWS
CHUNK = 256
CHUNKS = FF // CHUNK
HALF = ROWS // 2
OWN = ROWS // 128
BLOCK = OWN + 1
BATCH = 16
BIAS = 529
BOTH = ("lat", "lon")
F32 = jnp.float32
BF16 = jnp.bfloat16
VMEM = pl.BlockSpec(memory_space=pltpu.VMEM)
PARAMS = pltpu.CompilerParams(vmem_limit_bytes=58 * 1024 * 1024)

NN = (((1,), (0,)), ((), ()))
NT = (((1,), (1,)), ((), ()))
TN = (((0,), (0,)), ((), ()))


def split(value):
    high = value.astype(BF16)
    return high, (value - high.astype(F32)).astype(BF16)


def dot(a, b, dims):
    return lax.dot_general(a, b, dims, preferred_element_type=F32)


def dot3(a, b, dims):
    return dot(a[0], b[0], dims) + dot(a[0], b[1], dims) + dot(a[1], b[0], dims)


def unit(value):
    center = value - jnp.mean(value, axis=-1, keepdims=True)
    scale = lax.rsqrt(jnp.mean(center * center, axis=-1, keepdims=True) + 1e-05)
    return center * scale, scale


def unit_back(grad, normed, scale):
    mean = jnp.mean(grad, axis=-1, keepdims=True)
    along = jnp.mean(grad * normed, axis=-1, keepdims=True)
    return scale * (grad - mean - normed * along)


STEPS = 6


def prepare(qkv, proj, up, down, table, index, wq_h, wq_l, wp_h, wp_l, wu_h, wu_l, wd_h, wd_l, bias):
    for flat, rows, blocks, high, low in (
        (qkv, D // STEPS, 9, wq_h, wq_l),
        (proj, D // STEPS, 3, wp_h, wp_l),
        (down, FF // STEPS, 3, wd_h.at[0], wd_l.at[0]),
    ):
        for b in range(blocks):
            h, l = split(flat[pl.ds(b, rows, stride=blocks), :])
            high[:, 128 * b : 128 * b + 128] = h
            low[:, 128 * b : 128 * b + 128] = l
    for f in range(CHUNKS):
        for b in range(2):
            h, l = split(up[pl.ds(2 * f + b, D // STEPS, stride=12), :])
            wu_h[f, :, 128 * b : 128 * b + 128] = h
            wu_l[f, :, 128 * b : 128 * b + 128] = l
    lines = jnp.concatenate([table[...], jnp.zeros((HEADS, 640 - BIAS), F32)], axis=1)
    for k in range(WT // 8 // STEPS):
        at = pl.multiple_of((pl.program_id(0) * (WT // 8 // STEPS) + k) * 8, 8)
        columns = index[pl.ds(at, 8), :]
        columns = jnp.concatenate([columns, jnp.zeros((8, 256 - WT), jnp.int32)], axis=1)
        low = columns & 127
        part = columns >> 7
        for h in range(HEADS):
            found = jnp.zeros((8, 256), F32)
            for p in range(5):
                line = jnp.broadcast_to(lines[h : h + 1, 128 * p : 128 * p + 128], (8, 128))
                taken = jnp.concatenate(
                    [
                        jnp.take_along_axis(line, low[:, :128], axis=1),
                        jnp.take_along_axis(line, low[:, 128:], axis=1),
                    ],
                    axis=1,
                )
                found = jnp.where(part == p, taken, found)
            bias[h // PER, pl.ds(pl.multiple_of((h % PER) * WT + at, 8), 8), :] = found[:, :WT]


def prepared(flat, table, index):
    shapes = [(D, 3 * D)] * 2 + [(D, D)] * 2 + [(CHUNKS, D, CHUNK)] * 2 + [(CHUNKS, CHUNK, D)] * 2
    piece = D // STEPS
    outs = [
        *[pl.BlockSpec((piece, 3 * D), lambda i: (i, 0))] * 2,
        *[pl.BlockSpec((piece, D), lambda i: (i, 0))] * 2,
        *[pl.BlockSpec((CHUNKS, piece, CHUNK), lambda i: (0, i, 0))] * 2,
        *[pl.BlockSpec((1, CHUNK, D), lambda i: (i, 0, 0))] * 2,
        pl.BlockSpec((GROUPS, PER * WT, WT), lambda i: (0, 0, 0)),
    ]

    def part(at, rows):
        return pl.BlockSpec((rows // STEPS, 128), lambda i: (at * STEPS // rows + i, 0))

    return pl.pallas_call(
        prepare,
        out_shape=[jax.ShapeDtypeStruct(s, BF16) for s in shapes]
        + [jax.ShapeDtypeStruct((GROUPS, PER * WT, WT), F32)],
        grid=(STEPS,),
        in_specs=[
            part(0, QKV_ROWS),
            part(PROJ_AT, PROJ_ROWS),
            part(UP_AT, MLP_ROWS),
            part(DOWN_AT, MLP_ROWS),
            pl.BlockSpec((HEADS, BIAS), lambda i: (0, 0)),
            pl.BlockSpec((WT, WT), lambda i: (0, 0)),
        ],
        out_specs=outs,
        compiler_params=PARAMS,
        name="prepare",
    )(flat, flat, flat, flat, table, index)


def gather_windows(target, local, east, south, corner):
    for wr in range(2):
        for wc in range(2):
            for r in range(WIN):
                row = wr * WIN + r
                at = (wr * 2 + wc) * WT + r * WIN
                if row < TILE - SHIFT:
                    near, far, k = local, east, row + SHIFT
                else:
                    near, far, k = south, corner, row - (TILE - SHIFT)
                if wc == 0:
                    target[at : at + WIN, :] = near[k, SHIFT : SHIFT + WIN, :]
                else:
                    target[at : at + SHIFT, :] = near[k, SHIFT + WIN : TILE, :]
                    target[at + SHIFT : at + WIN, :] = far[k, 0:SHIFT, :]


def scatter_windows(source, local, east, south, corner):
    for wr in range(2):
        for wc in range(2):
            for r in range(WIN):
                row = wr * WIN + r
                at = (wr * 2 + wc) * WT + r * WIN
                if row < TILE - SHIFT:
                    near, far, k = local, east, row + SHIFT
                else:
                    near, far, k = south, corner, row - (TILE - SHIFT)
                if wc == 0:
                    near[k, SHIFT : SHIFT + WIN, :] = source[at : at + WIN, :]
                else:
                    near[k, SHIFT + WIN : TILE, :] = source[at : at + SHIFT, :]
                    far[k, 0:SHIFT, :] = source[at + SHIFT : at + WIN, :]


def head_lane():
    return lax.broadcasted_iota(jnp.int32, (WT, 128), 1) >> 5


def stacked(value):
    lane = head_lane()
    return jnp.concatenate([jnp.where(lane == h, value, 0.0) for h in range(PER)], axis=0)


def unstacked(value):
    lane = head_lane()
    total = jnp.where(lane == 0, value[:WT], 0.0)
    for h in range(1, PER):
        total = jnp.where(lane == h, value[h * WT : h * WT + WT], total)
    return total


def find_labels(region, last, label_row, label_col):
    eye = lax.broadcasted_iota(jnp.int32, (WT, WT), 0) == lax.broadcasted_iota(jnp.int32, (WT, WT), 1)
    for wr in range(2):
        for wc in range(2):
            w = wr * 2 + wc
            pieces = []
            for r in range(WIN):
                row = wr * WIN + r
                ids = region[row : row + 1, wc * WIN : wc * WIN + WIN]
                pieces.append(ids + (4 * last if row >= TILE - SHIFT else 0))
            line = jnp.concatenate(pieces, axis=1).astype(F32)
            label_row[w] = line
            wide = jnp.where(eye, jnp.broadcast_to(line, (WT, WT)), 0.0)
            label_col[w] = jnp.sum(wide, axis=1, keepdims=True)


SCALE = 1.0 / math.sqrt(32.0)


def block_pass(
    x_l, c_l, east, south, corner, wq_h, wq_l, wp_h, wp_l, wu_h, wu_l, wd_h, wd_l,
    bias, region, place,
    keep, send, dscore, o_l, o_e, o_s, o_c,
    x, cot, qkv, ctx, prob, n2h, n2l, ch, cl, grad, dqkv, dctx, grads, label_row, label_col, sems,
):
    find_labels(region, place[1], label_row, label_col)
    gather_windows(x, x_l, east.at[0], south.at[0], corner.at[0])
    gather_windows(cot, c_l, east.at[1], south.at[1], corner.at[1])
    n1 = split(unit(x[...])[0])
    qkv[...] = dot3(n1, (wq_h[...], wq_l[...]), NN)

    def attend(step, carry):
        w, g = step // GROUPS, step % GROUPS
        rows = pl.ds(pl.multiple_of(w * WT, 16), WT)
        lanes = pl.ds(pl.multiple_of(g * 128, 128), 128)
        q = split(stacked(qkv[rows, pl.ds(pl.multiple_of(g * 128, 128), 128)] * SCALE))
        k = split(qkv[rows, pl.ds(pl.multiple_of(D + g * 128, 128), 128)])
        v = split(qkv[rows, pl.ds(pl.multiple_of(2 * D + g * 128, 128), 128)])
        allowed = label_col[w] == label_row[w]
        score = dot3(q, k, NT) + bias[g]
        score = jnp.where(jnp.concatenate([allowed] * PER, axis=0), score, -jnp.inf)
        raised = jnp.exp(score - jnp.max(score, axis=-1, keepdims=True))
        p = raised * (1.0 / jnp.sum(raised, axis=-1, keepdims=True))
        prob[step] = p
        ctx[rows, lanes] = unstacked(dot3(split(p), v, NN))
        return carry

    lax.fori_loop(0, WINS * GROUPS, attend, 0)

    mixed = x[...] + dot3(split(ctx[...]), (wp_h[...], wp_l[...]), NN)
    n2, scale2 = unit(mixed)
    n2h[...], n2l[...] = split(n2)
    ch[...], cl[...] = split(cot[...])
    grad[...] = jnp.zeros_like(grad)

    def feed(f, carry):
        n = (n2h[...], n2l[...])
        c = (ch[...], cl[...])
        up = (wu_h[f], wu_l[f])
        u = dot3(n, up, NN)
        back = dot3(c, (wd_h[f], wd_l[f]), NT)
        inner = 0.7978845608028654 * (u + 0.044715 * u * u * u)
        t = jnp.tanh(inner)
        hidden = split(0.5 * u * (1.0 + t))
        slope = 0.5 * (1.0 + t) + 0.5 * u * (1.0 - t * t) * (
            0.7978845608028654 * (1.0 + 3.0 * 0.044715 * u * u)
        )
        du = split(back * slope)
        gdown = dot3(hidden, c, TN)
        for b in range(3):
            grads[pl.ds(DOWN_AT + 3 * CHUNK * f + b, CHUNK, stride=3), :] = gdown[:, 128 * b : 128 * b + 128]
        gup = dot3(n, du, TN)
        for b in range(2):
            grads[pl.ds(UP_AT + 2 * f + b, D, stride=12), :] = gup[:, 128 * b : 128 * b + 128]
        grad[...] += dot3(du, up, NT)
        return carry

    lax.fori_loop(0, CHUNKS, feed, 0)

    mixed = x[...] + dot3(split(ctx[...]), (wp_h[...], wp_l[...]), NN)
    n2, scale2 = unit(mixed)
    grad[...] = cot[...] + unit_back(grad[...], n2, scale2)
    gm = split(grad[...])
    dctx[...] = dot3(gm, (wp_h[...], wp_l[...]), NT)
    gproj = dot3(split(ctx[...]), gm, TN)
    for b in range(3):
        grads[pl.ds(PROJ_AT + b, D, stride=3), :] = gproj[:, 128 * b : 128 * b + 128]
    dscore[...] = jnp.zeros_like(dscore)

    def attend_back(step, carry):
        w, g = step // GROUPS, step % GROUPS
        rows = pl.ds(pl.multiple_of(w * WT, 16), WT)
        q_at = pl.ds(pl.multiple_of(g * 128, 128), 128)
        k_at = pl.ds(pl.multiple_of(D + g * 128, 128), 128)
        v_at = pl.ds(pl.multiple_of(2 * D + g * 128, 128), 128)
        q = split(stacked(qkv[rows, q_at] * SCALE))
        k = split(qkv[rows, k_at])
        v = split(qkv[rows, v_at])
        d = split(stacked(dctx[rows, q_at]))
        p = prob[step]
        dp = dot3(d, v, NT)
        ds = p * (dp - jnp.sum(dp * p, axis=-1, keepdims=True))
        dscore[g] += ds
        ps, dss = split(p), split(ds)
        dqkv[rows, v_at] = dot3(ps, d, TN)
        dqkv[rows, q_at] = unstacked(dot3(dss, k, NN)) * SCALE
        dqkv[rows, k_at] = dot3(dss, q, TN)
        return carry

    lax.fori_loop(0, WINS * GROUPS, attend_back, 0)

    n1, scale1 = unit(x[...])
    dq = split(dqkv[...])
    gqkv = dot3(split(n1), dq, TN)
    for b in range(9):
        grads[pl.ds(b, D, stride=9), :] = gqkv[:, 128 * b : 128 * b + 128]
    back = dot3(dq, (wq_h[...], wq_l[...]), NT)
    grad[...] += unit_back(back, n1, scale1)
    core = place[0]
    out = pltpu.make_async_copy(
        grads.at[pl.ds(pl.multiple_of((1 - core) * HALF, 8), HALF)], send, sems.at[0]
    )
    stay = pltpu.make_async_copy(
        grads.at[pl.ds(pl.multiple_of(core * HALF, 8), HALF)], keep, sems.at[1]
    )
    out.start()
    stay.start()
    scatter_windows(grad, o_l, o_e, o_s, o_c)
    out.wait()
    stay.wait()


def run_block(tiles, edges, weights, bias, region, place):
    halo = [(TILE, TILE, D), (TILE, 8, D), (SHIFT, TILE, D), (SHIFT, 8, D)]
    outs = [(HALF, 128), (HALF, 128), (GROUPS, PER * WT, WT)] + halo
    whole = pl.BlockSpec(memory_space=pl.ANY)
    scratch = [
        pltpu.VMEM((TOK, D), F32),
        pltpu.VMEM((TOK, D), F32),
        pltpu.VMEM((TOK, 3 * D), F32),
        pltpu.VMEM((TOK, D), F32),
        pltpu.VMEM((WINS * GROUPS, PER * WT, WT), F32),
        pltpu.VMEM((TOK, D), BF16),
        pltpu.VMEM((TOK, D), BF16),
        pltpu.VMEM((TOK, D), BF16),
        pltpu.VMEM((TOK, D), BF16),
        pltpu.VMEM((TOK, D), F32),
        pltpu.VMEM((TOK, 3 * D), F32),
        pltpu.VMEM((TOK, D), F32),
        pltpu.VMEM((ROWS, 128), F32),
        pltpu.VMEM((WINS, 1, WT), F32),
        pltpu.VMEM((WINS, WT, 1), F32),
        pltpu.SemaphoreType.DMA((2,)),
    ]
    args = (*tiles, *edges, *weights, bias, region, place)
    return pl.pallas_call(
        block_pass,
        out_shape=[jax.ShapeDtypeStruct(s, F32) for s in outs],
        in_specs=[VMEM] * (len(args) - 1) + [pl.BlockSpec(memory_space=pltpu.SMEM)],
        out_specs=[whole] * 2 + [VMEM] * (len(outs) - 2),
        scratch_shapes=scratch,
        compiler_params=PARAMS,
        name="block_pass",
    )(*args)


def table_sum(scores, index, out, sums):
    sums[...] = jnp.zeros_like(sums)
    column = lax.broadcasted_iota(jnp.int32, (128, WT), 0)

    def one(i):
        line = index[pl.ds(i, 1), :]
        part = jnp.broadcast_to(line >> 7, (16, WT))
        hot = (column == jnp.broadcast_to(line & 127, (128, WT))).astype(F32).astype(BF16)
        high, low = split(scores[i])
        pieces = []
        for p in range(5):
            here = part == p
            pieces.append(jnp.where(here, high, jnp.zeros_like(high)))
            pieces.append(jnp.where(here, low, jnp.zeros_like(low)))
        return dot(jnp.concatenate(pieces, axis=0), hot, NT)

    def step(k, carry):
        sums[...] += (one(4 * k) + one(4 * k + 1)) + (one(4 * k + 2) + one(4 * k + 3))
        return carry

    lax.fori_loop(0, WT // 4, step, 0)
    out[...] = jnp.zeros_like(out)
    for p in range(5):
        both = sums[32 * p : 32 * p + 16, :] + sums[32 * p + 16 : 32 * p + 32, :]
        out[HEADS * p : HEADS * p + HEADS, :] = both[:HEADS]


def table_gradient(dscore, index):
    scores = dscore.reshape(HEADS, WT, WT).transpose(1, 0, 2)
    scores = jnp.pad(scores, ((0, 0), (0, 4), (0, 0)))
    return pl.pallas_call(
        table_sum,
        out_shape=jax.ShapeDtypeStruct((64, 128), F32),
        in_specs=[VMEM] * 2,
        out_specs=VMEM,
        scratch_shapes=[pltpu.VMEM((160, 128), F32)],
        compiler_params=PARAMS,
        name="table_sum",
    )(scores, index)


def chip_order():
    return [(y_lo * 4 + x) * 16 + zy * 2 for y_lo in range(2) for x in range(4) for zy in range(8)]


def chip_groups():
    return [[d + core for d in chip_order()] for core in range(2)]


def core_swap():
    return [(d, d ^ 1) for d in range(128)]


def worker_pairs():
    return [(core * 64 + q, d + core) for core in range(2) for q, d in enumerate(chip_order())]


def exchanged(value, groups):
    return lax.all_to_all(value, BOTH, 0, 0, axis_index_groups=groups, tiled=True)


def around(value, axis, by):
    size = lax.axis_size(axis)
    return lax.ppermute(value, axis, [(i, (i + by) % size) for i in range(size)])


def diagonal(value, by):
    lat, lon = lax.axis_size("lat"), lax.axis_size("lon")
    return lax.ppermute(
        value,
        BOTH,
        [
            (a * lon + o, ((a + by) % lat) * lon + (o + by) % lon)
            for a in range(lat)
            for o in range(lon)
        ],
    )


def pack(x_east, x_south, c_east, c_south, east, south, corner):
    for i, (e, t) in enumerate(((x_east, x_south), (c_east, c_south))):
        east[i] = e[...]
        south[i] = t[...]
        corner[i] = t[:, 0:8, :]


def edges_of(x, c):
    east_in = pl.BlockSpec((TILE, 8, D), lambda i: (0, 0, 0))
    south_in = pl.BlockSpec((SHIFT, TILE, D), lambda i: (0, 0, 0))
    shapes = [(2, TILE, 8, D), (2, SHIFT, TILE, D), (2, SHIFT, 8, D)]
    east, south, corner = pl.pallas_call(
        pack,
        out_shape=[jax.ShapeDtypeStruct(s, F32) for s in shapes],
        grid=(1,),
        in_specs=[east_in, south_in] * 2,
        out_specs=[pl.BlockSpec(s, lambda i: (0, 0, 0, 0)) for s in shapes],
        compiler_params=PARAMS,
        name="pack",
    )(x, x, c, c)
    return around(east, "lon", -1), around(south, "lat", -1), diagonal(corner, -1)


def merge(keep, came, line, line_came, out):
    for q in range(BATCH):
        rows = slice(q * OWN, q * OWN + OWN)
        out[q * BLOCK : q * BLOCK + OWN, :] = keep[rows, :] + came[rows, :]
        out[q * BLOCK + OWN : (q + 1) * BLOCK, :] = line[q : q + 1, :] + line_came[q : q + 1, :]


def merged(keep, came, line, line_came):
    halves = pl.BlockSpec((BATCH * OWN, 128), lambda i: (i, 0))
    lines = pl.BlockSpec((BATCH, 128), lambda i: (i, 0))
    return pl.pallas_call(
        merge,
        out_shape=jax.ShapeDtypeStruct((64 * BLOCK, 128), F32),
        grid=(64 // BATCH,),
        in_specs=[halves, halves, lines, lines],
        out_specs=pl.BlockSpec((BATCH * BLOCK, 128), lambda i: (i, 0)),
        compiler_params=PARAMS,
        name="merge",
    )(keep, came, line, line_came)


def adam(parts, weights, first, second, new, first_new, second_new, factor):
    total = parts[0:BLOCK, :]
    for q in range(1, 64):
        total = total + parts[q * BLOCK : q * BLOCK + BLOCK, :]
    total = total * factor
    grad, line = total[:OWN], total[OWN:]
    m = 0.9 * first[...] + 0.1 * grad
    s = 0.95 * second[...] + 0.05 * grad * grad
    first_new[...] = m
    second_new[...] = s
    fresh = weights[...] - 0.01 * m / (jnp.sqrt(s) + 1e-08)
    fresh = jnp.concatenate([fresh, line], axis=0)
    for q in range(64):
        new[q * BLOCK : q * BLOCK + BLOCK, :] = fresh


def lay_out(place, blocks, *refs):
    out = refs[-1]
    for q in range(BATCH):
        out[q * OWN : q * OWN + OWN, :] = blocks[q * BLOCK : q * BLOCK + OWN, :]


def lay_out_own(place, blocks, out, lines):
    lay_out(place, blocks, out)
    for q in range(BATCH):
        lines[q : q + 1, :] = blocks[q * BLOCK + OWN : q * BLOCK + BLOCK, :]


def own_half(place, blocks):
    steps = 64 // BATCH
    return pl.pallas_call(
        lay_out_own,
        out_shape=[jax.ShapeDtypeStruct((ROWS, 128), F32), jax.ShapeDtypeStruct((64, 128), F32)],
        grid_spec=pltpu.PrefetchScalarGridSpec(
            num_scalar_prefetch=1,
            grid=(steps,),
            in_specs=[pl.BlockSpec((BATCH * BLOCK, 128), lambda i, spot: (i, 0))],
            out_specs=[
                pl.BlockSpec((BATCH * OWN, 128), lambda i, spot: (spot[0] * steps + i, 0)),
                pl.BlockSpec((BATCH, 128), lambda i, spot: (i, 0)),
            ],
        ),
        compiler_params=PARAMS,
        name="lay_out_own",
    )(place, blocks)


def other_half(place, blocks, so_far):
    steps = 64 // BATCH
    return pl.pallas_call(
        lay_out,
        out_shape=jax.ShapeDtypeStruct((ROWS, 128), F32),
        grid_spec=pltpu.PrefetchScalarGridSpec(
            num_scalar_prefetch=1,
            grid=(steps,),
            in_specs=[
                pl.BlockSpec((BATCH * BLOCK, 128), lambda i, spot: (i, 0)),
                pl.BlockSpec(memory_space=pl.ANY),
            ],
            out_specs=pl.BlockSpec((BATCH * OWN, 128), lambda i, spot: ((1 - spot[0]) * steps + i, 0)),
        ),
        input_output_aliases={2: 0},
        compiler_params=PARAMS,
        name="lay_out_other",
    )(place, blocks, so_far)


def per_device(
    block_input, cotangent, weights, first_moment, second_moment, bias_table, bias_index, region_ids
):
    lat_at, lon_at = lax.axis_index("lat"), lax.axis_index("lon")
    factor = 1.0 / math.sqrt(TOK * 128)
    flat = weights.reshape(ROWS, 128)
    *pairs, bias = prepared(flat, bias_table, bias_index)
    edges = edges_of(block_input, cotangent)
    core = lon_at % 2
    place = jnp.stack([core, (lat_at == 7).astype(jnp.int32)]).astype(jnp.int32)
    keep, send, dscore, o_l, o_e, o_s, o_c = run_block(
        (block_input, cotangent), edges, pairs, bias, region_ids, place
    )
    came = lax.ppermute(send, BOTH, core_swap())
    line = table_gradient(dscore, bias_index)
    line_came = lax.ppermute(line, BOTH, core_swap())
    summed = merged(keep, came, line, line_came)
    parts = exchanged(summed.reshape(64, 1, BLOCK * 128), chip_groups())

    _, o_e, o_s, o_c, first_moment, second_moment = lax.optimization_barrier(
        (summed, o_e, o_s, o_c, first_moment, second_moment)
    )
    from_west = around(o_e, "lon", 1)
    from_north = around(o_s, "lat", 1)
    from_corner = diagonal(o_c, 1)
    pairs_of = worker_pairs()
    moments = jnp.stack([first_moment.reshape(OWN, 128), second_moment.reshape(OWN, 128)])
    moments = lax.ppermute(moments, BOTH, pairs_of)
    parts, from_west, from_north, from_corner, moments = lax.optimization_barrier(
        (parts, from_west, from_north, from_corner, moments)
    )

    shard = core * 64 + lat_at * 8 + lon_at // 2
    own = lax.dynamic_slice_in_dim(flat, shard * OWN, OWN, 0)
    new, first_new, second_new = pl.pallas_call(
        functools.partial(adam, factor=factor),
        out_shape=[jax.ShapeDtypeStruct((n, 128), F32) for n in (64 * BLOCK, OWN, OWN)],
        in_specs=[VMEM] * 4,
        out_specs=[VMEM] * 3,
        compiler_params=PARAMS,
        name="adam",
    )(parts.reshape(64 * BLOCK, 128), own, moments[0], moments[1])
    mine = exchanged(new.reshape(64, 1, BLOCK * 128), chip_groups())
    back = [(b, a) for a, b in pairs_of]
    moments = lax.ppermute(jnp.stack([first_new, second_new]), BOTH, back)
    top = jnp.concatenate([from_corner[:, :SHIFT], from_north[:, SHIFT:]], axis=1)
    rest = jnp.concatenate([from_west[SHIFT:, :SHIFT], o_l[SHIFT:, SHIFT:]], axis=1)
    grad_input = jnp.concatenate([top, rest], axis=0)
    mine, moments, grad_input = lax.optimization_barrier((mine, moments, grad_input))

    mine = mine.reshape(64 * BLOCK, 128)
    theirs = lax.ppermute(mine, BOTH, core_swap())
    weights_new, table = own_half(place, mine)
    table_new = table[: HEADS * 5].reshape(5, HEADS, 128).transpose(1, 0, 2)
    table_new = table_new.reshape(HEADS, 640)[:, :BIAS]
    weights_new = other_half(place, theirs, weights_new)
    return (
        grad_input,
        weights_new.reshape(-1),
        moments[0].reshape(-1),
        moments[1].reshape(-1),
        table_new,
    )


def solution(mesh):
    placed = (
        P("lat", "lon", None),
        P("lat", "lon", None),
        P(),
        P(BOTH),
        P(BOTH),
        P(),
        P(),
        P("lat", "lon"),
    )
    return jax.shard_map(
        per_device,
        mesh=mesh,
        in_specs=placed,
        out_specs=(P("lat", "lon", None), P(), P(BOTH), P(BOTH), P()),
        check_vma=False,
    )
```

```python
import functools
import math

import jax
import jax.numpy as jnp
from jax import lax
from jax.experimental import pallas as pl
from jax.experimental.pallas import tpu as pltpu
from jax.sharding import PartitionSpec as P

D = 384
HEADS = 12
FF = 1536
WIN = 12
SHIFT = 6
WT = WIN * WIN
TILE = 24
TOK = TILE * TILE
WINS = TOK // WT
GROUPS = 3
PER = 4
QKV_ROWS = D * 3 * D // 128
PROJ_ROWS = D * D // 128
MLP_ROWS = D * FF // 128
PROJ_AT = QKV_ROWS
UP_AT = QKV_ROWS + PROJ_ROWS
DOWN_AT = UP_AT + MLP_ROWS
ROWS = DOWN_AT + MLP_ROWS
CHUNK = 256
CHUNKS = FF // CHUNK
HALF = ROWS // 2
OWN = ROWS // 128
BLOCK = OWN + 1
BATCH = 16
BIAS = 529
BOTH = ("lat", "lon")
F32 = jnp.float32
BF16 = jnp.bfloat16
VMEM = pl.BlockSpec(memory_space=pltpu.VMEM)
PARAMS = pltpu.CompilerParams(vmem_limit_bytes=58 * 1024 * 1024)

NN = (((1,), (0,)), ((), ()))
NT = (((1,), (1,)), ((), ()))
TN = (((0,), (0,)), ((), ()))


def split(value):
    high = value.astype(BF16)
    return high, (value - high.astype(F32)).astype(BF16)


def dot(a, b, dims):
    return lax.dot_general(a, b, dims, preferred_element_type=F32)


def dot3(a, b, dims):
    return dot(a[0], b[0], dims) + dot(a[0], b[1], dims) + dot(a[1], b[0], dims)


def dot3_deep(a, b, dims):
    (x,), (y,) = dims[0]
    left = jnp.concatenate([a[0], a[0], a[1]], axis=x)
    right = jnp.concatenate([b[0], b[1], b[0]], axis=y)
    return dot(left, right, dims)


def dot3_wide(a, b, dims):
    wide = dot(a[0], jnp.concatenate([b[0], b[1]], axis=1), dims)
    return wide[:, :128] + wide[:, 128:] + dot(a[1], b[0], dims)


def unit(value):
    center = value - jnp.mean(value, axis=-1, keepdims=True)
    scale = lax.rsqrt(jnp.mean(center * center, axis=-1, keepdims=True) + 1e-05)
    return center * scale, scale


def unit_back(grad, normed, scale):
    mean = jnp.mean(grad, axis=-1, keepdims=True)
    along = jnp.mean(grad * normed, axis=-1, keepdims=True)
    return scale * (grad - mean - normed * along)


STEPS = 6


def prepare(qkv, proj, up, down, table, index, wq_h, wq_l, wp_h, wp_l, wu_h, wu_l, wd_h, wd_l, bias):
    for flat, rows, blocks, high, low in (
        (qkv, D // STEPS, 9, wq_h, wq_l),
        (proj, D // STEPS, 3, wp_h, wp_l),
        (down, FF // STEPS, 3, wd_h.at[0], wd_l.at[0]),
    ):
        for b in range(blocks):
            h, l = split(flat[pl.ds(b, rows, stride=blocks), :])
            high[:, 128 * b : 128 * b + 128] = h
            low[:, 128 * b : 128 * b + 128] = l
    for f in range(CHUNKS):
        for b in range(2):
            h, l = split(up[pl.ds(2 * f + b, D // STEPS, stride=12), :])
            wu_h[f, :, 128 * b : 128 * b + 128] = h
            wu_l[f, :, 128 * b : 128 * b + 128] = l
    lines = jnp.concatenate([table[...], jnp.zeros((HEADS, 640 - BIAS), F32)], axis=1)
    for k in range(WT // 8 // STEPS):
        at = pl.multiple_of((pl.program_id(0) * (WT // 8 // STEPS) + k) * 8, 8)
        columns = index[pl.ds(at, 8), :]
        columns = jnp.concatenate([columns, jnp.zeros((8, 256 - WT), jnp.int32)], axis=1)
        low = columns & 127
        part = columns >> 7
        for h in range(HEADS):
            found = jnp.zeros((8, 256), F32)
            for p in range(5):
                line = jnp.broadcast_to(lines[h : h + 1, 128 * p : 128 * p + 128], (8, 128))
                taken = jnp.concatenate(
                    [
                        jnp.take_along_axis(line, low[:, :128], axis=1),
                        jnp.take_along_axis(line, low[:, 128:], axis=1),
                    ],
                    axis=1,
                )
                found = jnp.where(part == p, taken, found)
            bias[h // PER, pl.ds(pl.multiple_of((h % PER) * WT + at, 8), 8), :] = found[:, :WT]


def prepared(flat, table, index):
    shapes = [(D, 3 * D)] * 2 + [(D, D)] * 2 + [(CHUNKS, D, CHUNK)] * 2 + [(CHUNKS, CHUNK, D)] * 2
    piece = D // STEPS
    outs = [
        *[pl.BlockSpec((piece, 3 * D), lambda i: (i, 0))] * 2,
        *[pl.BlockSpec((piece, D), lambda i: (i, 0))] * 2,
        *[pl.BlockSpec((CHUNKS, piece, CHUNK), lambda i: (0, i, 0))] * 2,
        *[pl.BlockSpec((1, CHUNK, D), lambda i: (i, 0, 0))] * 2,
        pl.BlockSpec((GROUPS, PER * WT, WT), lambda i: (0, 0, 0)),
    ]

    def part(at, rows):
        return pl.BlockSpec((rows // STEPS, 128), lambda i: (at * STEPS // rows + i, 0))

    return pl.pallas_call(
        prepare,
        out_shape=[jax.ShapeDtypeStruct(s, BF16) for s in shapes]
        + [jax.ShapeDtypeStruct((GROUPS, PER * WT, WT), F32)],
        grid=(STEPS,),
        in_specs=[
            part(0, QKV_ROWS),
            part(PROJ_AT, PROJ_ROWS),
            part(UP_AT, MLP_ROWS),
            part(DOWN_AT, MLP_ROWS),
            pl.BlockSpec((HEADS, BIAS), lambda i: (0, 0)),
            pl.BlockSpec((WT, WT), lambda i: (0, 0)),
        ],
        out_specs=outs,
        compiler_params=PARAMS,
        name="prepare",
    )(flat, flat, flat, flat, table, index)


def gather_windows(target, local, east, south, corner):
    for wr in range(2):
        for wc in range(2):
            for r in range(WIN):
                row = wr * WIN + r
                at = (wr * 2 + wc) * WT + r * WIN
                if row < TILE - SHIFT:
                    near, far, k = local, east, row + SHIFT
                else:
                    near, far, k = south, corner, row - (TILE - SHIFT)
                if wc == 0:
                    target[at : at + WIN, :] = near[k, SHIFT : SHIFT + WIN, :]
                else:
                    target[at : at + SHIFT, :] = near[k, SHIFT + WIN : TILE, :]
                    target[at + SHIFT : at + WIN, :] = far[k, 0:SHIFT, :]


def scatter_windows(source, local, east, south, corner):
    for wr in range(2):
        for wc in range(2):
            for r in range(WIN):
                row = wr * WIN + r
                at = (wr * 2 + wc) * WT + r * WIN
                if row < TILE - SHIFT:
                    near, far, k = local, east, row + SHIFT
                else:
                    near, far, k = south, corner, row - (TILE - SHIFT)
                if wc == 0:
                    near[k, SHIFT : SHIFT + WIN, :] = source[at : at + WIN, :]
                else:
                    near[k, SHIFT + WIN : TILE, :] = source[at : at + SHIFT, :]
                    far[k, 0:SHIFT, :] = source[at + SHIFT : at + WIN, :]


def head_lane():
    return lax.broadcasted_iota(jnp.int32, (WT, 128), 1) >> 5


def stacked(value):
    lane = head_lane()
    return jnp.concatenate([jnp.where(lane == h, value, 0.0) for h in range(PER)], axis=0)


def unstacked(value):
    lane = head_lane()
    total = jnp.where(lane == 0, value[:WT], 0.0)
    for h in range(1, PER):
        total = jnp.where(lane == h, value[h * WT : h * WT + WT], total)
    return total


def find_labels(region, last, label_row, label_col):
    eye = lax.broadcasted_iota(jnp.int32, (WT, WT), 0) == lax.broadcasted_iota(jnp.int32, (WT, WT), 1)
    for wr in range(2):
        for wc in range(2):
            w = wr * 2 + wc
            pieces = []
            for r in range(WIN):
                row = wr * WIN + r
                ids = region[row : row + 1, wc * WIN : wc * WIN + WIN]
                pieces.append(ids + (4 * last if row >= TILE - SHIFT else 0))
            line = jnp.concatenate(pieces, axis=1).astype(F32)
            label_row[w] = line
            wide = jnp.where(eye, jnp.broadcast_to(line, (WT, WT)), 0.0)
            label_col[w] = jnp.sum(wide, axis=1, keepdims=True)


SCALE = 1.0 / math.sqrt(32.0)


def block_pass(
    x_l, c_l, east, south, corner, region, place, *rest
):
    stored, rest = rest[:9], rest[9:]
    (
    keep, send, dscore, x_out, grad_out, dqkv_out,
    x, cot, qkv, ctx, prob, n2h, n2l, ch, cl, grad, dqkv, dctx, grads, label_row, label_col, norm2, scale2, sems,
    ) = rest[:-9]
    held = rest[-9:]
    wq_h, wq_l, wp_h, wp_l, wu_h, wu_l, wd_h, wd_l, bias = held
    loads = [pltpu.make_async_copy(a, b, sems.at[i]) for i, (a, b) in enumerate(zip(stored, held))]
    for i in (0, 1, 8, 2, 3, 4, 5, 6, 7):
        loads[i].start()
    core = place[0]

    def piece(i, half, start, rows):
        source = grads.at[pl.ds(start, rows)]
        spot = pl.ds(start - half * HALF, rows)
        for target, here in ((keep, core == half), (send, core != half)):
            yield here, pltpu.make_async_copy(source, target.at[spot], sems.at[9 + i])

    def start(*what):
        for here, copy in piece(*what):
            pl.when(here)(copy.start)

    def finish(*what):
        for here, copy in piece(*what):
            pl.when(here)(copy.wait)

    pieces = (
        (0, 1, HALF, HALF),
        (1, 0, UP_AT, HALF - UP_AT),
        (2, 0, 0, UP_AT),
    )
    find_labels(region, place[1], label_row, label_col)
    gather_windows(x, x_l, east.at[0], south.at[0], corner.at[0])
    kept = [
        pltpu.make_async_copy(a, b, sems.at[12 + i])
        for i, (a, b) in enumerate(((x, x_out), (grad, grad_out), (dqkv, dqkv_out)))
    ]
    kept[0].start()
    gather_windows(cot, c_l, east.at[1], south.at[1], corner.at[1])
    n1 = split(unit(x[...])[0])
    loads[0].wait()
    loads[1].wait()
    qkv[...] = dot3_deep(n1, (wq_h[...], wq_l[...]), NN)

    loads[8].wait()

    def attend(step, carry):
        w, g = step // GROUPS, step % GROUPS
        rows = pl.ds(pl.multiple_of(w * WT, 16), WT)
        lanes = pl.ds(pl.multiple_of(g * 128, 128), 128)
        q = split(stacked(qkv[rows, pl.ds(pl.multiple_of(g * 128, 128), 128)] * SCALE))
        k = split(qkv[rows, pl.ds(pl.multiple_of(D + g * 128, 128), 128)])
        v = split(qkv[rows, pl.ds(pl.multiple_of(2 * D + g * 128, 128), 128)])
        allowed = label_col[w] == label_row[w]
        score = dot3_deep(q, k, NT) + bias[g]
        score = jnp.where(jnp.concatenate([allowed] * PER, axis=0), score, -jnp.inf)
        raised = jnp.exp(score - jnp.max(score, axis=-1, keepdims=True))
        p = raised * (1.0 / jnp.sum(raised, axis=-1, keepdims=True))
        prob[step] = p
        ctx[rows, lanes] = unstacked(dot3_wide(split(p), v, NN))
        return carry

    lax.fori_loop(0, WINS * GROUPS, attend, 0, unroll=12)

    for i in range(2, 8):
        loads[i].wait()
    mixed = x[...] + dot3_deep(split(ctx[...]), (wp_h[...], wp_l[...]), NN)
    norm2[...], scale2[...] = unit(mixed)
    n2h[...], n2l[...] = split(norm2[...])
    ch[...], cl[...] = split(cot[...])
    grad[...] = jnp.zeros_like(grad)

    def feed(f, carry):
        n = (n2h[...], n2l[...])
        c = (ch[...], cl[...])
        up = (wu_h[f], wu_l[f])
        u = dot3_deep(n, up, NN)
        back = dot3_deep(c, (wd_h[f], wd_l[f]), NT)
        inner = 0.7978845608028654 * (u + 0.044715 * u * u * u)
        t = jnp.tanh(inner)
        hidden = split(0.5 * u * (1.0 + t))
        slope = 0.5 * (1.0 + t) + 0.5 * u * (1.0 - t * t) * (
            0.7978845608028654 * (1.0 + 3.0 * 0.044715 * u * u)
        )
        du = split(back * slope)
        gdown = dot3_deep(hidden, c, TN)
        for b in range(3):
            grads[pl.ds(DOWN_AT + 3 * CHUNK * f + b, CHUNK, stride=3), :] = gdown[:, 128 * b : 128 * b + 128]
        gup = dot3_deep(n, du, TN)
        for b in range(2):
            grads[pl.ds(UP_AT + 2 * f + b, D, stride=12), :] = gup[:, 128 * b : 128 * b + 128]
        grad[...] += dot3_deep(du, up, NT)
        return carry

    lax.fori_loop(0, CHUNKS, feed, 0)

    start(*pieces[0])
    start(*pieces[1])
    grad[...] = cot[...] + unit_back(grad[...], norm2[...], scale2[...])
    kept[1].start()
    gm = split(grad[...])
    dctx[...] = dot3_deep(gm, (wp_h[...], wp_l[...]), NT)
    gproj = dot3_deep(split(ctx[...]), gm, TN)
    for b in range(3):
        grads[pl.ds(PROJ_AT + b, D, stride=3), :] = gproj[:, 128 * b : 128 * b + 128]
    dscore[...] = jnp.zeros_like(dscore)

    def attend_back(step, carry):
        w, g = step // GROUPS, step % GROUPS
        rows = pl.ds(pl.multiple_of(w * WT, 16), WT)
        q_at = pl.ds(pl.multiple_of(g * 128, 128), 128)
        k_at = pl.ds(pl.multiple_of(D + g * 128, 128), 128)
        v_at = pl.ds(pl.multiple_of(2 * D + g * 128, 128), 128)
        q = split(stacked(qkv[rows, q_at] * SCALE))
        k = split(qkv[rows, k_at])
        v = split(qkv[rows, v_at])
        d = split(stacked(dctx[rows, q_at]))
        p = prob[step]
        dp = dot3_deep(d, v, NT)
        ds = p * (dp - jnp.sum(dp * p, axis=-1, keepdims=True))
        dscore[g] += ds
        ps, dss = split(p), split(ds)
        dqkv[rows, v_at] = dot3_wide(ps, d, TN)
        dqkv[rows, q_at] = unstacked(dot3_wide(dss, k, NN)) * SCALE
        dqkv[rows, k_at] = dot3_wide(dss, q, TN)
        return carry

    lax.fori_loop(0, WINS * GROUPS, attend_back, 0, unroll=4)

    kept[2].start()
    dq = split(dqkv[...])
    gqkv = dot3_deep(split(unit(x[...])[0]), dq, TN)
    for b in range(9):
        grads[pl.ds(b, D, stride=9), :] = gqkv[:, 128 * b : 128 * b + 128]
    start(*pieces[2])
    for copy in kept:
        copy.wait()
    for what in pieces:
        finish(*what)


def input_grad(x, grad, dqkv, wq_h, wq_l, o_l, o_e, o_s, o_c, total):
    n1, scale1 = unit(x[...])
    back = dot3_deep(split(dqkv[...]), (wq_h[...], wq_l[...]), NT)
    total[...] = grad[...] + unit_back(back, n1, scale1)
    scatter_windows(total, o_l, o_e, o_s, o_c)


def run_input_grad(x, grad, dqkv, wq_h, wq_l):
    halo = [(TILE, TILE, D), (TILE, 8, D), (SHIFT, TILE, D), (SHIFT, 8, D)]
    return pl.pallas_call(
        input_grad,
        out_shape=[jax.ShapeDtypeStruct(s, F32) for s in halo],
        in_specs=[VMEM] * 5,
        out_specs=[VMEM] * 4,
        scratch_shapes=[pltpu.VMEM((TOK, D), F32)],
        compiler_params=PARAMS,
        name="input_grad",
    )(x, grad, dqkv, wq_h, wq_l)


def run_block(tiles, edges, weights, bias, region, place):
    outs = [(HALF, 128), (HALF, 128), (GROUPS, PER * WT, WT), (TOK, D), (TOK, D), (TOK, 3 * D)]
    whole = pl.BlockSpec(memory_space=pl.ANY)
    scratch = [
        pltpu.VMEM((TOK, D), F32),
        pltpu.VMEM((TOK, D), F32),
        pltpu.VMEM((TOK, 3 * D), F32),
        pltpu.VMEM((TOK, D), F32),
        pltpu.VMEM((WINS * GROUPS, PER * WT, WT), F32),
        pltpu.VMEM((TOK, D), BF16),
        pltpu.VMEM((TOK, D), BF16),
        pltpu.VMEM((TOK, D), BF16),
        pltpu.VMEM((TOK, D), BF16),
        pltpu.VMEM((TOK, D), F32),
        pltpu.VMEM((TOK, 3 * D), F32),
        pltpu.VMEM((TOK, D), F32),
        pltpu.VMEM((ROWS, 128), F32),
        pltpu.VMEM((WINS, 1, WT), F32),
        pltpu.VMEM((WINS, WT, 1), F32),
        pltpu.VMEM((TOK, D), F32),
        pltpu.VMEM((TOK, 1), F32),
        pltpu.SemaphoreType.DMA((15,)),
        *[pltpu.VMEM(a.shape, a.dtype) for a in (*weights, bias)],
    ]
    args = (*tiles, *edges, region, place, *weights, bias)
    return pl.pallas_call(
        block_pass,
        out_shape=[jax.ShapeDtypeStruct(s, F32) for s in outs],
        in_specs=[VMEM] * 6 + [pl.BlockSpec(memory_space=pltpu.SMEM)] + [whole] * 9,
        out_specs=[whole] * 2 + [VMEM] + [whole] * 3,
        scratch_shapes=scratch,
        compiler_params=PARAMS,
        name="block_pass",
    )(*args)


def table_sum(scores, index, out, sums):
    sums[...] = jnp.zeros_like(sums)
    column = lax.broadcasted_iota(jnp.int32, (128, WT), 0)

    def one(i):
        line = index[pl.ds(i, 1), :]
        part = jnp.broadcast_to(line >> 7, (16, WT))
        hot = (column == jnp.broadcast_to(line & 127, (128, WT))).astype(F32).astype(BF16)
        high, low = split(scores[i])
        pieces = []
        for p in range(5):
            here = part == p
            pieces.append(jnp.where(here, high, jnp.zeros_like(high)))
            pieces.append(jnp.where(here, low, jnp.zeros_like(low)))
        return dot(jnp.concatenate(pieces, axis=0), hot, NT)

    def step(k, carry):
        at = 8 * k
        quads = [(one(at + i) + one(at + i + 1)) + (one(at + i + 2) + one(at + i + 3)) for i in (0, 4)]
        sums[...] += quads[0] + quads[1]
        return carry

    lax.fori_loop(0, WT // 8, step, 0)
    out[...] = jnp.zeros_like(out)
    for p in range(5):
        both = sums[32 * p : 32 * p + 16, :] + sums[32 * p + 16 : 32 * p + 32, :]
        out[HEADS * p : HEADS * p + HEADS, :] = both[:HEADS]


def table_gradient(dscore, index):
    scores = dscore.reshape(HEADS, WT, WT).transpose(1, 0, 2)
    scores = jnp.pad(scores, ((0, 0), (0, 4), (0, 0)))
    return pl.pallas_call(
        table_sum,
        out_shape=jax.ShapeDtypeStruct((64, 128), F32),
        in_specs=[VMEM] * 2,
        out_specs=VMEM,
        scratch_shapes=[pltpu.VMEM((160, 128), F32)],
        compiler_params=PARAMS,
        name="table_sum",
    )(scores, index)


def chip_order():
    return [(y_lo * 4 + x) * 16 + zy * 2 for y_lo in range(2) for x in range(4) for zy in range(8)]


def chip_groups():
    return [[d + core for d in chip_order()] for core in range(2)]


def core_swap():
    return [(d, d ^ 1) for d in range(128)]


def worker_pairs():
    return [(core * 64 + q, d + core) for core in range(2) for q, d in enumerate(chip_order())]


def exchanged(value, groups):
    return lax.all_to_all(value, BOTH, 0, 0, axis_index_groups=groups, tiled=True)


def around(value, axis, by):
    size = lax.axis_size(axis)
    return lax.ppermute(value, axis, [(i, (i + by) % size) for i in range(size)])


def diagonal(value, by):
    lat, lon = lax.axis_size("lat"), lax.axis_size("lon")
    return lax.ppermute(
        value,
        BOTH,
        [
            (a * lon + o, ((a + by) % lat) * lon + (o + by) % lon)
            for a in range(lat)
            for o in range(lon)
        ],
    )


def pack(x_east, x_south, c_east, c_south, east, south, corner):
    for i, (e, t) in enumerate(((x_east, x_south), (c_east, c_south))):
        east[i] = e[...]
        south[i] = t[...]
        corner[i] = t[:, 0:8, :]


def edges_of(x, c):
    east_in = pl.BlockSpec((TILE, 8, D), lambda i: (0, 0, 0))
    south_in = pl.BlockSpec((SHIFT, TILE, D), lambda i: (0, 0, 0))
    shapes = [(2, TILE, 8, D), (2, SHIFT, TILE, D), (2, SHIFT, 8, D)]
    east, south, corner = pl.pallas_call(
        pack,
        out_shape=[jax.ShapeDtypeStruct(s, F32) for s in shapes],
        grid=(1,),
        in_specs=[east_in, south_in] * 2,
        out_specs=[pl.BlockSpec(s, lambda i: (0, 0, 0, 0)) for s in shapes],
        compiler_params=PARAMS,
        name="pack",
    )(x, x, c, c)
    return around(east, "lon", -1), around(south, "lat", -1), diagonal(corner, -1)


def merge(keep, came, line, line_came, out):
    for q in range(BATCH):
        rows = slice(q * OWN, q * OWN + OWN)
        out[q * BLOCK : q * BLOCK + OWN, :] = keep[rows, :] + came[rows, :]
        out[q * BLOCK + OWN : (q + 1) * BLOCK, :] = line[q : q + 1, :] + line_came[q : q + 1, :]


def merged(keep, came, line, line_came):
    halves = pl.BlockSpec((BATCH * OWN, 128), lambda i: (i, 0))
    lines = pl.BlockSpec((BATCH, 128), lambda i: (i, 0))
    return pl.pallas_call(
        merge,
        out_shape=jax.ShapeDtypeStruct((64 * BLOCK, 128), F32),
        grid=(64 // BATCH,),
        in_specs=[halves, halves, lines, lines],
        out_specs=pl.BlockSpec((BATCH * BLOCK, 128), lambda i: (i, 0)),
        compiler_params=PARAMS,
        name="merge",
    )(keep, came, line, line_came)


def adam(parts, weights, first, second, new, first_new, second_new, factor):
    total = parts[0:BLOCK, :]
    for q in range(1, 64):
        total = total + parts[q * BLOCK : q * BLOCK + BLOCK, :]
    total = total * factor
    grad, line = total[:OWN], total[OWN:]
    m = 0.9 * first[...] + 0.1 * grad
    s = 0.95 * second[...] + 0.05 * grad * grad
    first_new[...] = m
    second_new[...] = s
    fresh = weights[...] - 0.01 * m / (jnp.sqrt(s) + 1e-08)
    fresh = jnp.concatenate([fresh, line], axis=0)
    for q in range(64):
        new[q * BLOCK : q * BLOCK + BLOCK, :] = fresh


def lay_out(place, blocks, *refs):
    out = refs[-1]
    for q in range(BATCH):
        out[q * OWN : q * OWN + OWN, :] = blocks[q * BLOCK : q * BLOCK + OWN, :]


def lay_out_own(place, blocks, out, lines):
    lay_out(place, blocks, out)
    for q in range(BATCH):
        lines[q : q + 1, :] = blocks[q * BLOCK + OWN : q * BLOCK + BLOCK, :]


def own_half(place, blocks):
    steps = 64 // BATCH
    return pl.pallas_call(
        lay_out_own,
        out_shape=[jax.ShapeDtypeStruct((ROWS, 128), F32), jax.ShapeDtypeStruct((64, 128), F32)],
        grid_spec=pltpu.PrefetchScalarGridSpec(
            num_scalar_prefetch=1,
            grid=(steps,),
            in_specs=[pl.BlockSpec((BATCH * BLOCK, 128), lambda i, spot: (i, 0))],
            out_specs=[
                pl.BlockSpec((BATCH * OWN, 128), lambda i, spot: (spot[0] * steps + i, 0)),
                pl.BlockSpec((BATCH, 128), lambda i, spot: (i, 0)),
            ],
        ),
        compiler_params=PARAMS,
        name="lay_out_own",
    )(place, blocks)


def other_half(place, blocks, so_far):
    steps = 64 // BATCH
    return pl.pallas_call(
        lay_out,
        out_shape=jax.ShapeDtypeStruct((ROWS, 128), F32),
        grid_spec=pltpu.PrefetchScalarGridSpec(
            num_scalar_prefetch=1,
            grid=(steps,),
            in_specs=[
                pl.BlockSpec((BATCH * BLOCK, 128), lambda i, spot: (i, 0)),
                pl.BlockSpec(memory_space=pl.ANY),
            ],
            out_specs=pl.BlockSpec((BATCH * OWN, 128), lambda i, spot: ((1 - spot[0]) * steps + i, 0)),
        ),
        input_output_aliases={2: 0},
        compiler_params=PARAMS,
        name="lay_out_other",
    )(place, blocks, so_far)


def per_device(
    block_input, cotangent, weights, first_moment, second_moment, bias_table, bias_index, region_ids
):
    lat_at, lon_at = lax.axis_index("lat"), lax.axis_index("lon")
    factor = 1.0 / math.sqrt(TOK * 128)
    flat = weights.reshape(ROWS, 128)
    *pairs, bias = prepared(flat, bias_table, bias_index)
    edges = edges_of(block_input, cotangent)
    core = lon_at % 2
    place = jnp.stack([core, (lat_at == 7).astype(jnp.int32)]).astype(jnp.int32)
    keep, send, dscore, x, grad, dqkv = run_block(
        (block_input, cotangent), edges, pairs, bias, region_ids, place
    )
    came = lax.ppermute(send, BOTH, core_swap())
    line = table_gradient(dscore, bias_index)
    line_came = lax.ppermute(line, BOTH, core_swap())
    summed = merged(keep, came, line, line_came)
    parts = exchanged(summed.reshape(64, 1, BLOCK * 128), chip_groups())

    _, dqkv, first_moment, second_moment = lax.optimization_barrier(
        (summed, dqkv, first_moment, second_moment)
    )
    o_l, o_e, o_s, o_c = run_input_grad(x, grad, dqkv, pairs[0], pairs[1])
    from_west = around(o_e, "lon", 1)
    from_north = around(o_s, "lat", 1)
    from_corner = diagonal(o_c, 1)
    pairs_of = worker_pairs()
    moments = jnp.stack([first_moment.reshape(OWN, 128), second_moment.reshape(OWN, 128)])
    moments = lax.ppermute(moments, BOTH, pairs_of)
    parts, from_west, from_north, from_corner, moments = lax.optimization_barrier(
        (parts, from_west, from_north, from_corner, moments)
    )

    shard = core * 64 + lat_at * 8 + lon_at // 2
    own = lax.dynamic_slice_in_dim(flat, shard * OWN, OWN, 0)
    new, first_new, second_new = pl.pallas_call(
        functools.partial(adam, factor=factor),
        out_shape=[jax.ShapeDtypeStruct((n, 128), F32) for n in (64 * BLOCK, OWN, OWN)],
        in_specs=[VMEM] * 4,
        out_specs=[VMEM] * 3,
        compiler_params=PARAMS,
        name="adam",
    )(parts.reshape(64 * BLOCK, 128), own, moments[0], moments[1])
    mine = exchanged(new.reshape(64, 1, BLOCK * 128), chip_groups())
    back = [(b, a) for a, b in pairs_of]
    moments = lax.ppermute(jnp.stack([first_new, second_new]), BOTH, back)
    top = jnp.concatenate([from_corner[:, :SHIFT], from_north[:, SHIFT:]], axis=1)
    rest = jnp.concatenate([from_west[SHIFT:, :SHIFT], o_l[SHIFT:, SHIFT:]], axis=1)
    grad_input = jnp.concatenate([top, rest], axis=0)
    mine, moments, grad_input = lax.optimization_barrier((mine, moments, grad_input))

    mine = mine.reshape(64 * BLOCK, 128)
    theirs = lax.ppermute(mine, BOTH, core_swap())
    weights_new, table = own_half(place, mine)
    table_new = table[: HEADS * 5].reshape(5, HEADS, 128).transpose(1, 0, 2)
    table_new = table_new.reshape(HEADS, 640)[:, :BIAS]
    weights_new = other_half(place, theirs, weights_new)
    return (
        grad_input,
        weights_new.reshape(-1),
        moments[0].reshape(-1),
        moments[1].reshape(-1),
        table_new,
    )


def solution(mesh):
    placed = (
        P("lat", "lon", None),
        P("lat", "lon", None),
        P(),
        P(BOTH),
        P(BOTH),
        P(),
        P(),
        P("lat", "lon"),
    )
    return jax.shard_map(
        per_device,
        mesh=mesh,
        in_specs=placed,
        out_specs=(P("lat", "lon", None), P(), P(BOTH), P(BOTH), P()),
        check_vma=False,
    )
```

```python
import functools
import math

import jax
import jax.numpy as jnp
from jax import lax
from jax.experimental import pallas as pl
from jax.experimental.pallas import tpu as pltpu
from jax.sharding import PartitionSpec as P

D = 384
HEADS = 12
FF = 1536
WIN = 12
SHIFT = 6
WT = WIN * WIN
TILE = 24
TOK = TILE * TILE
WINS = TOK // WT
GROUPS = 3
PER = 4
QKV_ROWS = D * 3 * D // 128
PROJ_ROWS = D * D // 128
MLP_ROWS = D * FF // 128
PROJ_AT = QKV_ROWS
UP_AT = QKV_ROWS + PROJ_ROWS
DOWN_AT = UP_AT + MLP_ROWS
ROWS = DOWN_AT + MLP_ROWS
CHUNK = 256
CHUNKS = FF // CHUNK
MLP_HALF = MLP_ROWS
ATT_HALF = UP_AT // 2
OWN_MLP = MLP_HALF // 64
OWN_ATT = ATT_HALF // 64
OWN = OWN_MLP + OWN_ATT
SUM_BLOCK = OWN_ATT + 1
BLOCK = OWN + 1
BATCH = 16
BIAS = 529
BOTH = ("lat", "lon")
F32 = jnp.float32
BF16 = jnp.bfloat16
VMEM = pl.BlockSpec(memory_space=pltpu.VMEM)
PARAMS = pltpu.CompilerParams(vmem_limit_bytes=58 * 1024 * 1024)

NN = (((1,), (0,)), ((), ()))
NT = (((1,), (1,)), ((), ()))
TN = (((0,), (0,)), ((), ()))


def split(value):
    high = value.astype(BF16)
    return high, (value - high.astype(F32)).astype(BF16)


def dot(a, b, dims):
    return lax.dot_general(a, b, dims, preferred_element_type=F32)


def dot3(a, b, dims):
    return dot(a[0], b[0], dims) + dot(a[0], b[1], dims) + dot(a[1], b[0], dims)


def dot3_deep(a, b, dims):
    (x,), (y,) = dims[0]
    left = jnp.concatenate([a[0], a[0], a[1]], axis=x)
    right = jnp.concatenate([b[0], b[1], b[0]], axis=y)
    return dot(left, right, dims)


def dot3_wide(a, b, dims):
    wide = dot(a[0], jnp.concatenate([b[0], b[1]], axis=1), dims)
    return wide[:, :128] + wide[:, 128:] + dot(a[1], b[0], dims)


def unit(value):
    center = value - jnp.mean(value, axis=-1, keepdims=True)
    scale = lax.rsqrt(jnp.mean(center * center, axis=-1, keepdims=True) + 1e-05)
    return center * scale, scale


def unit_back(grad, normed, scale):
    mean = jnp.mean(grad, axis=-1, keepdims=True)
    along = jnp.mean(grad * normed, axis=-1, keepdims=True)
    return scale * (grad - mean - normed * along)


STEPS = 6


def prepare(qkv, proj, up, down, table, index, wq_h, wq_l, wp_h, wp_l, wu_h, wu_l, wd_h, wd_l, bias):
    for flat, rows, blocks, high, low in (
        (qkv, D // STEPS, 9, wq_h, wq_l),
        (proj, D // STEPS, 3, wp_h, wp_l),
        (down, FF // STEPS, 3, wd_h.at[0], wd_l.at[0]),
    ):
        for b in range(blocks):
            h, l = split(flat[pl.ds(b, rows, stride=blocks), :])
            high[:, 128 * b : 128 * b + 128] = h
            low[:, 128 * b : 128 * b + 128] = l
    for f in range(CHUNKS):
        for b in range(2):
            h, l = split(up[pl.ds(2 * f + b, D // STEPS, stride=12), :])
            wu_h[f, :, 128 * b : 128 * b + 128] = h
            wu_l[f, :, 128 * b : 128 * b + 128] = l
    lines = jnp.concatenate([table[...], jnp.zeros((HEADS, 640 - BIAS), F32)], axis=1)
    for k in range(WT // 8 // STEPS):
        at = pl.multiple_of((pl.program_id(0) * (WT // 8 // STEPS) + k) * 8, 8)
        columns = index[pl.ds(at, 8), :]
        columns = jnp.concatenate([columns, jnp.zeros((8, 256 - WT), jnp.int32)], axis=1)
        low = columns & 127
        part = columns >> 7
        for h in range(HEADS):
            found = jnp.zeros((8, 256), F32)
            for p in range(5):
                line = jnp.broadcast_to(lines[h : h + 1, 128 * p : 128 * p + 128], (8, 128))
                taken = jnp.concatenate(
                    [
                        jnp.take_along_axis(line, low[:, :128], axis=1),
                        jnp.take_along_axis(line, low[:, 128:], axis=1),
                    ],
                    axis=1,
                )
                found = jnp.where(part == p, taken, found)
            bias[h // PER, pl.ds(pl.multiple_of((h % PER) * WT + at, 8), 8), :] = found[:, :WT]


def prepared(flat, table, index):
    shapes = [(D, 3 * D)] * 2 + [(D, D)] * 2 + [(CHUNKS, D, CHUNK)] * 2 + [(CHUNKS, CHUNK, D)] * 2
    piece = D // STEPS
    outs = [
        *[pl.BlockSpec((piece, 3 * D), lambda i: (i, 0))] * 2,
        *[pl.BlockSpec((piece, D), lambda i: (i, 0))] * 2,
        *[pl.BlockSpec((CHUNKS, piece, CHUNK), lambda i: (0, i, 0))] * 2,
        *[pl.BlockSpec((1, CHUNK, D), lambda i: (i, 0, 0))] * 2,
        pl.BlockSpec((GROUPS, PER * WT, WT), lambda i: (0, 0, 0)),
    ]

    def part(at, rows):
        return pl.BlockSpec((rows // STEPS, 128), lambda i: (at * STEPS // rows + i, 0))

    return pl.pallas_call(
        prepare,
        out_shape=[jax.ShapeDtypeStruct(s, BF16) for s in shapes]
        + [jax.ShapeDtypeStruct((GROUPS, PER * WT, WT), F32)],
        grid=(STEPS,),
        in_specs=[
            part(0, QKV_ROWS),
            part(PROJ_AT, PROJ_ROWS),
            part(UP_AT, MLP_ROWS),
            part(DOWN_AT, MLP_ROWS),
            pl.BlockSpec((HEADS, BIAS), lambda i: (0, 0)),
            pl.BlockSpec((WT, WT), lambda i: (0, 0)),
        ],
        out_specs=outs,
        compiler_params=PARAMS,
        name="prepare",
    )(flat, flat, flat, flat, table, index)


def gather_windows(target, local, east, south, corner):
    for wr in range(2):
        for wc in range(2):
            for r in range(WIN):
                row = wr * WIN + r
                at = (wr * 2 + wc) * WT + r * WIN
                if row < TILE - SHIFT:
                    near, far, k = local, east, row + SHIFT
                else:
                    near, far, k = south, corner, row - (TILE - SHIFT)
                if wc == 0:
                    target[at : at + WIN, :] = near[k, SHIFT : SHIFT + WIN, :]
                else:
                    target[at : at + SHIFT, :] = near[k, SHIFT + WIN : TILE, :]
                    target[at + SHIFT : at + WIN, :] = far[k, 0:SHIFT, :]


def scatter_windows(source, local, east, south, corner):
    for wr in range(2):
        for wc in range(2):
            for r in range(WIN):
                row = wr * WIN + r
                at = (wr * 2 + wc) * WT + r * WIN
                if row < TILE - SHIFT:
                    near, far, k = local, east, row + SHIFT
                else:
                    near, far, k = south, corner, row - (TILE - SHIFT)
                if wc == 0:
                    near[k, SHIFT : SHIFT + WIN, :] = source[at : at + WIN, :]
                else:
                    near[k, SHIFT + WIN : TILE, :] = source[at : at + SHIFT, :]
                    far[k, 0:SHIFT, :] = source[at + SHIFT : at + WIN, :]


def head_lane():
    return lax.broadcasted_iota(jnp.int32, (WT, 128), 1) >> 5


def stacked(value):
    lane = head_lane()
    return jnp.concatenate([jnp.where(lane == h, value, 0.0) for h in range(PER)], axis=0)


def unstacked(value):
    lane = head_lane()
    total = jnp.where(lane == 0, value[:WT], 0.0)
    for h in range(1, PER):
        total = jnp.where(lane == h, value[h * WT : h * WT + WT], total)
    return total


def find_labels(region, last, label_row, label_col):
    eye = lax.broadcasted_iota(jnp.int32, (WT, WT), 0) == lax.broadcasted_iota(jnp.int32, (WT, WT), 1)
    for wr in range(2):
        for wc in range(2):
            w = wr * 2 + wc
            pieces = []
            for r in range(WIN):
                row = wr * WIN + r
                ids = region[row : row + 1, wc * WIN : wc * WIN + WIN]
                pieces.append(ids + (4 * last if row >= TILE - SHIFT else 0))
            line = jnp.concatenate(pieces, axis=1).astype(F32)
            label_row[w] = line
            wide = jnp.where(eye, jnp.broadcast_to(line, (WT, WT)), 0.0)
            label_col[w] = jnp.sum(wide, axis=1, keepdims=True)


SCALE = 1.0 / math.sqrt(32.0)


def ship(grads, outs, core, rows, sems):
    for h in range(2):
        source = grads.at[pl.ds(h * rows, rows)]
        for target, here in ((outs[0], core == h), (outs[1], core != h)):
            yield here, pltpu.make_async_copy(source, target, sems.at[h])


def forward_and_feed(
    x_l, c_l, east, south, corner, region, place, *rest
):
    stored, rest = rest[:9], rest[9:]
    (
        keep, send, x_out, grad_out, qkv_out, prob_out, ctx_out,
        x, cot, qkv, ctx, prob, n2h, n2l, ch, cl, grad, grads, label_row, label_col, norm2, scale2,
        sems, prob_sems,
    ) = rest[:-9]
    held = rest[-9:]
    wq_h, wq_l, wp_h, wp_l, wu_h, wu_l, wd_h, wd_l, bias = held
    loads = [pltpu.make_async_copy(a, b, sems.at[i]) for i, (a, b) in enumerate(zip(stored, held))]
    for i in (0, 1, 8, 2, 3, 4, 5, 6, 7):
        loads[i].start()
    core = place[0]
    find_labels(region, place[1], label_row, label_col)
    gather_windows(x, x_l, east.at[0], south.at[0], corner.at[0])
    kept = [
        pltpu.make_async_copy(a, b, sems.at[9 + i])
        for i, (a, b) in enumerate(((x, x_out), (grad, grad_out), (qkv, qkv_out), (ctx, ctx_out)))
    ]
    kept[0].start()
    gather_windows(cot, c_l, east.at[1], south.at[1], corner.at[1])
    n1 = split(unit(x[...])[0])
    loads[0].wait()
    loads[1].wait()
    qkv[...] = dot3_deep(n1, (wq_h[...], wq_l[...]), NN)
    kept[2].start()
    loads[8].wait()

    def attend(step, carry):
        w, g = step // GROUPS, step % GROUPS
        rows = pl.ds(pl.multiple_of(w * WT, 16), WT)
        lanes = pl.ds(pl.multiple_of(g * 128, 128), 128)
        q = split(stacked(qkv[rows, pl.ds(pl.multiple_of(g * 128, 128), 128)] * SCALE))
        k = split(qkv[rows, pl.ds(pl.multiple_of(D + g * 128, 128), 128)])
        v = split(qkv[rows, pl.ds(pl.multiple_of(2 * D + g * 128, 128), 128)])
        allowed = label_col[w] == label_row[w]
        score = dot3_deep(q, k, NT) + bias[g]
        score = jnp.where(jnp.concatenate([allowed] * PER, axis=0), score, -jnp.inf)
        raised = jnp.exp(score - jnp.max(score, axis=-1, keepdims=True))
        p = raised * (1.0 / jnp.sum(raised, axis=-1, keepdims=True))
        prob[step] = p
        pltpu.make_async_copy(prob.at[step], prob_out.at[step], prob_sems.at[step]).start()
        ctx[rows, lanes] = unstacked(dot3_wide(split(p), v, NN))
        return carry

    lax.fori_loop(0, WINS * GROUPS, attend, 0, unroll=12)
    kept[3].start()
    for i in range(2, 8):
        loads[i].wait()
    mixed = x[...] + dot3_deep(split(ctx[...]), (wp_h[...], wp_l[...]), NN)
    norm2[...], scale2[...] = unit(mixed)
    n2h[...], n2l[...] = split(norm2[...])
    ch[...], cl[...] = split(cot[...])
    grad[...] = jnp.zeros_like(grad)

    def feed(f, carry):
        n = (n2h[...], n2l[...])
        c = (ch[...], cl[...])
        up = (wu_h[f], wu_l[f])
        u = dot3_deep(n, up, NN)
        back = dot3_deep(c, (wd_h[f], wd_l[f]), NT)
        inner = 0.7978845608028654 * (u + 0.044715 * u * u * u)
        t = jnp.tanh(inner)
        hidden = split(0.5 * u * (1.0 + t))
        slope = 0.5 * (1.0 + t) + 0.5 * u * (1.0 - t * t) * (
            0.7978845608028654 * (1.0 + 3.0 * 0.044715 * u * u)
        )
        du = split(back * slope)
        gdown = dot3_deep(hidden, c, TN)
        for b in range(3):
            grads[pl.ds(MLP_ROWS + 3 * CHUNK * f + b, CHUNK, stride=3), :] = gdown[:, 128 * b : 128 * b + 128]
        gup = dot3_deep(n, du, TN)
        for b in range(2):
            grads[pl.ds(2 * f + b, D, stride=12), :] = gup[:, 128 * b : 128 * b + 128]
        grad[...] += dot3_deep(du, up, NT)
        return carry

    lax.fori_loop(0, CHUNKS, feed, 0)
    for here, copy in ship(grads, (keep, send), core, MLP_HALF, sems.at[pl.ds(13, 2)]):
        pl.when(here)(copy.start)
    grad[...] = cot[...] + unit_back(grad[...], norm2[...], scale2[...])
    kept[1].start()
    for copy in kept:
        copy.wait()
    for step in range(WINS * GROUPS):
        pltpu.make_async_copy(prob.at[step], prob_out.at[step], prob_sems.at[step]).wait()
    for here, copy in ship(grads, (keep, send), core, MLP_HALF, sems.at[pl.ds(13, 2)]):
        pl.when(here)(copy.wait)


def run_forward(tiles, edges, weights, bias, region, place):
    whole = pl.BlockSpec(memory_space=pl.ANY)
    probs = (WINS * GROUPS, PER * WT, WT)
    outs = [(MLP_HALF, 128), (MLP_HALF, 128), (TOK, D), (TOK, D), (TOK, 3 * D), probs, (TOK, D)]
    scratch = [
        pltpu.VMEM((TOK, D), F32),
        pltpu.VMEM((TOK, D), F32),
        pltpu.VMEM((TOK, 3 * D), F32),
        pltpu.VMEM((TOK, D), F32),
        pltpu.VMEM(probs, F32),
        pltpu.VMEM((TOK, D), BF16),
        pltpu.VMEM((TOK, D), BF16),
        pltpu.VMEM((TOK, D), BF16),
        pltpu.VMEM((TOK, D), BF16),
        pltpu.VMEM((TOK, D), F32),
        pltpu.VMEM((2 * MLP_ROWS, 128), F32),
        pltpu.VMEM((WINS, 1, WT), F32),
        pltpu.VMEM((WINS, WT, 1), F32),
        pltpu.VMEM((TOK, D), F32),
        pltpu.VMEM((TOK, 1), F32),
        pltpu.SemaphoreType.DMA((15,)),
        pltpu.SemaphoreType.DMA((WINS * GROUPS,)),
        *[pltpu.VMEM(a.shape, a.dtype) for a in (*weights, bias)],
    ]
    args = (*tiles, *edges, region, place, *weights, bias)
    return pl.pallas_call(
        forward_and_feed,
        out_shape=[jax.ShapeDtypeStruct(s, F32) for s in outs],
        in_specs=[VMEM] * 6 + [pl.BlockSpec(memory_space=pltpu.SMEM)] + [whole] * 9,
        out_specs=[whole] * len(outs),
        scratch_shapes=scratch,
        compiler_params=PARAMS,
        name="forward_and_feed",
    )(*args)


def attention_back(
    grad, ctx, wp_h, wp_l, place, qkv_in, x_in, prob_in,
    keep, send, dscore, dqkv_out,
    qkv, x, prob, dctx, dqkv, grads, sems, prob_sems,
):
    loads = [pltpu.make_async_copy(a, b, sems.at[i]) for i, (a, b) in enumerate(((qkv_in, qkv), (x_in, x)))]
    loads[0].start()
    for step in range(WINS * GROUPS):
        pltpu.make_async_copy(prob_in.at[step], prob.at[step], prob_sems.at[step]).start()
    loads[1].start()
    core = place[0]
    gm = split(grad[...])
    dctx[...] = dot3_deep(gm, (wp_h[...], wp_l[...]), NT)
    gproj = dot3_deep(split(ctx[...]), gm, TN)
    for b in range(3):
        grads[pl.ds(PROJ_AT + b, D, stride=3), :] = gproj[:, 128 * b : 128 * b + 128]
    dscore[...] = jnp.zeros_like(dscore)
    loads[0].wait()

    def attend_back(step, carry):
        w, g = step // GROUPS, step % GROUPS
        rows = pl.ds(pl.multiple_of(w * WT, 16), WT)
        q_at = pl.ds(pl.multiple_of(g * 128, 128), 128)
        k_at = pl.ds(pl.multiple_of(D + g * 128, 128), 128)
        v_at = pl.ds(pl.multiple_of(2 * D + g * 128, 128), 128)
        q = split(stacked(qkv[rows, q_at] * SCALE))
        k = split(qkv[rows, k_at])
        v = split(qkv[rows, v_at])
        d = split(stacked(dctx[rows, q_at]))
        pltpu.make_async_copy(prob_in.at[step], prob.at[step], prob_sems.at[step]).wait()
        p = prob[step]
        dp = dot3_deep(d, v, NT)
        ds = p * (dp - jnp.sum(dp * p, axis=-1, keepdims=True))
        dscore[g] += ds
        ps, dss = split(p), split(ds)
        dqkv[rows, v_at] = dot3_wide(ps, d, TN)
        dqkv[rows, q_at] = unstacked(dot3_wide(dss, k, NN)) * SCALE
        dqkv[rows, k_at] = dot3_wide(dss, q, TN)
        return carry

    lax.fori_loop(0, WINS * GROUPS, attend_back, 0, unroll=4)
    out = pltpu.make_async_copy(dqkv, dqkv_out, sems.at[2])
    out.start()
    loads[1].wait()
    gqkv = dot3_deep(split(unit(x[...])[0]), split(dqkv[...]), TN)
    for b in range(9):
        grads[pl.ds(b, D, stride=9), :] = gqkv[:, 128 * b : 128 * b + 128]
    for here, copy in ship(grads, (keep, send), core, ATT_HALF, sems.at[pl.ds(3, 2)]):
        pl.when(here)(copy.start)
    out.wait()
    for here, copy in ship(grads, (keep, send), core, ATT_HALF, sems.at[pl.ds(3, 2)]):
        pl.when(here)(copy.wait)


def run_attention_back(grad, ctx, wp_h, wp_l, place, qkv, x, prob):
    whole = pl.BlockSpec(memory_space=pl.ANY)
    outs = [(ATT_HALF, 128), (ATT_HALF, 128), (GROUPS, PER * WT, WT), (TOK, 3 * D)]
    return pl.pallas_call(
        attention_back,
        out_shape=[jax.ShapeDtypeStruct(s, F32) for s in outs],
        in_specs=[VMEM] * 4 + [pl.BlockSpec(memory_space=pltpu.SMEM)] + [whole] * 3,
        out_specs=[whole] * 2 + [VMEM, whole],
        scratch_shapes=[
            pltpu.VMEM((TOK, 3 * D), F32),
            pltpu.VMEM((TOK, D), F32),
            pltpu.VMEM(prob.shape, F32),
            pltpu.VMEM((TOK, D), F32),
            pltpu.VMEM((TOK, 3 * D), F32),
            pltpu.VMEM((UP_AT, 128), F32),
            pltpu.SemaphoreType.DMA((5,)),
            pltpu.SemaphoreType.DMA((WINS * GROUPS,)),
        ],
        compiler_params=PARAMS,
        name="attention_back",
    )(grad, ctx, wp_h, wp_l, place, qkv, x, prob)


def input_grad(x, grad, dqkv, wq_h, wq_l, o_l, o_e, o_s, o_c, total):
    n1, scale1 = unit(x[...])
    back = dot3_deep(split(dqkv[...]), (wq_h[...], wq_l[...]), NT)
    total[...] = grad[...] + unit_back(back, n1, scale1)
    scatter_windows(total, o_l, o_e, o_s, o_c)


def run_input_grad(x, grad, dqkv, wq_h, wq_l):
    halo = [(TILE, TILE, D), (TILE, 8, D), (SHIFT, TILE, D), (SHIFT, 8, D)]
    return pl.pallas_call(
        input_grad,
        out_shape=[jax.ShapeDtypeStruct(s, F32) for s in halo],
        in_specs=[VMEM] * 5,
        out_specs=[VMEM] * 4,
        scratch_shapes=[pltpu.VMEM((TOK, D), F32)],
        compiler_params=PARAMS,
        name="input_grad",
    )(x, grad, dqkv, wq_h, wq_l)


def run_block(tiles, edges, weights, bias, region, place):
    outs = [(HALF, 128), (HALF, 128), (GROUPS, PER * WT, WT), (TOK, D), (TOK, D), (TOK, 3 * D)]
    whole = pl.BlockSpec(memory_space=pl.ANY)
    scratch = [
        pltpu.VMEM((TOK, D), F32),
        pltpu.VMEM((TOK, D), F32),
        pltpu.VMEM((TOK, 3 * D), F32),
        pltpu.VMEM((TOK, D), F32),
        pltpu.VMEM((WINS * GROUPS, PER * WT, WT), F32),
        pltpu.VMEM((TOK, D), BF16),
        pltpu.VMEM((TOK, D), BF16),
        pltpu.VMEM((TOK, D), BF16),
        pltpu.VMEM((TOK, D), BF16),
        pltpu.VMEM((TOK, D), F32),
        pltpu.VMEM((TOK, 3 * D), F32),
        pltpu.VMEM((TOK, D), F32),
        pltpu.VMEM((ROWS, 128), F32),
        pltpu.VMEM((WINS, 1, WT), F32),
        pltpu.VMEM((WINS, WT, 1), F32),
        pltpu.VMEM((TOK, D), F32),
        pltpu.VMEM((TOK, 1), F32),
        pltpu.SemaphoreType.DMA((15,)),
        *[pltpu.VMEM(a.shape, a.dtype) for a in (*weights, bias)],
    ]
    args = (*tiles, *edges, region, place, *weights, bias)
    return pl.pallas_call(
        block_pass,
        out_shape=[jax.ShapeDtypeStruct(s, F32) for s in outs],
        in_specs=[VMEM] * 6 + [pl.BlockSpec(memory_space=pltpu.SMEM)] + [whole] * 9,
        out_specs=[whole] * 2 + [VMEM] + [whole] * 3,
        scratch_shapes=scratch,
        compiler_params=PARAMS,
        name="block_pass",
    )(*args)


def table_sum(scores, index, out, sums):
    sums[...] = jnp.zeros_like(sums)
    column = lax.broadcasted_iota(jnp.int32, (128, WT), 0)

    def one(i):
        line = index[pl.ds(i, 1), :]
        part = jnp.broadcast_to(line >> 7, (16, WT))
        hot = (column == jnp.broadcast_to(line & 127, (128, WT))).astype(F32).astype(BF16)
        high, low = split(scores[i])
        pieces = []
        for p in range(5):
            here = part == p
            pieces.append(jnp.where(here, high, jnp.zeros_like(high)))
            pieces.append(jnp.where(here, low, jnp.zeros_like(low)))
        return dot(jnp.concatenate(pieces, axis=0), hot, NT)

    def step(k, carry):
        at = 8 * k
        quads = [(one(at + i) + one(at + i + 1)) + (one(at + i + 2) + one(at + i + 3)) for i in (0, 4)]
        sums[...] += quads[0] + quads[1]
        return carry

    lax.fori_loop(0, WT // 8, step, 0)
    out[...] = jnp.zeros_like(out)
    for p in range(5):
        both = sums[32 * p : 32 * p + 16, :] + sums[32 * p + 16 : 32 * p + 32, :]
        out[HEADS * p : HEADS * p + HEADS, :] = both[:HEADS]


def table_gradient(dscore, index):
    scores = dscore.reshape(HEADS, WT, WT).transpose(1, 0, 2)
    scores = jnp.pad(scores, ((0, 0), (0, 4), (0, 0)))
    return pl.pallas_call(
        table_sum,
        out_shape=jax.ShapeDtypeStruct((64, 128), F32),
        in_specs=[VMEM] * 2,
        out_specs=VMEM,
        scratch_shapes=[pltpu.VMEM((160, 128), F32)],
        compiler_params=PARAMS,
        name="table_sum",
    )(scores, index)


def chip_order():
    return [(y_lo * 4 + x) * 16 + zy * 2 for y_lo in range(2) for x in range(4) for zy in range(8)]


def chip_groups():
    return [[d + core for d in chip_order()] for core in range(2)]


def core_swap():
    return [(d, d ^ 1) for d in range(128)]


def worker_of(d):
    return (d % 2) * 64 + d // 2


def piece_rounds():
    device = {worker_of(d): d for d in range(128)}
    edges = []
    for p in range(384):
        worker, slot = (p, 0) if p < 128 else ((p - 128) // 2, 1 + p % 2)
        edges.append((p // 3, p % 3, device[worker], slot))
    rounds = []
    while edges:
        by_owner = {}
        for e in edges:
            by_owner.setdefault(e[0], []).append(e)
        taken = {}

        def place_owner(owner, seen):
            for e in by_owner[owner]:
                if e[2] not in seen:
                    seen.add(e[2])
                    if e[2] not in taken or place_owner(taken[e[2]][0], seen):
                        taken[e[2]] = e
                        return True
            return False

        for owner in range(128):
            place_owner(owner, set())
        chosen = sorted(taken.values())
        rounds.append(chosen)
        edges = [e for e in edges if e not in chosen]
    return rounds


def looked_up(values, me):
    return lax.dynamic_slice_in_dim(jnp.asarray(values, jnp.int32), me, 1, 0)[0]


def in_order(came, order, me):
    stacked_parts = jnp.stack(came, axis=1)
    picked = [
        lax.dynamic_slice_in_dim(stacked_parts, looked_up([o[i] for o in order], me), 1, 1) for i in range(3)
    ]
    return jnp.concatenate(picked, axis=1)


def send_moments(moments, me):
    came = []
    for chosen in piece_rounds():
        piece = looked_up([e[1] for e in chosen], me)
        value = lax.dynamic_slice_in_dim(moments, piece, 1, 1)[:, 0]
        came.append(lax.ppermute(value, BOTH, [(e[0], e[2]) for e in chosen]))
    return came


def sorted_moments(came, me):
    order = [[0] * 3 for _ in range(128)]
    for r, chosen in enumerate(piece_rounds()):
        for e in chosen:
            order[e[2]][e[3]] = r
    return in_order(came, order, me)


def return_moments(moments, me):
    rounds = piece_rounds()
    came = []
    for chosen in rounds:
        slots = [0] * 128
        for e in chosen:
            slots[e[2]] = e[3]
        value = lax.dynamic_slice_in_dim(moments, looked_up(slots, me), 1, 1)[:, 0]
        came.append(lax.ppermute(value, BOTH, [(e[2], e[0]) for e in chosen]))
    order = [[0] * 3 for _ in range(128)]
    for r, chosen in enumerate(rounds):
        for e in chosen:
            order[e[0]][e[1]] = r
    return in_order(came, order, me)


def exchanged(value, groups):
    return lax.all_to_all(value, BOTH, 0, 0, axis_index_groups=groups, tiled=True)


def around(value, axis, by):
    size = lax.axis_size(axis)
    return lax.ppermute(value, axis, [(i, (i + by) % size) for i in range(size)])


def diagonal(value, by):
    lat, lon = lax.axis_size("lat"), lax.axis_size("lon")
    return lax.ppermute(
        value,
        BOTH,
        [
            (a * lon + o, ((a + by) % lat) * lon + (o + by) % lon)
            for a in range(lat)
            for o in range(lon)
        ],
    )


def pack(x_east, x_south, c_east, c_south, east, south, corner):
    for i, (e, t) in enumerate(((x_east, x_south), (c_east, c_south))):
        east[i] = e[...]
        south[i] = t[...]
        corner[i] = t[:, 0:8, :]


def edges_of(x, c):
    east_in = pl.BlockSpec((TILE, 8, D), lambda i: (0, 0, 0))
    south_in = pl.BlockSpec((SHIFT, TILE, D), lambda i: (0, 0, 0))
    shapes = [(2, TILE, 8, D), (2, SHIFT, TILE, D), (2, SHIFT, 8, D)]
    east, south, corner = pl.pallas_call(
        pack,
        out_shape=[jax.ShapeDtypeStruct(s, F32) for s in shapes],
        grid=(1,),
        in_specs=[east_in, south_in] * 2,
        out_specs=[pl.BlockSpec(s, lambda i: (0, 0, 0, 0)) for s in shapes],
        compiler_params=PARAMS,
        name="pack",
    )(x, x, c, c)
    return around(east, "lon", -1), around(south, "lat", -1), diagonal(corner, -1)


def merge(keep, came, line, line_came, out):
    for q in range(BATCH):
        rows = slice(q * OWN_ATT, q * OWN_ATT + OWN_ATT)
        out[q * SUM_BLOCK : q * SUM_BLOCK + OWN_ATT, :] = keep[rows, :] + came[rows, :]
        out[q * SUM_BLOCK + OWN_ATT : (q + 1) * SUM_BLOCK, :] = line[q : q + 1, :] + line_came[q : q + 1, :]


def merged(keep, came, line, line_came):
    halves = pl.BlockSpec((BATCH * OWN_ATT, 128), lambda i: (i, 0))
    lines = pl.BlockSpec((BATCH, 128), lambda i: (i, 0))
    return pl.pallas_call(
        merge,
        out_shape=jax.ShapeDtypeStruct((64 * SUM_BLOCK, 128), F32),
        grid=(64 // BATCH,),
        in_specs=[halves, halves, lines, lines],
        out_specs=pl.BlockSpec((BATCH * SUM_BLOCK, 128), lambda i: (i, 0)),
        compiler_params=PARAMS,
        name="merge",
    )(keep, came, line, line_came)


def add(keep, came, out):
    out[...] = keep[...] + came[...]


def added(keep, came):
    rows = pl.BlockSpec((MLP_HALF // 4, 128), lambda i: (i, 0))
    return pl.pallas_call(
        add,
        out_shape=jax.ShapeDtypeStruct((MLP_HALF, 128), F32),
        grid=(4,),
        in_specs=[rows] * 2,
        out_specs=rows,
        compiler_params=PARAMS,
        name="add",
    )(keep, came)


def adam(mlp, parts, weights, first, second, new, first_new, second_new, factor):
    total = parts[0:SUM_BLOCK, :]
    for q in range(1, 64):
        total = total + parts[q * SUM_BLOCK : q * SUM_BLOCK + SUM_BLOCK, :]
    total = total * factor
    deep = mlp[0:OWN_MLP, :]
    for q in range(1, 64):
        deep = deep + mlp[q * OWN_MLP : q * OWN_MLP + OWN_MLP, :]
    grad = jnp.concatenate([total[:OWN_ATT], deep * factor], axis=0)
    m = 0.9 * first[...] + 0.1 * grad
    s = 0.95 * second[...] + 0.05 * grad * grad
    first_new[...] = m
    second_new[...] = s
    fresh = weights[...] - 0.01 * m / (jnp.sqrt(s) + 1e-08)
    fresh = jnp.concatenate([fresh, total[OWN_ATT:]], axis=0)
    for q in range(64):
        new[q * BLOCK : q * BLOCK + BLOCK, :] = fresh


def lay_out(other, place, blocks, *refs):
    out, att, mlp, sems = refs[-4:]
    i = pl.program_id(0)
    half = (1 - place[0]) if other else place[0]
    for q in range(BATCH):
        at = q * BLOCK
        att[i, q * OWN_ATT : (q + 1) * OWN_ATT, :] = blocks[at : at + OWN_ATT, :]
        mlp[i, q * OWN_MLP : (q + 1) * OWN_MLP, :] = blocks[at + OWN_ATT : at + OWN, :]

    def copies(step):
        rows, more = BATCH * OWN_ATT, BATCH * OWN_MLP
        yield pltpu.make_async_copy(
            att.at[step],
            out.at[pl.ds(pl.multiple_of(half * ATT_HALF + step * rows, 8), rows)],
            sems.at[0, step],
        )
        yield pltpu.make_async_copy(
            mlp.at[step],
            out.at[pl.ds(pl.multiple_of(UP_AT + half * MLP_HALF + step * more, 8), more)],
            sems.at[1, step],
        )

    for copy in copies(i):
        copy.start()

    @pl.when(i == 64 // BATCH - 1)
    def _():
        for step in range(64 // BATCH):
            for copy in copies(step):
                copy.wait()


def lay_out_own(place, blocks, lines, out, *scratch):
    for q in range(BATCH):
        lines[q : q + 1, :] = blocks[q * BLOCK + OWN : q * BLOCK + BLOCK, :]
    lay_out(False, place, blocks, out, *scratch)


def half_weights(place, blocks, so_far):
    steps = 64 // BATCH
    whole = pl.BlockSpec(memory_space=pl.ANY)
    blocks_in = pl.BlockSpec((BATCH * BLOCK, 128), lambda i, spot: (i, 0))
    weights_out = jax.ShapeDtypeStruct((ROWS, 128), F32)
    scratch = [
        pltpu.VMEM((steps, BATCH * OWN_ATT, 128), F32),
        pltpu.VMEM((steps, BATCH * OWN_MLP, 128), F32),
        pltpu.SemaphoreType.DMA((2, steps)),
    ]
    if so_far is None:
        return pl.pallas_call(
            lay_out_own,
            out_shape=[jax.ShapeDtypeStruct((64, 128), F32), weights_out],
            grid_spec=pltpu.PrefetchScalarGridSpec(
                num_scalar_prefetch=1,
                grid=(steps,),
                in_specs=[blocks_in],
                out_specs=[pl.BlockSpec((BATCH, 128), lambda i, spot: (i, 0)), whole],
                scratch_shapes=scratch,
            ),
            compiler_params=PARAMS,
            name="lay_out_own",
        )(place, blocks)
    return pl.pallas_call(
        functools.partial(lay_out, True),
        out_shape=weights_out,
        grid_spec=pltpu.PrefetchScalarGridSpec(
            num_scalar_prefetch=1,
            grid=(steps,),
            in_specs=[blocks_in, whole],
            out_specs=whole,
            scratch_shapes=scratch,
        ),
        input_output_aliases={2: 0},
        compiler_params=PARAMS,
        name="lay_out_other",
    )(place, blocks, so_far)


def per_device(
    block_input, cotangent, weights, first_moment, second_moment, bias_table, bias_index, region_ids
):
    lat_at, lon_at = lax.axis_index("lat"), lax.axis_index("lon")
    factor = 1.0 / math.sqrt(TOK * 128)
    flat = weights.reshape(ROWS, 128)
    *pairs, bias = prepared(flat, bias_table, bias_index)
    edges = edges_of(block_input, cotangent)
    core = lon_at % 2
    place = jnp.stack([core, (lat_at == 7).astype(jnp.int32)]).astype(jnp.int32)
    me = lat_at * 16 + lon_at
    keep, send, x, grad, qkv, prob, ctx = run_forward(
        (block_input, cotangent), edges, pairs, bias, region_ids, place
    )
    came = lax.ppermute(send, BOTH, core_swap())
    _, first_moment, second_moment = lax.optimization_barrier((send, first_moment, second_moment))
    moments = jnp.stack([first_moment, second_moment]).reshape(2, 3, OWN_ATT * 128)
    moments = send_moments(moments, me)
    worker = core * 64 + lat_at * 8 + lon_at // 2
    own = jnp.concatenate(
        [
            lax.dynamic_slice_in_dim(flat, worker * OWN_ATT, OWN_ATT, 0),
            lax.dynamic_slice_in_dim(flat, UP_AT + worker * OWN_MLP, OWN_MLP, 0),
        ]
    )
    came, moments = lax.optimization_barrier((came, moments))
    mlp_sum = added(keep, came)
    mlp_parts = exchanged(mlp_sum.reshape(64, 1, OWN_MLP * 128), chip_groups())

    _, qkv, ctx, grad = lax.optimization_barrier((mlp_sum, qkv, ctx, grad))
    keep, send, dscore, dqkv = run_attention_back(grad, ctx, pairs[2], pairs[3], place, qkv, x, prob)
    came = lax.ppermute(send, BOTH, core_swap())
    line = table_gradient(dscore, bias_index)
    line_came = lax.ppermute(line, BOTH, core_swap())
    att_sum = merged(keep, came, line, line_came)
    att_sum, mlp_parts = lax.optimization_barrier((att_sum, mlp_parts))
    att_parts = exchanged(att_sum.reshape(64, 1, SUM_BLOCK * 128), chip_groups())
    _, own, moments = lax.optimization_barrier((att_sum, own, moments))
    moments = sorted_moments(moments, me).reshape(2, OWN, 128)
    new, first_new, second_new = pl.pallas_call(
        functools.partial(adam, factor=factor),
        out_shape=[jax.ShapeDtypeStruct((n, 128), F32) for n in (64 * BLOCK, OWN, OWN)],
        in_specs=[VMEM] * 5,
        out_specs=[VMEM] * 3,
        compiler_params=PARAMS,
        name="adam",
    )(mlp_parts.reshape(MLP_HALF, 128), att_parts.reshape(64 * SUM_BLOCK, 128), own, moments[0], moments[1])
    mine = exchanged(new.reshape(64, 1, BLOCK * 128), chip_groups())

    _, dqkv, first_new, second_new = lax.optimization_barrier((new, dqkv, first_new, second_new))
    o_l, o_e, o_s, o_c = run_input_grad(x, grad, dqkv, pairs[0], pairs[1])
    from_west = around(o_e, "lon", 1)
    from_north = around(o_s, "lat", 1)
    from_corner = diagonal(o_c, 1)
    moments = jnp.stack([first_new, second_new]).reshape(2, 3, OWN_ATT * 128)
    moments = return_moments(moments, me).reshape(2, -1)
    top = jnp.concatenate([from_corner[:, :SHIFT], from_north[:, SHIFT:]], axis=1)
    rest = jnp.concatenate([from_west[SHIFT:, :SHIFT], o_l[SHIFT:, SHIFT:]], axis=1)
    grad_input = jnp.concatenate([top, rest], axis=0)
    mine, moments, grad_input = lax.optimization_barrier((mine, moments, grad_input))

    mine = mine.reshape(64 * BLOCK, 128)
    theirs = lax.ppermute(mine, BOTH, core_swap())
    table, weights_new = half_weights(place, mine, None)
    table_new = table[: HEADS * 5].reshape(5, HEADS, 128).transpose(1, 0, 2)
    table_new = table_new.reshape(HEADS, 640)[:, :BIAS]
    weights_new = half_weights(place, theirs, weights_new)
    return (grad_input, weights_new.reshape(-1), moments[0], moments[1], table_new)


def solution(mesh):
    placed = (
        P("lat", "lon", None),
        P("lat", "lon", None),
        P(),
        P(BOTH),
        P(BOTH),
        P(),
        P(),
        P("lat", "lon"),
    )
    return jax.shard_map(
        per_device,
        mesh=mesh,
        in_specs=placed,
        out_specs=(P("lat", "lon", None), P(), P(BOTH), P(BOTH), P()),
        check_vma=False,
    )
```

```python
import functools
import math

import jax
import jax.numpy as jnp
from jax import lax
from jax.experimental import pallas as pl
from jax.experimental.pallas import tpu as pltpu
from jax.sharding import PartitionSpec as P

D = 384
HEADS = 12
FF = 1536
WIN = 12
SHIFT = 6
WT = WIN * WIN
TILE = 24
TOK = TILE * TILE
WINS = TOK // WT
GROUPS = 3
PER = 4
QKV_ROWS = D * 3 * D // 128
PROJ_ROWS = D * D // 128
MLP_ROWS = D * FF // 128
PROJ_AT = QKV_ROWS
UP_AT = QKV_ROWS + PROJ_ROWS
DOWN_AT = UP_AT + MLP_ROWS
ROWS = DOWN_AT + MLP_ROWS
CHUNK = 256
CHUNKS = FF // CHUNK
HALF = ROWS // 2
OWN = ROWS // 128
BLOCK = OWN + 1
BATCH = 32
BIAS = 529
BOTH = ("lat", "lon")
F32 = jnp.float32
BF16 = jnp.bfloat16
VMEM = pl.BlockSpec(memory_space=pltpu.VMEM)
PARAMS = pltpu.CompilerParams(vmem_limit_bytes=58 * 1024 * 1024)

NN = (((1,), (0,)), ((), ()))
NT = (((1,), (1,)), ((), ()))
TN = (((0,), (0,)), ((), ()))


def split(value):
    high = value.astype(BF16)
    return high, (value - high.astype(F32)).astype(BF16)


def dot(a, b, dims):
    return lax.dot_general(a, b, dims, preferred_element_type=F32)


def dot3(a, b, dims):
    return dot(a[0], b[0], dims) + dot(a[0], b[1], dims) + dot(a[1], b[0], dims)


def dot3_deep(a, b, dims):
    (x,), (y,) = dims[0]
    left = jnp.concatenate([a[0], a[0], a[1]], axis=x)
    right = jnp.concatenate([b[0], b[1], b[0]], axis=y)
    return dot(left, right, dims)


def dot3_wide(a, b, dims):
    wide = dot(a[0], jnp.concatenate([b[0], b[1]], axis=1), dims)
    return wide[:, :128] + wide[:, 128:] + dot(a[1], b[0], dims)


def unit(value):
    center = value - jnp.mean(value, axis=-1, keepdims=True)
    scale = lax.rsqrt(jnp.mean(center * center, axis=-1, keepdims=True) + 1e-05)
    return center * scale, scale


def unit_back(grad, normed, scale):
    mean = jnp.mean(grad, axis=-1, keepdims=True)
    along = jnp.mean(grad * normed, axis=-1, keepdims=True)
    return scale * (grad - mean - normed * along)


STEPS = 6


def prepare(qkv, proj, up, down, table, index, wq_h, wq_l, wp_h, wp_l, wu_h, wu_l, wd_h, wd_l, bias):
    for flat, rows, blocks, high, low in (
        (qkv, D // STEPS, 9, wq_h, wq_l),
        (proj, D // STEPS, 3, wp_h, wp_l),
        (down, FF // STEPS, 3, wd_h.at[0], wd_l.at[0]),
    ):
        for b in range(blocks):
            h, l = split(flat[pl.ds(b, rows, stride=blocks), :])
            high[:, 128 * b : 128 * b + 128] = h
            low[:, 128 * b : 128 * b + 128] = l
    for f in range(CHUNKS):
        for b in range(2):
            h, l = split(up[pl.ds(2 * f + b, D // STEPS, stride=12), :])
            wu_h[f, :, 128 * b : 128 * b + 128] = h
            wu_l[f, :, 128 * b : 128 * b + 128] = l
    lines = jnp.concatenate([table[...], jnp.zeros((HEADS, 640 - BIAS), F32)], axis=1)
    for k in range(WT // 8 // STEPS):
        at = pl.multiple_of((pl.program_id(0) * (WT // 8 // STEPS) + k) * 8, 8)
        columns = index[pl.ds(at, 8), :]
        columns = jnp.concatenate([columns, jnp.zeros((8, 256 - WT), jnp.int32)], axis=1)
        low = columns & 127
        part = columns >> 7
        for h in range(HEADS):
            found = jnp.zeros((8, 256), F32)
            for p in range(5):
                line = jnp.broadcast_to(lines[h : h + 1, 128 * p : 128 * p + 128], (8, 128))
                taken = jnp.concatenate(
                    [
                        jnp.take_along_axis(line, low[:, :128], axis=1),
                        jnp.take_along_axis(line, low[:, 128:], axis=1),
                    ],
                    axis=1,
                )
                found = jnp.where(part == p, taken, found)
            bias[h // PER, pl.ds(pl.multiple_of((h % PER) * WT + at, 8), 8), :] = found[:, :WT]


def prepared(flat, table, index):
    shapes = [(D, 3 * D)] * 2 + [(D, D)] * 2 + [(CHUNKS, D, CHUNK)] * 2 + [(CHUNKS, CHUNK, D)] * 2
    piece = D // STEPS
    outs = [
        *[pl.BlockSpec((piece, 3 * D), lambda i: (i, 0))] * 2,
        *[pl.BlockSpec((piece, D), lambda i: (i, 0))] * 2,
        *[pl.BlockSpec((CHUNKS, piece, CHUNK), lambda i: (0, i, 0))] * 2,
        *[pl.BlockSpec((1, CHUNK, D), lambda i: (i, 0, 0))] * 2,
        pl.BlockSpec((GROUPS, PER * WT, WT), lambda i: (0, 0, 0)),
    ]

    def part(at, rows):
        return pl.BlockSpec((rows // STEPS, 128), lambda i: (at * STEPS // rows + i, 0))

    return pl.pallas_call(
        prepare,
        out_shape=[jax.ShapeDtypeStruct(s, BF16) for s in shapes]
        + [jax.ShapeDtypeStruct((GROUPS, PER * WT, WT), F32)],
        grid=(STEPS,),
        in_specs=[
            part(0, QKV_ROWS),
            part(PROJ_AT, PROJ_ROWS),
            part(UP_AT, MLP_ROWS),
            part(DOWN_AT, MLP_ROWS),
            pl.BlockSpec((HEADS, BIAS), lambda i: (0, 0)),
            pl.BlockSpec((WT, WT), lambda i: (0, 0)),
        ],
        out_specs=outs,
        compiler_params=PARAMS,
        name="prepare",
    )(flat, flat, flat, flat, table, index)


INNER = TILE - SHIFT
EDGE = 112
CORNER = 40


def window_rows():
    for wr in range(2):
        for wc in range(2):
            for r in range(WIN):
                yield (wr * 2 + wc) * WT + r * WIN, wc, wr * WIN + r


def gather_windows(target, local, east, south, corner):
    for at, wc, row in window_rows():
        k, n = row + SHIFT, row - INNER
        if wc == 0:
            target[at : at + WIN, :] = (
                local[k, SHIFT : SHIFT + WIN, :] if n < 0 else south[INNER * n : INNER * n + WIN, :]
            )
        else:
            target[at : at + SHIFT, :] = (
                local[k, SHIFT + WIN : TILE, :] if n < 0 else south[INNER * n + WIN : INNER * n + INNER, :]
            )
            target[at + SHIFT : at + WIN, :] = (
                east[SHIFT * row : SHIFT * row + SHIFT, :] if n < 0 else corner[SHIFT * n : SHIFT * n + SHIFT, :]
            )


def scatter_windows(source, local, east, south, corner):
    for at, wc, row in window_rows():
        k, n = row + SHIFT, row - INNER
        near = source[at : at + (WIN if wc == 0 else SHIFT), :]
        if n < 0:
            first = SHIFT if wc == 0 else SHIFT + WIN
            local[k, first : first + near.shape[0], :] = near
        else:
            first = INNER * n + (0 if wc == 0 else WIN)
            south[first : first + near.shape[0], :] = near
        if wc == 1:
            far = source[at + SHIFT : at + WIN, :]
            if n < 0:
                east[SHIFT * row : SHIFT * row + SHIFT, :] = far
            else:
                corner[SHIFT * n : SHIFT * n + SHIFT, :] = far


def head_lane():
    return lax.broadcasted_iota(jnp.int32, (WT, 128), 1) >> 5


def stacked(value):
    lane = head_lane()
    return jnp.concatenate([jnp.where(lane == h, value, 0.0) for h in range(PER)], axis=0)


def unstacked(value):
    lane = head_lane()
    total = jnp.where(lane == 0, value[:WT], 0.0)
    for h in range(1, PER):
        total = jnp.where(lane == h, value[h * WT : h * WT + WT], total)
    return total


def find_labels(region, last, label_row, label_col):
    eye = lax.broadcasted_iota(jnp.int32, (WT, WT), 0) == lax.broadcasted_iota(jnp.int32, (WT, WT), 1)
    for wr in range(2):
        for wc in range(2):
            w = wr * 2 + wc
            pieces = []
            for r in range(WIN):
                row = wr * WIN + r
                ids = region[row : row + 1, wc * WIN : wc * WIN + WIN]
                pieces.append(ids + (4 * last if row >= TILE - SHIFT else 0))
            line = jnp.concatenate(pieces, axis=1).astype(F32)
            label_row[w] = line
            wide = jnp.where(eye, jnp.broadcast_to(line, (WT, WT)), 0.0)
            label_col[w] = jnp.sum(wide, axis=1, keepdims=True)


SCALE = 1.0 / math.sqrt(32.0)


def block_pass(
    x_l, c_l, east, south, corner, region, place, *rest
):
    stored, rest = rest[:9], rest[9:]
    (
    keep, send, dscore, x_out, grad_out, dqkv_out,
    x, cot, qkv, ctx, prob, n2h, n2l, ch, cl, grad, dqkv, dctx, grads, label_row, label_col, norm2, scale2, sems,
    ) = rest[:-9]
    held = rest[-9:]
    wq_h, wq_l, wp_h, wp_l, wu_h, wu_l, wd_h, wd_l, bias = held
    loads = [pltpu.make_async_copy(a, b, sems.at[i]) for i, (a, b) in enumerate(zip(stored, held))]
    for i in (0, 1, 8, 2, 3, 4, 5, 6, 7):
        loads[i].start()
    core = place[0]

    def piece(i, half, start, rows):
        source = grads.at[pl.ds(start, rows)]
        spot = pl.ds(start - half * HALF, rows)
        for target, here in ((keep, core == half), (send, core != half)):
            yield here, pltpu.make_async_copy(source, target.at[spot], sems.at[9 + i])

    def start(*what):
        for here, copy in piece(*what):
            pl.when(here)(copy.start)

    def finish(*what):
        for here, copy in piece(*what):
            pl.when(here)(copy.wait)

    pieces = (
        (0, 1, HALF, HALF),
        (1, 0, UP_AT, HALF - UP_AT),
        (2, 0, 0, UP_AT),
    )
    find_labels(region, place[1], label_row, label_col)
    gather_windows(x, x_l, east.at[0], south.at[0], corner.at[0])
    kept = [
        pltpu.make_async_copy(a, b, sems.at[12 + i])
        for i, (a, b) in enumerate(((x, x_out), (grad, grad_out), (dqkv, dqkv_out)))
    ]
    kept[0].start()
    gather_windows(cot, c_l, east.at[1], south.at[1], corner.at[1])
    n1 = split(unit(x[...])[0])
    loads[0].wait()
    loads[1].wait()
    qkv[...] = dot3_deep(n1, (wq_h[...], wq_l[...]), NN)

    loads[8].wait()

    def attend(step, carry):
        w, g = step // GROUPS, step % GROUPS
        rows = pl.ds(pl.multiple_of(w * WT, 16), WT)
        lanes = pl.ds(pl.multiple_of(g * 128, 128), 128)
        q = split(stacked(qkv[rows, pl.ds(pl.multiple_of(g * 128, 128), 128)] * SCALE))
        k = split(qkv[rows, pl.ds(pl.multiple_of(D + g * 128, 128), 128)])
        v = split(qkv[rows, pl.ds(pl.multiple_of(2 * D + g * 128, 128), 128)])
        allowed = label_col[w] == label_row[w]
        score = dot3_deep(q, k, NT) + bias[g]
        score = jnp.where(jnp.concatenate([allowed] * PER, axis=0), score, -jnp.inf)
        raised = jnp.exp(score - jnp.max(score, axis=-1, keepdims=True))
        p = raised * (1.0 / jnp.sum(raised, axis=-1, keepdims=True))
        prob[step] = p
        ctx[rows, lanes] = unstacked(dot3_wide(split(p), v, NN))
        return carry

    lax.fori_loop(0, WINS * GROUPS, attend, 0, unroll=12)

    for i in range(2, 8):
        loads[i].wait()
    mixed = x[...] + dot3_deep(split(ctx[...]), (wp_h[...], wp_l[...]), NN)
    norm2[...], scale2[...] = unit(mixed)
    n2h[...], n2l[...] = split(norm2[...])
    ch[...], cl[...] = split(cot[...])
    grad[...] = jnp.zeros_like(grad)

    def feed(f, carry):
        n = (n2h[...], n2l[...])
        c = (ch[...], cl[...])
        up = (wu_h[f], wu_l[f])
        u = dot3_deep(n, up, NN)
        back = dot3_deep(c, (wd_h[f], wd_l[f]), NT)
        inner = 0.7978845608028654 * (u + 0.044715 * u * u * u)
        t = jnp.tanh(inner)
        hidden = split(0.5 * u * (1.0 + t))
        slope = 0.5 * (1.0 + t) + 0.5 * u * (1.0 - t * t) * (
            0.7978845608028654 * (1.0 + 3.0 * 0.044715 * u * u)
        )
        du = split(back * slope)
        gdown = dot3_deep(hidden, c, TN)
        for b in range(3):
            grads[pl.ds(DOWN_AT + 3 * CHUNK * f + b, CHUNK, stride=3), :] = gdown[:, 128 * b : 128 * b + 128]
        gup = dot3_deep(n, du, TN)
        for b in range(2):
            grads[pl.ds(UP_AT + 2 * f + b, D, stride=12), :] = gup[:, 128 * b : 128 * b + 128]
        grad[...] += dot3_deep(du, up, NT)
        return carry

    lax.fori_loop(0, CHUNKS, feed, 0)

    start(*pieces[0])
    start(*pieces[1])
    grad[...] = cot[...] + unit_back(grad[...], norm2[...], scale2[...])
    kept[1].start()
    gm = split(grad[...])
    dctx[...] = dot3_deep(gm, (wp_h[...], wp_l[...]), NT)
    gproj = dot3_deep(split(ctx[...]), gm, TN)
    for b in range(3):
        grads[pl.ds(PROJ_AT + b, D, stride=3), :] = gproj[:, 128 * b : 128 * b + 128]
    dscore[...] = jnp.zeros_like(dscore)

    def attend_back(step, carry):
        w, g = step // GROUPS, step % GROUPS
        rows = pl.ds(pl.multiple_of(w * WT, 16), WT)
        q_at = pl.ds(pl.multiple_of(g * 128, 128), 128)
        k_at = pl.ds(pl.multiple_of(D + g * 128, 128), 128)
        v_at = pl.ds(pl.multiple_of(2 * D + g * 128, 128), 128)
        q = split(stacked(qkv[rows, q_at] * SCALE))
        k = split(qkv[rows, k_at])
        v = split(qkv[rows, v_at])
        d = split(stacked(dctx[rows, q_at]))
        p = prob[step]
        dp = dot3_deep(d, v, NT)
        ds = p * (dp - jnp.sum(dp * p, axis=-1, keepdims=True))
        dscore[g] += ds
        ps, dss = split(p), split(ds)
        dqkv[rows, v_at] = dot3_wide(ps, d, TN)
        dqkv[rows, q_at] = unstacked(dot3_wide(dss, k, NN)) * SCALE
        dqkv[rows, k_at] = dot3_wide(dss, q, TN)
        return carry

    lax.fori_loop(0, WINS * GROUPS, attend_back, 0, unroll=4)

    kept[2].start()
    dq = split(dqkv[...])
    gqkv = dot3_deep(split(unit(x[...])[0]), dq, TN)
    for b in range(9):
        grads[pl.ds(b, D, stride=9), :] = gqkv[:, 128 * b : 128 * b + 128]
    start(*pieces[2])
    for copy in kept:
        copy.wait()
    for what in pieces:
        finish(*what)


def input_grad(x, grad, dqkv, wq_h, wq_l, o_l, o_e, o_s, o_c, total):
    n1, scale1 = unit(x[...])
    back = dot3_deep(split(dqkv[...]), (wq_h[...], wq_l[...]), NT)
    total[...] = grad[...] + unit_back(back, n1, scale1)
    scatter_windows(total, o_l, o_e, o_s, o_c)


def run_input_grad(x, grad, dqkv, wq_h, wq_l):
    halo = [(TILE, TILE, D), (EDGE, D), (EDGE, D), (CORNER, D)]
    return pl.pallas_call(
        input_grad,
        out_shape=[jax.ShapeDtypeStruct(s, F32) for s in halo],
        in_specs=[VMEM] * 5,
        out_specs=[VMEM] * 4,
        scratch_shapes=[pltpu.VMEM((TOK, D), F32)],
        compiler_params=PARAMS,
        name="input_grad",
    )(x, grad, dqkv, wq_h, wq_l)


def run_block(tiles, edges, weights, bias, region, place):
    outs = [(HALF, 128), (HALF, 128), (GROUPS, PER * WT, WT), (TOK, D), (TOK, D), (TOK, 3 * D)]
    whole = pl.BlockSpec(memory_space=pl.ANY)
    scratch = [
        pltpu.VMEM((TOK, D), F32),
        pltpu.VMEM((TOK, D), F32),
        pltpu.VMEM((TOK, 3 * D), F32),
        pltpu.VMEM((TOK, D), F32),
        pltpu.VMEM((WINS * GROUPS, PER * WT, WT), F32),
        pltpu.VMEM((TOK, D), BF16),
        pltpu.VMEM((TOK, D), BF16),
        pltpu.VMEM((TOK, D), BF16),
        pltpu.VMEM((TOK, D), BF16),
        pltpu.VMEM((TOK, D), F32),
        pltpu.VMEM((TOK, 3 * D), F32),
        pltpu.VMEM((TOK, D), F32),
        pltpu.VMEM((ROWS, 128), F32),
        pltpu.VMEM((WINS, 1, WT), F32),
        pltpu.VMEM((WINS, WT, 1), F32),
        pltpu.VMEM((TOK, D), F32),
        pltpu.VMEM((TOK, 1), F32),
        pltpu.SemaphoreType.DMA((15,)),
        *[pltpu.VMEM(a.shape, a.dtype) for a in (*weights, bias)],
    ]
    args = (*tiles, *edges, region, place, *weights, bias)
    return pl.pallas_call(
        block_pass,
        out_shape=[jax.ShapeDtypeStruct(s, F32) for s in outs],
        in_specs=[VMEM] * 6 + [pl.BlockSpec(memory_space=pltpu.SMEM)] + [whole] * 9,
        out_specs=[whole] * 2 + [VMEM] + [whole] * 3,
        scratch_shapes=scratch,
        compiler_params=PARAMS,
        name="block_pass",
    )(*args)


def table_sum(by_head, index, out, sums, scores):
    sums[...] = jnp.zeros_like(sums)
    for h in range(16):
        if h < HEADS:
            scores[:, h, :] = by_head[h // PER, (h % PER) * WT : (h % PER) * WT + WT, :]
        else:
            scores[:, h, :] = jnp.zeros((WT, WT), F32)
    column = lax.broadcasted_iota(jnp.int32, (128, WT), 0)

    def one(i):
        line = index[pl.ds(i, 1), :]
        part = jnp.broadcast_to(line >> 7, (16, WT))
        hot = (column == jnp.broadcast_to(line & 127, (128, WT))).astype(F32).astype(BF16)
        high, low = split(scores[i])
        pieces = []
        for p in range(5):
            here = part == p
            pieces.append(jnp.where(here, high, jnp.zeros_like(high)))
            pieces.append(jnp.where(here, low, jnp.zeros_like(low)))
        return dot(jnp.concatenate(pieces, axis=0), hot, NT)

    def step(k, carry):
        at = 8 * k
        quads = [(one(at + i) + one(at + i + 1)) + (one(at + i + 2) + one(at + i + 3)) for i in (0, 4)]
        sums[...] += quads[0] + quads[1]
        return carry

    lax.fori_loop(0, WT // 8, step, 0)
    out[...] = jnp.zeros_like(out)
    for p in range(5):
        both = sums[32 * p : 32 * p + 16, :] + sums[32 * p + 16 : 32 * p + 32, :]
        out[HEADS * p : HEADS * p + HEADS, :] = both[:HEADS]


def table_gradient(dscore, index):
    return pl.pallas_call(
        table_sum,
        out_shape=jax.ShapeDtypeStruct((64, 128), F32),
        in_specs=[VMEM] * 2,
        out_specs=VMEM,
        scratch_shapes=[pltpu.VMEM((160, 128), F32), pltpu.VMEM((WT, 16, WT), F32)],
        compiler_params=PARAMS,
        name="table_sum",
    )(dscore, index)


def chip_order():
    return [(y_lo * 4 + x) * 16 + zy * 2 for y_lo in range(2) for x in range(4) for zy in range(8)]


def chip_groups():
    return [[d + core for d in chip_order()] for core in range(2)]


def core_swap():
    return [(d, d ^ 1) for d in range(128)]


def worker_pairs():
    return [(core * 64 + q, d + core) for core in range(2) for q, d in enumerate(chip_order())]


def exchanged(value, groups):
    return lax.all_to_all(value, BOTH, 0, 0, axis_index_groups=groups, tiled=True)


def around(value, axis, by):
    size = lax.axis_size(axis)
    return lax.ppermute(value, axis, [(i, (i + by) % size) for i in range(size)])


def diagonal(value, by):
    lat, lon = lax.axis_size("lat"), lax.axis_size("lon")
    return lax.ppermute(
        value,
        BOTH,
        [
            (a * lon + o, ((a + by) % lat) * lon + (o + by) % lon)
            for a in range(lat)
            for o in range(lon)
        ],
    )


def pack(x, c, east, south, corner):
    for i, tile in enumerate((x, c)):
        for k in range(SHIFT, TILE):
            east[i, SHIFT * (k - SHIFT) : SHIFT * (k - SHIFT) + SHIFT, :] = tile[k, 0:SHIFT, :]
        for n in range(SHIFT):
            south[i, INNER * n : INNER * n + INNER, :] = tile[n, SHIFT:TILE, :]
            corner[i, SHIFT * n : SHIFT * n + SHIFT, :] = tile[n, 0:SHIFT, :]


def edges_of(x, c):
    shapes = [(2, EDGE, D), (2, EDGE, D), (2, CORNER, D)]
    east, south, corner = pl.pallas_call(
        pack,
        out_shape=[jax.ShapeDtypeStruct(s, F32) for s in shapes],
        in_specs=[VMEM] * 2,
        out_specs=[VMEM] * 3,
        compiler_params=PARAMS,
        name="pack",
    )(x, c)
    return around(east, "lon", -1), around(south, "lat", -1), diagonal(corner, -1)


def unpack_edges(local, west, north, corner, out):
    out[SHIFT:TILE, SHIFT:TILE, :] = local[SHIFT:TILE, SHIFT:TILE, :]
    for k in range(SHIFT, TILE):
        out[k, 0:SHIFT, :] = west[SHIFT * (k - SHIFT) : SHIFT * (k - SHIFT) + SHIFT, :]
    for n in range(SHIFT):
        out[n, SHIFT:TILE, :] = north[INNER * n : INNER * n + INNER, :]
        out[n, 0:SHIFT, :] = corner[SHIFT * n : SHIFT * n + SHIFT, :]


def with_edges(local, west, north, corner):
    return pl.pallas_call(
        unpack_edges,
        out_shape=jax.ShapeDtypeStruct((TILE, TILE, D), F32),
        in_specs=[VMEM] * 4,
        out_specs=VMEM,
        compiler_params=PARAMS,
        name="unpack_edges",
    )(local, west, north, corner)


def merge(keep, came, line, line_came, out):
    for q in range(BATCH):
        rows = slice(q * OWN, q * OWN + OWN)
        out[q * BLOCK : q * BLOCK + OWN, :] = keep[rows, :] + came[rows, :]
        out[q * BLOCK + OWN : (q + 1) * BLOCK, :] = line[q : q + 1, :] + line_came[q : q + 1, :]


def merged(keep, came, line, line_came):
    halves = pl.BlockSpec((BATCH * OWN, 128), lambda i: (i, 0))
    lines = pl.BlockSpec((BATCH, 128), lambda i: (i, 0))
    return pl.pallas_call(
        merge,
        out_shape=jax.ShapeDtypeStruct((64 * BLOCK, 128), F32),
        grid=(64 // BATCH,),
        in_specs=[halves, halves, lines, lines],
        out_specs=pl.BlockSpec((BATCH * BLOCK, 128), lambda i: (i, 0)),
        compiler_params=PARAMS,
        name="merge",
    )(keep, came, line, line_came)


def adam(parts, weights, first, second, new, first_new, second_new, factor):
    total = parts[0:BLOCK, :]
    for q in range(1, 64):
        total = total + parts[q * BLOCK : q * BLOCK + BLOCK, :]
    total = total * factor
    grad, line = total[:OWN], total[OWN:]
    m = 0.9 * first[...] + 0.1 * grad
    s = 0.95 * second[...] + 0.05 * grad * grad
    first_new[...] = m
    second_new[...] = s
    fresh = weights[...] - 0.01 * m / (jnp.sqrt(s) + 1e-08)
    fresh = jnp.concatenate([fresh, line], axis=0)
    for q in range(64):
        new[q * BLOCK : q * BLOCK + BLOCK, :] = fresh


def lay_out(place, blocks, *refs):
    out = refs[-1]
    for q in range(BATCH):
        out[q * OWN : q * OWN + OWN, :] = blocks[q * BLOCK : q * BLOCK + OWN, :]


def lay_out_own(place, blocks, out, lines):
    lay_out(place, blocks, out)
    for q in range(BATCH):
        lines[q : q + 1, :] = blocks[q * BLOCK + OWN : q * BLOCK + BLOCK, :]


def own_half(place, blocks):
    steps = 64 // BATCH
    return pl.pallas_call(
        lay_out_own,
        out_shape=[jax.ShapeDtypeStruct((ROWS, 128), F32), jax.ShapeDtypeStruct((64, 128), F32)],
        grid_spec=pltpu.PrefetchScalarGridSpec(
            num_scalar_prefetch=1,
            grid=(steps,),
            in_specs=[pl.BlockSpec((BATCH * BLOCK, 128), lambda i, spot: (i, 0))],
            out_specs=[
                pl.BlockSpec((BATCH * OWN, 128), lambda i, spot: (spot[0] * steps + i, 0)),
                pl.BlockSpec((BATCH, 128), lambda i, spot: (i, 0)),
            ],
        ),
        compiler_params=PARAMS,
        name="lay_out_own",
    )(place, blocks)


def other_half(place, blocks, so_far):
    steps = 64 // BATCH
    return pl.pallas_call(
        lay_out,
        out_shape=jax.ShapeDtypeStruct((ROWS, 128), F32),
        grid_spec=pltpu.PrefetchScalarGridSpec(
            num_scalar_prefetch=1,
            grid=(steps,),
            in_specs=[
                pl.BlockSpec((BATCH * BLOCK, 128), lambda i, spot: (i, 0)),
                pl.BlockSpec(memory_space=pl.ANY),
            ],
            out_specs=pl.BlockSpec((BATCH * OWN, 128), lambda i, spot: ((1 - spot[0]) * steps + i, 0)),
        ),
        input_output_aliases={2: 0},
        compiler_params=PARAMS,
        name="lay_out_other",
    )(place, blocks, so_far)


def per_device(
    block_input, cotangent, weights, first_moment, second_moment, bias_table, bias_index, region_ids
):
    lat_at, lon_at = lax.axis_index("lat"), lax.axis_index("lon")
    factor = 1.0 / math.sqrt(TOK * 128)
    flat = weights.reshape(ROWS, 128)
    *pairs, bias = prepared(flat, bias_table, bias_index)
    edges = edges_of(block_input, cotangent)
    core = lon_at % 2
    place = jnp.stack([core, (lat_at == 7).astype(jnp.int32)]).astype(jnp.int32)
    keep, send, dscore, x, grad, dqkv = run_block(
        (block_input, cotangent), edges, pairs, bias, region_ids, place
    )
    came = lax.ppermute(send, BOTH, core_swap())
    line = table_gradient(dscore, bias_index)
    line_came = lax.ppermute(line, BOTH, core_swap())
    summed = merged(keep, came, line, line_came)
    parts = exchanged(summed.reshape(64, 1, BLOCK * 128), chip_groups())

    _, dqkv, first_moment, second_moment = lax.optimization_barrier(
        (summed, dqkv, first_moment, second_moment)
    )
    o_l, o_e, o_s, o_c = run_input_grad(x, grad, dqkv, pairs[0], pairs[1])
    from_west = around(o_e, "lon", 1)
    from_north = around(o_s, "lat", 1)
    from_corner = diagonal(o_c, 1)
    pairs_of = worker_pairs()
    moments = jnp.stack([first_moment.reshape(OWN, 128), second_moment.reshape(OWN, 128)])
    moments = lax.ppermute(moments, BOTH, pairs_of)
    parts, from_west, from_north, from_corner, moments = lax.optimization_barrier(
        (parts, from_west, from_north, from_corner, moments)
    )

    shard = core * 64 + lat_at * 8 + lon_at // 2
    own = lax.dynamic_slice_in_dim(flat, shard * OWN, OWN, 0)
    new, first_new, second_new = pl.pallas_call(
        functools.partial(adam, factor=factor),
        out_shape=[jax.ShapeDtypeStruct((n, 128), F32) for n in (64 * BLOCK, OWN, OWN)],
        in_specs=[VMEM] * 4,
        out_specs=[VMEM] * 3,
        compiler_params=PARAMS,
        name="adam",
    )(parts.reshape(64 * BLOCK, 128), own, moments[0], moments[1])
    mine = exchanged(new.reshape(64, 1, BLOCK * 128), chip_groups())
    back = [(b, a) for a, b in pairs_of]
    moments = lax.ppermute(jnp.stack([first_new, second_new]), BOTH, back)
    grad_input = with_edges(o_l, from_west, from_north, from_corner)
    mine, moments, grad_input = lax.optimization_barrier((mine, moments, grad_input))

    mine = mine.reshape(64 * BLOCK, 128)
    theirs = lax.ppermute(mine, BOTH, core_swap())
    weights_new, table = own_half(place, mine)
    table_new = table[: HEADS * 5].reshape(5, HEADS, 128).transpose(1, 0, 2)
    table_new = table_new.reshape(HEADS, 640)[:, :BIAS]
    weights_new = other_half(place, theirs, weights_new)
    return (
        grad_input,
        weights_new.reshape(-1),
        moments[0].reshape(-1),
        moments[1].reshape(-1),
        table_new,
    )


def solution(mesh):
    placed = (
        P("lat", "lon", None),
        P("lat", "lon", None),
        P(),
        P(BOTH),
        P(BOTH),
        P(),
        P(),
        P("lat", "lon"),
    )
    return jax.shard_map(
        per_device,
        mesh=mesh,
        in_specs=placed,
        out_specs=(P("lat", "lon", None), P(), P(BOTH), P(BOTH), P()),
        check_vma=False,
    )
```

```python
import functools
import math

import jax
import jax.numpy as jnp
from jax import lax
from jax.experimental import pallas as pl
from jax.experimental.pallas import tpu as pltpu
from jax.sharding import PartitionSpec as P

D = 384
HEADS = 12
FF = 1536
WIN = 12
SHIFT = 6
WT = WIN * WIN
TILE = 24
TOK = TILE * TILE
WINS = TOK // WT
GROUPS = 3
PER = 4
QKV_ROWS = D * 3 * D // 128
PROJ_ROWS = D * D // 128
MLP_ROWS = D * FF // 128
PROJ_AT = QKV_ROWS
UP_AT = QKV_ROWS + PROJ_ROWS
DOWN_AT = UP_AT + MLP_ROWS
ROWS = DOWN_AT + MLP_ROWS
CHUNK = 256
CHUNKS = FF // CHUNK
HALF = ROWS // 2
OWN = ROWS // 128
BLOCK = OWN + 1
BATCH = 32
BIAS = 529
BOTH = ("lat", "lon")
F32 = jnp.float32
BF16 = jnp.bfloat16
VMEM = pl.BlockSpec(memory_space=pltpu.VMEM)
PARAMS = pltpu.CompilerParams(vmem_limit_bytes=58 * 1024 * 1024)

NN = (((1,), (0,)), ((), ()))
NT = (((1,), (1,)), ((), ()))
TN = (((0,), (0,)), ((), ()))


def split(value):
    high = value.astype(BF16)
    return high, (value - high.astype(F32)).astype(BF16)


def dot(a, b, dims):
    return lax.dot_general(a, b, dims, preferred_element_type=F32)


def dot3(a, b, dims):
    return dot(a[0], b[0], dims) + dot(a[0], b[1], dims) + dot(a[1], b[0], dims)


def dot3_deep(a, b, dims):
    (x,), (y,) = dims[0]
    left = jnp.concatenate([a[0], a[0], a[1]], axis=x)
    right = jnp.concatenate([b[0], b[1], b[0]], axis=y)
    return dot(left, right, dims)


def dot3_wide(a, b, dims):
    wide = dot(a[0], jnp.concatenate([b[0], b[1]], axis=1), dims)
    return wide[:, :128] + wide[:, 128:] + dot(a[1], b[0], dims)


def unit(value):
    center = value - jnp.mean(value, axis=-1, keepdims=True)
    scale = lax.rsqrt(jnp.mean(center * center, axis=-1, keepdims=True) + 1e-05)
    return center * scale, scale


def unit_back(grad, normed, scale):
    mean = jnp.mean(grad, axis=-1, keepdims=True)
    along = jnp.mean(grad * normed, axis=-1, keepdims=True)
    return scale * (grad - mean - normed * along)


def lookup(table, index, bias):
    lines = jnp.concatenate([table[...], jnp.zeros((HEADS, 640 - BIAS), F32)], axis=1)

    def rows_of(step, carry):
        at = pl.multiple_of(step * 8, 8)
        columns = index[pl.ds(at, 8), :]
        columns = jnp.concatenate([columns, jnp.zeros((8, 256 - WT), jnp.int32)], axis=1)
        low = columns & 127
        part = columns >> 7
        for h in range(HEADS):
            found = jnp.zeros((8, 256), F32)
            for p in range(5):
                line = jnp.broadcast_to(lines[h : h + 1, 128 * p : 128 * p + 128], (8, 128))
                taken = jnp.concatenate(
                    [
                        jnp.take_along_axis(line, low[:, :128], axis=1),
                        jnp.take_along_axis(line, low[:, 128:], axis=1),
                    ],
                    axis=1,
                )
                found = jnp.where(part == p, taken, found)
            bias[h // PER, pl.ds(pl.multiple_of((h % PER) * WT + at, 8), 8), :] = found[:, :WT]
        return carry

    lax.fori_loop(0, WT // 8, rows_of, 0, unroll=3)


def bias_of_pairs(table, index):
    return pl.pallas_call(
        lookup,
        out_shape=jax.ShapeDtypeStruct((GROUPS, PER * WT, WT), F32),
        in_specs=[VMEM] * 2,
        out_specs=VMEM,
        compiler_params=PARAMS,
        name="lookup",
    )(table, index)


def pair_of(flat, at, rows, blocks, high, low):
    for b in range(blocks):
        h, l = split(flat[pl.ds(at + b, rows, stride=blocks), :])
        high[:, 128 * b : 128 * b + 128] = h
        low[:, 128 * b : 128 * b + 128] = l


INNER = TILE - SHIFT
EDGE = 112
CORNER = 40


def window_rows():
    for wr in range(2):
        for wc in range(2):
            for r in range(WIN):
                yield (wr * 2 + wc) * WT + r * WIN, wc, wr * WIN + r


def gather_windows(target, local, east, south, corner):
    for at, wc, row in window_rows():
        k, n = row + SHIFT, row - INNER
        if wc == 0:
            target[at : at + WIN, :] = (
                local[k, SHIFT : SHIFT + WIN, :] if n < 0 else south[INNER * n : INNER * n + WIN, :]
            )
        else:
            target[at : at + SHIFT, :] = (
                local[k, SHIFT + WIN : TILE, :] if n < 0 else south[INNER * n + WIN : INNER * n + INNER, :]
            )
            target[at + SHIFT : at + WIN, :] = (
                east[SHIFT * row : SHIFT * row + SHIFT, :] if n < 0 else corner[SHIFT * n : SHIFT * n + SHIFT, :]
            )


def scatter_windows(source, local, east, south, corner):
    for at, wc, row in window_rows():
        k, n = row + SHIFT, row - INNER
        near = source[at : at + (WIN if wc == 0 else SHIFT), :]
        if n < 0:
            first = SHIFT if wc == 0 else SHIFT + WIN
            local[k, first : first + near.shape[0], :] = near
        else:
            first = INNER * n + (0 if wc == 0 else WIN)
            south[first : first + near.shape[0], :] = near
        if wc == 1:
            far = source[at + SHIFT : at + WIN, :]
            if n < 0:
                east[SHIFT * row : SHIFT * row + SHIFT, :] = far
            else:
                corner[SHIFT * n : SHIFT * n + SHIFT, :] = far


def head_lane():
    return lax.broadcasted_iota(jnp.int32, (WT, 128), 1) >> 5


def stacked(value):
    lane = head_lane()
    return jnp.concatenate([jnp.where(lane == h, value, 0.0) for h in range(PER)], axis=0)


def unstacked(value):
    lane = head_lane()
    total = jnp.where(lane == 0, value[:WT], 0.0)
    for h in range(1, PER):
        total = jnp.where(lane == h, value[h * WT : h * WT + WT], total)
    return total


def find_labels(region, last, label_row, label_col):
    eye = lax.broadcasted_iota(jnp.int32, (WT, WT), 0) == lax.broadcasted_iota(jnp.int32, (WT, WT), 1)
    for wr in range(2):
        for wc in range(2):
            w = wr * 2 + wc
            pieces = []
            for r in range(WIN):
                row = wr * WIN + r
                ids = region[row : row + 1, wc * WIN : wc * WIN + WIN]
                pieces.append(ids + (4 * last if row >= TILE - SHIFT else 0))
            line = jnp.concatenate(pieces, axis=1).astype(F32)
            label_row[w] = line
            wide = jnp.where(eye, jnp.broadcast_to(line, (WT, WT)), 0.0)
            label_col[w] = jnp.sum(wide, axis=1, keepdims=True)


SCALE = 1.0 / math.sqrt(32.0)


def block_pass(
    x_l, c_l, east, south, corner, region, place, *rest
):
    flat_in, bias = rest[:2]
    rest = rest[2:]
    (
    keep, send, dscore, x_out, grad_out, dqkv_out,
    x, cot, qkv, ctx, prob, n2h, n2l, ch, cl, grad, dqkv, dctx, grads, label_row, label_col, norm2, scale2, sems,
    ) = rest[:-9]
    held = rest[-9:]
    flat, wq_h, wq_l, wp_h, wp_l, wu_h, wu_l, wd_h, wd_l = held
    loads = []
    for i, (at, n) in enumerate(((0, QKV_ROWS), (QKV_ROWS, ROWS - QKV_ROWS))):
        rows = pl.ds(at, n)
        loads.append(pltpu.make_async_copy(flat_in.at[rows], flat.at[rows], sems.at[i]))
        loads[i].start()
    core = place[0]

    def piece(i, half, start, rows):
        source = grads.at[pl.ds(start, rows)]
        spot = pl.ds(start - half * HALF, rows)
        for target, here in ((keep, core == half), (send, core != half)):
            yield here, pltpu.make_async_copy(source, target.at[spot], sems.at[9 + i])

    def start(*what):
        for here, copy in piece(*what):
            pl.when(here)(copy.start)

    def finish(*what):
        for here, copy in piece(*what):
            pl.when(here)(copy.wait)

    pieces = (
        (0, 1, HALF, HALF),
        (1, 0, UP_AT, HALF - UP_AT),
        (2, 0, 0, UP_AT),
    )
    find_labels(region, place[1], label_row, label_col)
    gather_windows(x, x_l, east.at[0], south.at[0], corner.at[0])
    kept = [
        pltpu.make_async_copy(a, b, sems.at[12 + i])
        for i, (a, b) in enumerate(((x, x_out), (grad, grad_out), (dqkv, dqkv_out)))
    ]
    kept[0].start()
    gather_windows(cot, c_l, east.at[1], south.at[1], corner.at[1])
    n1 = split(unit(x[...])[0])
    loads[0].wait()
    pair_of(flat, 0, D, 9, wq_h, wq_l)
    qkv[...] = dot3_deep(n1, (wq_h[...], wq_l[...]), NN)

    def attend(step, carry):
        w, g = step // GROUPS, step % GROUPS
        rows = pl.ds(pl.multiple_of(w * WT, 16), WT)
        lanes = pl.ds(pl.multiple_of(g * 128, 128), 128)
        q = split(stacked(qkv[rows, pl.ds(pl.multiple_of(g * 128, 128), 128)] * SCALE))
        k = split(qkv[rows, pl.ds(pl.multiple_of(D + g * 128, 128), 128)])
        v = split(qkv[rows, pl.ds(pl.multiple_of(2 * D + g * 128, 128), 128)])
        allowed = label_col[w] == label_row[w]
        score = dot3_deep(q, k, NT) + bias[g]
        score = jnp.where(jnp.concatenate([allowed] * PER, axis=0), score, -jnp.inf)
        raised = jnp.exp(score - jnp.max(score, axis=-1, keepdims=True))
        p = raised * (1.0 / jnp.sum(raised, axis=-1, keepdims=True))
        prob[step] = p
        ctx[rows, lanes] = unstacked(dot3_wide(split(p), v, NN))
        return carry

    lax.fori_loop(0, WINS * GROUPS, attend, 0, unroll=12)

    loads[1].wait()
    pair_of(flat, PROJ_AT, D, 3, wp_h, wp_l)
    mixed = x[...] + dot3_deep(split(ctx[...]), (wp_h[...], wp_l[...]), NN)
    norm2[...], scale2[...] = unit(mixed)
    n2h[...], n2l[...] = split(norm2[...])
    ch[...], cl[...] = split(cot[...])
    grad[...] = jnp.zeros_like(grad)

    def feed(f, carry):
        pair_of(flat, DOWN_AT + 3 * CHUNK * f, CHUNK, 3, wd_h.at[f], wd_l.at[f])
        for b in range(2):
            h, l = split(flat[pl.ds(UP_AT + 2 * f + b, D, stride=12), :])
            wu_h[f, :, 128 * b : 128 * b + 128] = h
            wu_l[f, :, 128 * b : 128 * b + 128] = l
        n = (n2h[...], n2l[...])
        c = (ch[...], cl[...])
        up = (wu_h[f], wu_l[f])
        u = dot3_deep(n, up, NN)
        back = dot3_deep(c, (wd_h[f], wd_l[f]), NT)
        inner = 0.7978845608028654 * (u + 0.044715 * u * u * u)
        t = jnp.tanh(inner)
        hidden = split(0.5 * u * (1.0 + t))
        slope = 0.5 * (1.0 + t) + 0.5 * u * (1.0 - t * t) * (
            0.7978845608028654 * (1.0 + 3.0 * 0.044715 * u * u)
        )
        du = split(back * slope)
        gdown = dot3_deep(hidden, c, TN)
        for b in range(3):
            grads[pl.ds(DOWN_AT + 3 * CHUNK * f + b, CHUNK, stride=3), :] = gdown[:, 128 * b : 128 * b + 128]
        gup = dot3_deep(n, du, TN)
        for b in range(2):
            grads[pl.ds(UP_AT + 2 * f + b, D, stride=12), :] = gup[:, 128 * b : 128 * b + 128]
        grad[...] += dot3_deep(du, up, NT)
        return carry

    lax.fori_loop(0, CHUNKS, feed, 0)

    start(*pieces[0])
    start(*pieces[1])
    grad[...] = cot[...] + unit_back(grad[...], norm2[...], scale2[...])
    kept[1].start()
    gm = split(grad[...])
    dctx[...] = dot3_deep(gm, (wp_h[...], wp_l[...]), NT)
    gproj = dot3_deep(split(ctx[...]), gm, TN)
    for b in range(3):
        grads[pl.ds(PROJ_AT + b, D, stride=3), :] = gproj[:, 128 * b : 128 * b + 128]
    dscore[...] = jnp.zeros_like(dscore)

    def attend_back(step, carry):
        w, g = step // GROUPS, step % GROUPS
        rows = pl.ds(pl.multiple_of(w * WT, 16), WT)
        q_at = pl.ds(pl.multiple_of(g * 128, 128), 128)
        k_at = pl.ds(pl.multiple_of(D + g * 128, 128), 128)
        v_at = pl.ds(pl.multiple_of(2 * D + g * 128, 128), 128)
        q = split(stacked(qkv[rows, q_at] * SCALE))
        k = split(qkv[rows, k_at])
        v = split(qkv[rows, v_at])
        d = split(stacked(dctx[rows, q_at]))
        p = prob[step]
        dp = dot3_deep(d, v, NT)
        ds = p * (dp - jnp.sum(dp * p, axis=-1, keepdims=True))
        dscore[g] += ds
        ps, dss = split(p), split(ds)
        dqkv[rows, v_at] = dot3_wide(ps, d, TN)
        dqkv[rows, q_at] = unstacked(dot3_wide(dss, k, NN)) * SCALE
        dqkv[rows, k_at] = dot3_wide(dss, q, TN)
        return carry

    lax.fori_loop(0, WINS * GROUPS, attend_back, 0, unroll=4)

    kept[2].start()
    dq = split(dqkv[...])
    gqkv = dot3_deep(split(unit(x[...])[0]), dq, TN)
    for b in range(9):
        grads[pl.ds(b, D, stride=9), :] = gqkv[:, 128 * b : 128 * b + 128]
    start(*pieces[2])
    for copy in kept:
        copy.wait()
    for what in pieces:
        finish(*what)


def input_grad(x, grad, dqkv, flat, o_l, o_e, o_s, o_c, total, wq_h, wq_l):
    pair_of(flat, 0, D, 9, wq_h, wq_l)
    n1, scale1 = unit(x[...])
    back = dot3_deep(split(dqkv[...]), (wq_h[...], wq_l[...]), NT)
    total[...] = grad[...] + unit_back(back, n1, scale1)
    scatter_windows(total, o_l, o_e, o_s, o_c)


def run_input_grad(x, grad, dqkv, flat):
    halo = [(TILE, TILE, D), (EDGE, D), (EDGE, D), (CORNER, D)]

    def first(*shape):
        return pl.BlockSpec(shape, lambda i: (0,) * len(shape))

    return pl.pallas_call(
        input_grad,
        out_shape=[jax.ShapeDtypeStruct(s, F32) for s in halo],
        grid=(1,),
        in_specs=[first(TOK, D), first(TOK, D), first(TOK, 3 * D), first(QKV_ROWS, 128)],
        out_specs=[first(*s) for s in halo],
        scratch_shapes=[
            pltpu.VMEM((TOK, D), F32),
            pltpu.VMEM((D, 3 * D), BF16),
            pltpu.VMEM((D, 3 * D), BF16),
        ],
        compiler_params=PARAMS,
        name="input_grad",
    )(x, grad, dqkv, flat)


def run_block(tiles, edges, flat, bias, region, place):
    outs = [(HALF, 128), (HALF, 128), (GROUPS, PER * WT, WT), (TOK, D), (TOK, D), (TOK, 3 * D)]
    whole = pl.BlockSpec(memory_space=pl.ANY)
    scratch = [
        pltpu.VMEM((TOK, D), F32),
        pltpu.VMEM((TOK, D), F32),
        pltpu.VMEM((TOK, 3 * D), F32),
        pltpu.VMEM((TOK, D), F32),
        pltpu.VMEM((WINS * GROUPS, PER * WT, WT), F32),
        pltpu.VMEM((TOK, D), BF16),
        pltpu.VMEM((TOK, D), BF16),
        pltpu.VMEM((TOK, D), BF16),
        pltpu.VMEM((TOK, D), BF16),
        pltpu.VMEM((TOK, D), F32),
        pltpu.VMEM((TOK, 3 * D), F32),
        pltpu.VMEM((TOK, D), F32),
        pltpu.VMEM((ROWS, 128), F32),
        pltpu.VMEM((WINS, 1, WT), F32),
        pltpu.VMEM((WINS, WT, 1), F32),
        pltpu.VMEM((TOK, D), F32),
        pltpu.VMEM((TOK, 1), F32),
        pltpu.SemaphoreType.DMA((15,)),
        pltpu.VMEM((ROWS, 128), F32),
        *[pltpu.VMEM((D, 3 * D), BF16)] * 2,
        *[pltpu.VMEM((D, D), BF16)] * 2,
        *[pltpu.VMEM((CHUNKS, D, CHUNK), BF16)] * 2,
        *[pltpu.VMEM((CHUNKS, CHUNK, D), BF16)] * 2,
    ]
    args = (*tiles, *edges, region, place, flat, bias)
    return pl.pallas_call(
        block_pass,
        out_shape=[jax.ShapeDtypeStruct(s, F32) for s in outs],
        in_specs=[VMEM] * 6 + [pl.BlockSpec(memory_space=pltpu.SMEM)] + [whole, VMEM],
        out_specs=[whole] * 2 + [VMEM] + [whole] * 3,
        scratch_shapes=scratch,
        compiler_params=PARAMS,
        name="block_pass",
    )(*args)


def table_sum(by_head, index, out, sums, scores):
    sums[...] = jnp.zeros_like(sums)
    for h in range(16):
        if h < HEADS:
            scores[:, h, :] = by_head[h // PER, (h % PER) * WT : (h % PER) * WT + WT, :]
        else:
            scores[:, h, :] = jnp.zeros((WT, WT), F32)
    column = lax.broadcasted_iota(jnp.int32, (128, WT), 0)

    def one(i):
        line = index[pl.ds(i, 1), :]
        part = jnp.broadcast_to(line >> 7, (16, WT))
        hot = (column == jnp.broadcast_to(line & 127, (128, WT))).astype(F32).astype(BF16)
        high, low = split(scores[i])
        pieces = []
        for p in range(5):
            here = part == p
            pieces.append(jnp.where(here, high, jnp.zeros_like(high)))
            pieces.append(jnp.where(here, low, jnp.zeros_like(low)))
        return dot(jnp.concatenate(pieces, axis=0), hot, NT)

    def step(k, carry):
        at = 8 * k
        quads = [(one(at + i) + one(at + i + 1)) + (one(at + i + 2) + one(at + i + 3)) for i in (0, 4)]
        sums[...] += quads[0] + quads[1]
        return carry

    lax.fori_loop(0, WT // 8, step, 0)
    out[...] = jnp.zeros_like(out)
    for p in range(5):
        both = sums[32 * p : 32 * p + 16, :] + sums[32 * p + 16 : 32 * p + 32, :]
        out[HEADS * p : HEADS * p + HEADS, :] = both[:HEADS]


def table_gradient(dscore, index):
    return pl.pallas_call(
        table_sum,
        out_shape=jax.ShapeDtypeStruct((64, 128), F32),
        in_specs=[VMEM] * 2,
        out_specs=VMEM,
        scratch_shapes=[pltpu.VMEM((160, 128), F32), pltpu.VMEM((WT, 16, WT), F32)],
        compiler_params=PARAMS,
        name="table_sum",
    )(dscore, index)


def chip_order():
    return [(y_lo * 4 + x) * 16 + zy * 2 for y_lo in range(2) for x in range(4) for zy in range(8)]


def chip_groups():
    return [[d + core for d in chip_order()] for core in range(2)]


def core_swap():
    return [(d, d ^ 1) for d in range(128)]


def worker_pairs():
    return [(core * 64 + q, d + core) for core in range(2) for q, d in enumerate(chip_order())]


def exchanged(value, groups):
    return lax.all_to_all(value, BOTH, 0, 0, axis_index_groups=groups, tiled=True)


def around(value, axis, by):
    size = lax.axis_size(axis)
    return lax.ppermute(value, axis, [(i, (i + by) % size) for i in range(size)])


def diagonal(value, by):
    lat, lon = lax.axis_size("lat"), lax.axis_size("lon")
    return lax.ppermute(
        value,
        BOTH,
        [
            (a * lon + o, ((a + by) % lat) * lon + (o + by) % lon)
            for a in range(lat)
            for o in range(lon)
        ],
    )


def pack(x, c, east, south, corner):
    for i, tile in enumerate((x, c)):
        for k in range(SHIFT, TILE):
            east[i, SHIFT * (k - SHIFT) : SHIFT * (k - SHIFT) + SHIFT, :] = tile[k, 0:SHIFT, :]
        for n in range(SHIFT):
            south[i, INNER * n : INNER * n + INNER, :] = tile[n, SHIFT:TILE, :]
            corner[i, SHIFT * n : SHIFT * n + SHIFT, :] = tile[n, 0:SHIFT, :]


def edges_of(x, c):
    shapes = [(2, EDGE, D), (2, EDGE, D), (2, CORNER, D)]
    east, south, corner = pl.pallas_call(
        pack,
        out_shape=[jax.ShapeDtypeStruct(s, F32) for s in shapes],
        in_specs=[VMEM] * 2,
        out_specs=[VMEM] * 3,
        compiler_params=PARAMS,
        name="pack",
    )(x, c)
    return around(east, "lon", -1), around(south, "lat", -1), diagonal(corner, -1)


def unpack_edges(local, west, north, corner, out):
    out[SHIFT:TILE, SHIFT:TILE, :] = local[SHIFT:TILE, SHIFT:TILE, :]
    for k in range(SHIFT, TILE):
        out[k, 0:SHIFT, :] = west[SHIFT * (k - SHIFT) : SHIFT * (k - SHIFT) + SHIFT, :]
    for n in range(SHIFT):
        out[n, SHIFT:TILE, :] = north[INNER * n : INNER * n + INNER, :]
        out[n, 0:SHIFT, :] = corner[SHIFT * n : SHIFT * n + SHIFT, :]


def with_edges(local, west, north, corner):
    return pl.pallas_call(
        unpack_edges,
        out_shape=jax.ShapeDtypeStruct((TILE, TILE, D), F32),
        in_specs=[VMEM] * 4,
        out_specs=VMEM,
        compiler_params=PARAMS,
        name="unpack_edges",
    )(local, west, north, corner)


def merge(keep, came, line, line_came, out):
    for q in range(BATCH):
        rows = slice(q * OWN, q * OWN + OWN)
        out[q * BLOCK : q * BLOCK + OWN, :] = keep[rows, :] + came[rows, :]
        out[q * BLOCK + OWN : (q + 1) * BLOCK, :] = line[q : q + 1, :] + line_came[q : q + 1, :]


def merged(keep, came, line, line_came):
    halves = pl.BlockSpec((BATCH * OWN, 128), lambda i: (i, 0))
    lines = pl.BlockSpec((BATCH, 128), lambda i: (i, 0))
    return pl.pallas_call(
        merge,
        out_shape=jax.ShapeDtypeStruct((64 * BLOCK, 128), F32),
        grid=(64 // BATCH,),
        in_specs=[halves, halves, lines, lines],
        out_specs=pl.BlockSpec((BATCH * BLOCK, 128), lambda i: (i, 0)),
        compiler_params=PARAMS,
        name="merge",
    )(keep, came, line, line_came)


def adam(parts, weights, first, second, new, first_new, second_new, factor):
    total = parts[0:BLOCK, :]
    for q in range(1, 64):
        total = total + parts[q * BLOCK : q * BLOCK + BLOCK, :]
    total = total * factor
    grad, line = total[:OWN], total[OWN:]
    m = 0.9 * first[...] + 0.1 * grad
    s = 0.95 * second[...] + 0.05 * grad * grad
    first_new[...] = m
    second_new[...] = s
    fresh = weights[...] - 0.01 * m / (jnp.sqrt(s) + 1e-08)
    fresh = jnp.concatenate([fresh, line], axis=0)
    for q in range(64):
        new[q * BLOCK : q * BLOCK + BLOCK, :] = fresh


def lay_out(place, blocks, *refs):
    out = refs[-1]
    for q in range(BATCH):
        out[q * OWN : q * OWN + OWN, :] = blocks[q * BLOCK : q * BLOCK + OWN, :]


def lay_out_own(place, blocks, out, lines):
    lay_out(place, blocks, out)
    for q in range(BATCH):
        lines[q : q + 1, :] = blocks[q * BLOCK + OWN : q * BLOCK + BLOCK, :]


def own_half(place, blocks):
    steps = 64 // BATCH
    return pl.pallas_call(
        lay_out_own,
        out_shape=[jax.ShapeDtypeStruct((ROWS, 128), F32), jax.ShapeDtypeStruct((64, 128), F32)],
        grid_spec=pltpu.PrefetchScalarGridSpec(
            num_scalar_prefetch=1,
            grid=(steps,),
            in_specs=[pl.BlockSpec((BATCH * BLOCK, 128), lambda i, spot: (i, 0))],
            out_specs=[
                pl.BlockSpec((BATCH * OWN, 128), lambda i, spot: (spot[0] * steps + i, 0)),
                pl.BlockSpec((BATCH, 128), lambda i, spot: (i, 0)),
            ],
        ),
        compiler_params=PARAMS,
        name="lay_out_own",
    )(place, blocks)


def other_half(place, blocks, so_far):
    steps = 64 // BATCH
    return pl.pallas_call(
        lay_out,
        out_shape=jax.ShapeDtypeStruct((ROWS, 128), F32),
        grid_spec=pltpu.PrefetchScalarGridSpec(
            num_scalar_prefetch=1,
            grid=(steps,),
            in_specs=[
                pl.BlockSpec((BATCH * BLOCK, 128), lambda i, spot: (i, 0)),
                pl.BlockSpec(memory_space=pl.ANY),
            ],
            out_specs=pl.BlockSpec((BATCH * OWN, 128), lambda i, spot: ((1 - spot[0]) * steps + i, 0)),
        ),
        input_output_aliases={2: 0},
        compiler_params=PARAMS,
        name="lay_out_other",
    )(place, blocks, so_far)


def per_device(
    block_input, cotangent, weights, first_moment, second_moment, bias_table, bias_index, region_ids
):
    lat_at, lon_at = lax.axis_index("lat"), lax.axis_index("lon")
    factor = 1.0 / math.sqrt(TOK * 128)
    flat = weights.reshape(ROWS, 128)
    bias = bias_of_pairs(bias_table, bias_index)
    edges = edges_of(block_input, cotangent)
    core = lon_at % 2
    place = jnp.stack([core, (lat_at == 7).astype(jnp.int32)]).astype(jnp.int32)
    keep, send, dscore, x, grad, dqkv = run_block(
        (block_input, cotangent), edges, flat, bias, region_ids, place
    )
    came = lax.ppermute(send, BOTH, core_swap())
    line = table_gradient(dscore, bias_index)
    line_came = lax.ppermute(line, BOTH, core_swap())
    summed = merged(keep, came, line, line_came)
    parts = exchanged(summed.reshape(64, 1, BLOCK * 128), chip_groups())

    _, dqkv, first_moment, second_moment = lax.optimization_barrier(
        (summed, dqkv, first_moment, second_moment)
    )
    o_l, o_e, o_s, o_c = run_input_grad(x, grad, dqkv, flat)
    from_west = around(o_e, "lon", 1)
    from_north = around(o_s, "lat", 1)
    from_corner = diagonal(o_c, 1)
    pairs_of = worker_pairs()
    moments = jnp.stack([first_moment.reshape(OWN, 128), second_moment.reshape(OWN, 128)])
    moments = lax.ppermute(moments, BOTH, pairs_of)
    parts, from_west, from_north, from_corner, moments = lax.optimization_barrier(
        (parts, from_west, from_north, from_corner, moments)
    )

    shard = core * 64 + lat_at * 8 + lon_at // 2
    own = lax.dynamic_slice_in_dim(flat, shard * OWN, OWN, 0)
    new, first_new, second_new = pl.pallas_call(
        functools.partial(adam, factor=factor),
        out_shape=[jax.ShapeDtypeStruct((n, 128), F32) for n in (64 * BLOCK, OWN, OWN)],
        in_specs=[VMEM] * 4,
        out_specs=[VMEM] * 3,
        compiler_params=PARAMS,
        name="adam",
    )(parts.reshape(64 * BLOCK, 128), own, moments[0], moments[1])
    mine = exchanged(new.reshape(64, 1, BLOCK * 128), chip_groups())
    back = [(b, a) for a, b in pairs_of]
    moments = lax.ppermute(jnp.stack([first_new, second_new]), BOTH, back)
    grad_input = with_edges(o_l, from_west, from_north, from_corner)
    mine, moments, grad_input = lax.optimization_barrier((mine, moments, grad_input))

    mine = mine.reshape(64 * BLOCK, 128)
    theirs = lax.ppermute(mine, BOTH, core_swap())
    weights_new, table = own_half(place, mine)
    table_new = table[: HEADS * 5].reshape(5, HEADS, 128).transpose(1, 0, 2)
    table_new = table_new.reshape(HEADS, 640)[:, :BIAS]
    weights_new = other_half(place, theirs, weights_new)
    return (
        grad_input,
        weights_new.reshape(-1),
        moments[0].reshape(-1),
        moments[1].reshape(-1),
        table_new,
    )


def solution(mesh):
    placed = (
        P("lat", "lon", None),
        P("lat", "lon", None),
        P(),
        P(BOTH),
        P(BOTH),
        P(),
        P(),
        P("lat", "lon"),
    )
    return jax.shard_map(
        per_device,
        mesh=mesh,
        in_specs=placed,
        out_specs=(P("lat", "lon", None), P(), P(BOTH), P(BOTH), P()),
        check_vma=False,
    )
```

```python
import functools
import math

import jax
import jax.numpy as jnp
from jax import lax
from jax.experimental import pallas as pl
from jax.experimental.pallas import tpu as pltpu
from jax.sharding import PartitionSpec as P

D = 384
HEADS = 12
FF = 1536
WIN = 12
SHIFT = 6
WT = WIN * WIN
TILE = 24
TOK = TILE * TILE
WINS = TOK // WT
GROUPS = 3
PER = 4
QKV_ROWS = D * 3 * D // 128
PROJ_ROWS = D * D // 128
MLP_ROWS = D * FF // 128
PROJ_AT = QKV_ROWS
UP_AT = QKV_ROWS + PROJ_ROWS
DOWN_AT = UP_AT + MLP_ROWS
ROWS = DOWN_AT + MLP_ROWS
CHUNK = 256
CHUNKS = FF // CHUNK
HALF = ROWS // 2
OWN = ROWS // 128
BLOCK = OWN + 1
BATCH = 32
BIAS = 529
BOTH = ("lat", "lon")
F32 = jnp.float32
BF16 = jnp.bfloat16
VMEM = pl.BlockSpec(memory_space=pltpu.VMEM)
PARAMS = pltpu.CompilerParams(vmem_limit_bytes=58 * 1024 * 1024)

NN = (((1,), (0,)), ((), ()))
NT = (((1,), (1,)), ((), ()))
TN = (((0,), (0,)), ((), ()))


def split(value):
    high = value.astype(BF16)
    return high, (value - high.astype(F32)).astype(BF16)


def dot(a, b, dims):
    return lax.dot_general(a, b, dims, preferred_element_type=F32)


def dot3(a, b, dims):
    return dot(a[0], b[0], dims) + dot(a[0], b[1], dims) + dot(a[1], b[0], dims)


def dot3_deep(a, b, dims):
    (x,), (y,) = dims[0]
    left = jnp.concatenate([a[0], a[0], a[1]], axis=x)
    right = jnp.concatenate([b[0], b[1], b[0]], axis=y)
    return dot(left, right, dims)


def dot3_wide(a, b, dims):
    wide = dot(a[0], jnp.concatenate([b[0], b[1]], axis=1), dims)
    return wide[:, :128] + wide[:, 128:] + dot(a[1], b[0], dims)


def unit(value):
    center = value - jnp.mean(value, axis=-1, keepdims=True)
    scale = lax.rsqrt(jnp.mean(center * center, axis=-1, keepdims=True) + 1e-05)
    return center * scale, scale


def unit_back(grad, normed, scale):
    mean = jnp.mean(grad, axis=-1, keepdims=True)
    along = jnp.mean(grad * normed, axis=-1, keepdims=True)
    return scale * (grad - mean - normed * along)


def lookup(table, index, bias):
    lines = jnp.concatenate([table[...], jnp.zeros((HEADS, 640 - BIAS), F32)], axis=1)

    def rows_of(step, carry):
        at = pl.multiple_of(step * 8, 8)
        columns = index[pl.ds(at, 8), :]
        columns = jnp.concatenate([columns, jnp.zeros((8, 256 - WT), jnp.int32)], axis=1)
        low = columns & 127
        part = columns >> 7
        for h in range(HEADS):
            found = jnp.zeros((8, 256), F32)
            for p in range(5):
                line = jnp.broadcast_to(lines[h : h + 1, 128 * p : 128 * p + 128], (8, 128))
                taken = jnp.concatenate(
                    [
                        jnp.take_along_axis(line, low[:, :128], axis=1),
                        jnp.take_along_axis(line, low[:, 128:], axis=1),
                    ],
                    axis=1,
                )
                found = jnp.where(part == p, taken, found)
            bias[h // PER, pl.ds(pl.multiple_of((h % PER) * WT + at, 8), 8), :] = found[:, :WT]
        return carry

    lax.fori_loop(0, WT // 8, rows_of, 0, unroll=3)


def bias_of_pairs(table, index):
    return pl.pallas_call(
        lookup,
        out_shape=jax.ShapeDtypeStruct((GROUPS, PER * WT, WT), F32),
        in_specs=[VMEM] * 2,
        out_specs=VMEM,
        compiler_params=PARAMS,
        name="lookup",
    )(table, index)


def pair_of(flat, at, rows, blocks, high, low):
    for b in range(blocks):
        h, l = split(flat[pl.ds(at + b, rows, stride=blocks), :])
        high[:, 128 * b : 128 * b + 128] = h
        low[:, 128 * b : 128 * b + 128] = l


INNER = TILE - SHIFT
EDGE = 112
CORNER = 40


def window_rows():
    for wr in range(2):
        for wc in range(2):
            for r in range(WIN):
                yield (wr * 2 + wc) * WT + r * WIN, wc, wr * WIN + r


def gather_windows(target, local, east, south, corner):
    for at, wc, row in window_rows():
        k, n = row + SHIFT, row - INNER
        if wc == 0:
            target[at : at + WIN, :] = (
                local[k, SHIFT : SHIFT + WIN, :] if n < 0 else south[INNER * n : INNER * n + WIN, :]
            )
        else:
            target[at : at + SHIFT, :] = (
                local[k, SHIFT + WIN : TILE, :] if n < 0 else south[INNER * n + WIN : INNER * n + INNER, :]
            )
            target[at + SHIFT : at + WIN, :] = (
                east[SHIFT * row : SHIFT * row + SHIFT, :] if n < 0 else corner[SHIFT * n : SHIFT * n + SHIFT, :]
            )


def scatter_windows(source, local, east, south, corner):
    for at, wc, row in window_rows():
        k, n = row + SHIFT, row - INNER
        near = source[at : at + (WIN if wc == 0 else SHIFT), :]
        if n < 0:
            first = SHIFT if wc == 0 else SHIFT + WIN
            local[k, first : first + near.shape[0], :] = near
        else:
            first = INNER * n + (0 if wc == 0 else WIN)
            south[first : first + near.shape[0], :] = near
        if wc == 1:
            far = source[at + SHIFT : at + WIN, :]
            if n < 0:
                east[SHIFT * row : SHIFT * row + SHIFT, :] = far
            else:
                corner[SHIFT * n : SHIFT * n + SHIFT, :] = far


def head_lane():
    return lax.broadcasted_iota(jnp.int32, (WT, 128), 1) >> 5


def stacked(value):
    lane = head_lane()
    return jnp.concatenate([jnp.where(lane == h, value, 0.0) for h in range(PER)], axis=0)


def unstacked(value):
    lane = head_lane()
    total = jnp.where(lane == 0, value[:WT], 0.0)
    for h in range(1, PER):
        total = jnp.where(lane == h, value[h * WT : h * WT + WT], total)
    return total


def find_labels(region, last, label_row, label_col):
    eye = lax.broadcasted_iota(jnp.int32, (WT, WT), 0) == lax.broadcasted_iota(jnp.int32, (WT, WT), 1)
    for wr in range(2):
        for wc in range(2):
            w = wr * 2 + wc
            pieces = []
            for r in range(WIN):
                row = wr * WIN + r
                ids = region[row : row + 1, wc * WIN : wc * WIN + WIN]
                pieces.append(ids + (4 * last if row >= TILE - SHIFT else 0))
            line = jnp.concatenate(pieces, axis=1).astype(F32)
            label_row[w] = line
            wide = jnp.where(eye, jnp.broadcast_to(line, (WT, WT)), 0.0)
            label_col[w] = jnp.sum(wide, axis=1, keepdims=True)


SCALE = 1.0 / math.sqrt(32.0)


def block_pass(
    x_l, c_l, east, south, corner, region, place, *rest
):
    flat_in, bias = rest[:2]
    rest = rest[2:]
    (
    keep, send, dscore, x_out, grad_out, dqkv_out,
    x, cot, qkv, ctx, prob, n2h, n2l, ch, cl, grad, dqkv, dctx, grads, label_row, label_col, norm2, scale2, sems,
    ) = rest[:-9]
    held = rest[-9:]
    flat, wq_h, wq_l, wp_h, wp_l, wu_h, wu_l, wd_h, wd_l = held
    loads = []
    for i, (at, n) in enumerate(((0, QKV_ROWS), (QKV_ROWS, ROWS - QKV_ROWS))):
        rows = pl.ds(at, n)
        loads.append(pltpu.make_async_copy(flat_in.at[rows], flat.at[rows], sems.at[i]))
        loads[i].start()
    core = place[0]

    def piece(i, half, start, rows):
        source = grads.at[pl.ds(start, rows)]
        spot = pl.ds(start - half * HALF, rows)
        for target, here in ((keep, core == half), (send, core != half)):
            yield here, pltpu.make_async_copy(source, target.at[spot], sems.at[9 + i])

    def start(*what):
        for here, copy in piece(*what):
            pl.when(here)(copy.start)

    def finish(*what):
        for here, copy in piece(*what):
            pl.when(here)(copy.wait)

    pieces = (
        (0, 1, HALF, HALF),
        (1, 0, UP_AT, HALF - UP_AT),
        (2, 0, 0, UP_AT),
    )
    find_labels(region, place[1], label_row, label_col)
    gather_windows(x, x_l, east.at[0], south.at[0], corner.at[0])
    kept = [
        pltpu.make_async_copy(a, b, sems.at[12 + i])
        for i, (a, b) in enumerate(((x, x_out), (grad, grad_out), (dqkv, dqkv_out)))
    ]
    kept[0].start()
    gather_windows(cot, c_l, east.at[1], south.at[1], corner.at[1])
    n1 = split(unit(x[...])[0])
    loads[0].wait()
    pair_of(flat, 0, D, 9, wq_h, wq_l)
    qkv[...] = dot3_deep(n1, (wq_h[...], wq_l[...]), NN)

    def attend(step, carry):
        w, g = step // GROUPS, step % GROUPS
        rows = pl.ds(pl.multiple_of(w * WT, 16), WT)
        lanes = pl.ds(pl.multiple_of(g * 128, 128), 128)
        q = split(stacked(qkv[rows, pl.ds(pl.multiple_of(g * 128, 128), 128)] * SCALE))
        k = split(qkv[rows, pl.ds(pl.multiple_of(D + g * 128, 128), 128)])
        v = split(qkv[rows, pl.ds(pl.multiple_of(2 * D + g * 128, 128), 128)])
        allowed = label_col[w] == label_row[w]
        score = dot3_deep(q, k, NT) + bias[g]
        score = jnp.where(jnp.concatenate([allowed] * PER, axis=0), score, -jnp.inf)
        raised = jnp.exp(score - jnp.max(score, axis=-1, keepdims=True))
        p = raised * (1.0 / jnp.sum(raised, axis=-1, keepdims=True))
        prob[step] = p
        ctx[rows, lanes] = unstacked(dot3_wide(split(p), v, NN))
        return carry

    lax.fori_loop(0, WINS * GROUPS, attend, 0, unroll=12)

    loads[1].wait()
    pair_of(flat, PROJ_AT, D, 3, wp_h, wp_l)
    mixed = x[...] + dot3_deep(split(ctx[...]), (wp_h[...], wp_l[...]), NN)
    norm2[...], scale2[...] = unit(mixed)
    n2h[...], n2l[...] = split(norm2[...])
    ch[...], cl[...] = split(cot[...])
    grad[...] = jnp.zeros_like(grad)

    def feed(f, carry):
        pair_of(flat, DOWN_AT + 3 * CHUNK * f, CHUNK, 3, wd_h.at[f], wd_l.at[f])
        for b in range(2):
            h, l = split(flat[pl.ds(UP_AT + 2 * f + b, D, stride=12), :])
            wu_h[f, :, 128 * b : 128 * b + 128] = h
            wu_l[f, :, 128 * b : 128 * b + 128] = l
        n = (n2h[...], n2l[...])
        c = (ch[...], cl[...])
        up = (wu_h[f], wu_l[f])
        u = dot3_deep(n, up, NN)
        back = dot3_deep(c, (wd_h[f], wd_l[f]), NT)
        inner = 0.7978845608028654 * (u + 0.044715 * u * u * u)
        t = jnp.tanh(inner)
        hidden = split(0.5 * u * (1.0 + t))
        slope = 0.5 * (1.0 + t) + 0.5 * u * (1.0 - t * t) * (
            0.7978845608028654 * (1.0 + 3.0 * 0.044715 * u * u)
        )
        du = split(back * slope)
        gdown = dot3_deep(hidden, c, TN)
        for b in range(3):
            grads[pl.ds(DOWN_AT + 3 * CHUNK * f + b, CHUNK, stride=3), :] = gdown[:, 128 * b : 128 * b + 128]
        gup = dot3_deep(n, du, TN)
        for b in range(2):
            grads[pl.ds(UP_AT + 2 * f + b, D, stride=12), :] = gup[:, 128 * b : 128 * b + 128]
        grad[...] += dot3_deep(du, up, NT)
        return carry

    lax.fori_loop(0, CHUNKS, feed, 0)

    start(*pieces[0])
    start(*pieces[1])
    grad[...] = cot[...] + unit_back(grad[...], norm2[...], scale2[...])
    kept[1].start()
    gm = split(grad[...])
    dctx[...] = dot3_deep(gm, (wp_h[...], wp_l[...]), NT)
    gproj = dot3_deep(split(ctx[...]), gm, TN)
    for b in range(3):
        grads[pl.ds(PROJ_AT + b, D, stride=3), :] = gproj[:, 128 * b : 128 * b + 128]
    dscore[...] = jnp.zeros_like(dscore)

    def attend_back(step, carry):
        w, g = step // GROUPS, step % GROUPS
        rows = pl.ds(pl.multiple_of(w * WT, 16), WT)
        q_at = pl.ds(pl.multiple_of(g * 128, 128), 128)
        k_at = pl.ds(pl.multiple_of(D + g * 128, 128), 128)
        v_at = pl.ds(pl.multiple_of(2 * D + g * 128, 128), 128)
        q = split(stacked(qkv[rows, q_at] * SCALE))
        k = split(qkv[rows, k_at])
        v = split(qkv[rows, v_at])
        d = split(stacked(dctx[rows, q_at]))
        p = prob[step]
        dp = dot3_deep(d, v, NT)
        ds = p * (dp - jnp.sum(dp * p, axis=-1, keepdims=True))
        dscore[g] += ds
        ps, dss = split(p), split(ds)
        dqkv[rows, v_at] = dot3_wide(ps, d, TN)
        dqkv[rows, q_at] = unstacked(dot3_wide(dss, k, NN)) * SCALE
        dqkv[rows, k_at] = dot3_wide(dss, q, TN)
        return carry

    lax.fori_loop(0, WINS * GROUPS, attend_back, 0, unroll=4)

    kept[2].start()
    dq = split(dqkv[...])
    gqkv = dot3_deep(split(unit(x[...])[0]), dq, TN)
    for b in range(9):
        grads[pl.ds(b, D, stride=9), :] = gqkv[:, 128 * b : 128 * b + 128]
    start(*pieces[2])
    for copy in kept:
        copy.wait()
    for what in pieces:
        finish(*what)


def input_grad(x, grad, dqkv, flat, o_l, o_e, o_s, o_c, total, wq_h, wq_l):
    pair_of(flat, 0, D, 9, wq_h, wq_l)
    n1, scale1 = unit(x[...])
    back = dot3_deep(split(dqkv[...]), (wq_h[...], wq_l[...]), NT)
    total[...] = grad[...] + unit_back(back, n1, scale1)
    scatter_windows(total, o_l, o_e, o_s, o_c)


def run_input_grad(x, grad, dqkv, flat):
    halo = [(TILE, TILE, D), (EDGE, D), (EDGE, D), (CORNER, D)]

    def first(*shape):
        return pl.BlockSpec(shape, lambda i: (0,) * len(shape))

    return pl.pallas_call(
        input_grad,
        out_shape=[jax.ShapeDtypeStruct(s, F32) for s in halo],
        grid=(1,),
        in_specs=[first(TOK, D), first(TOK, D), first(TOK, 3 * D), first(QKV_ROWS, 128)],
        out_specs=[first(*s) for s in halo],
        scratch_shapes=[
            pltpu.VMEM((TOK, D), F32),
            pltpu.VMEM((D, 3 * D), BF16),
            pltpu.VMEM((D, 3 * D), BF16),
        ],
        compiler_params=PARAMS,
        name="input_grad",
    )(x, grad, dqkv, flat)


def run_block(tiles, edges, flat, bias, region, place):
    outs = [(HALF, 128), (HALF, 128), (GROUPS, PER * WT, WT), (TOK, D), (TOK, D), (TOK, 3 * D)]
    whole = pl.BlockSpec(memory_space=pl.ANY)
    scratch = [
        pltpu.VMEM((TOK, D), F32),
        pltpu.VMEM((TOK, D), F32),
        pltpu.VMEM((TOK, 3 * D), F32),
        pltpu.VMEM((TOK, D), F32),
        pltpu.VMEM((WINS * GROUPS, PER * WT, WT), F32),
        pltpu.VMEM((TOK, D), BF16),
        pltpu.VMEM((TOK, D), BF16),
        pltpu.VMEM((TOK, D), BF16),
        pltpu.VMEM((TOK, D), BF16),
        pltpu.VMEM((TOK, D), F32),
        pltpu.VMEM((TOK, 3 * D), F32),
        pltpu.VMEM((TOK, D), F32),
        pltpu.VMEM((ROWS, 128), F32),
        pltpu.VMEM((WINS, 1, WT), F32),
        pltpu.VMEM((WINS, WT, 1), F32),
        pltpu.VMEM((TOK, D), F32),
        pltpu.VMEM((TOK, 1), F32),
        pltpu.SemaphoreType.DMA((15,)),
        pltpu.VMEM((ROWS, 128), F32),
        *[pltpu.VMEM((D, 3 * D), BF16)] * 2,
        *[pltpu.VMEM((D, D), BF16)] * 2,
        *[pltpu.VMEM((CHUNKS, D, CHUNK), BF16)] * 2,
        *[pltpu.VMEM((CHUNKS, CHUNK, D), BF16)] * 2,
    ]
    args = (*tiles, *edges, region, place, flat, bias)
    return pl.pallas_call(
        block_pass,
        out_shape=[jax.ShapeDtypeStruct(s, F32) for s in outs],
        in_specs=[VMEM] * 6 + [pl.BlockSpec(memory_space=pltpu.SMEM)] + [whole, VMEM],
        out_specs=[whole] * 2 + [VMEM] + [whole] * 3,
        scratch_shapes=scratch,
        compiler_params=PARAMS,
        name="block_pass",
    )(*args)


def table_sum(by_head, index, out, sums, scores):
    sums[...] = jnp.zeros_like(sums)
    for h in range(16):
        if h < HEADS:
            scores[:, h, :] = by_head[h // PER, (h % PER) * WT : (h % PER) * WT + WT, :]
        else:
            scores[:, h, :] = jnp.zeros((WT, WT), F32)
    column = lax.broadcasted_iota(jnp.int32, (128, WT), 0)

    def one(i):
        line = index[pl.ds(i, 1), :]
        part = jnp.broadcast_to(line >> 7, (16, WT))
        hot = (column == jnp.broadcast_to(line & 127, (128, WT))).astype(F32).astype(BF16)
        high, low = split(scores[i])
        pieces = []
        for p in range(5):
            here = part == p
            pieces.append(jnp.where(here, high, jnp.zeros_like(high)))
            pieces.append(jnp.where(here, low, jnp.zeros_like(low)))
        return dot(jnp.concatenate(pieces, axis=0), hot, NT)

    def step(k, carry):
        at = 8 * k
        quads = [(one(at + i) + one(at + i + 1)) + (one(at + i + 2) + one(at + i + 3)) for i in (0, 4)]
        sums[...] += quads[0] + quads[1]
        return carry

    lax.fori_loop(0, WT // 8, step, 0)
    out[...] = jnp.zeros_like(out)
    for p in range(5):
        both = sums[32 * p : 32 * p + 16, :] + sums[32 * p + 16 : 32 * p + 32, :]
        out[HEADS * p : HEADS * p + HEADS, :] = both[:HEADS]


def table_gradient(dscore, index):
    return pl.pallas_call(
        table_sum,
        out_shape=jax.ShapeDtypeStruct((64, 128), F32),
        in_specs=[VMEM] * 2,
        out_specs=VMEM,
        scratch_shapes=[pltpu.VMEM((160, 128), F32), pltpu.VMEM((WT, 16, WT), F32)],
        compiler_params=PARAMS,
        name="table_sum",
    )(dscore, index)


def chip_order():
    return [(y_lo * 4 + x) * 16 + zy * 2 for y_lo in range(2) for x in range(4) for zy in range(8)]


def chip_groups():
    return [[d + core for d in chip_order()] for core in range(2)]


def core_swap():
    return [(d, d ^ 1) for d in range(128)]


def worker_pairs():
    return [(core * 64 + q, d + core) for core in range(2) for q, d in enumerate(chip_order())]


def exchanged(value, groups):
    return lax.all_to_all(value, BOTH, 0, 0, axis_index_groups=groups, tiled=True)


def around(value, axis, by):
    size = lax.axis_size(axis)
    return lax.ppermute(value, axis, [(i, (i + by) % size) for i in range(size)])


def diagonal(value, by):
    lat, lon = lax.axis_size("lat"), lax.axis_size("lon")
    return lax.ppermute(
        value,
        BOTH,
        [
            (a * lon + o, ((a + by) % lat) * lon + (o + by) % lon)
            for a in range(lat)
            for o in range(lon)
        ],
    )


def pack(x, c, east, south, corner):
    for i, tile in enumerate((x, c)):
        for k in range(SHIFT, TILE):
            east[i, SHIFT * (k - SHIFT) : SHIFT * (k - SHIFT) + SHIFT, :] = tile[k, 0:SHIFT, :]
        for n in range(SHIFT):
            south[i, INNER * n : INNER * n + INNER, :] = tile[n, SHIFT:TILE, :]
            corner[i, SHIFT * n : SHIFT * n + SHIFT, :] = tile[n, 0:SHIFT, :]


def edges_of(x, c):
    shapes = [(2, EDGE, D), (2, EDGE, D), (2, CORNER, D)]
    east, south, corner = pl.pallas_call(
        pack,
        out_shape=[jax.ShapeDtypeStruct(s, F32) for s in shapes],
        in_specs=[VMEM] * 2,
        out_specs=[VMEM] * 3,
        compiler_params=PARAMS,
        name="pack",
    )(x, c)
    return around(east, "lon", -1), around(south, "lat", -1), diagonal(corner, -1)


def unpack_edges(local, west, north, corner, out):
    out[SHIFT:TILE, SHIFT:TILE, :] = local[SHIFT:TILE, SHIFT:TILE, :]
    for k in range(SHIFT, TILE):
        out[k, 0:SHIFT, :] = west[SHIFT * (k - SHIFT) : SHIFT * (k - SHIFT) + SHIFT, :]
    for n in range(SHIFT):
        out[n, SHIFT:TILE, :] = north[INNER * n : INNER * n + INNER, :]
        out[n, 0:SHIFT, :] = corner[SHIFT * n : SHIFT * n + SHIFT, :]


def with_edges(local, west, north, corner):
    return pl.pallas_call(
        unpack_edges,
        out_shape=jax.ShapeDtypeStruct((TILE, TILE, D), F32),
        in_specs=[VMEM] * 4,
        out_specs=VMEM,
        compiler_params=PARAMS,
        name="unpack_edges",
    )(local, west, north, corner)


def merge(keep, came, line, line_came, out):
    for q in range(BATCH):
        rows = slice(q * OWN, q * OWN + OWN)
        out[q * BLOCK : q * BLOCK + OWN, :] = keep[rows, :] + came[rows, :]
        out[q * BLOCK + OWN : (q + 1) * BLOCK, :] = line[q : q + 1, :] + line_came[q : q + 1, :]


def merged(keep, came, line, line_came):
    halves = pl.BlockSpec((BATCH * OWN, 128), lambda i: (i, 0))
    lines = pl.BlockSpec((BATCH, 128), lambda i: (i, 0))
    return pl.pallas_call(
        merge,
        out_shape=jax.ShapeDtypeStruct((64 * BLOCK, 128), F32),
        grid=(64 // BATCH,),
        in_specs=[halves, halves, lines, lines],
        out_specs=pl.BlockSpec((BATCH * BLOCK, 128), lambda i: (i, 0)),
        compiler_params=PARAMS,
        name="merge",
    )(keep, came, line, line_came)


def adam(parts, weights, first, second, new, first_new, second_new, factor):
    total = parts[0:BLOCK, :]
    for q in range(1, 64):
        total = total + parts[q * BLOCK : q * BLOCK + BLOCK, :]
    total = total * factor
    grad, line = total[:OWN], total[OWN:]
    m = 0.9 * first[...] + 0.1 * grad
    s = 0.95 * second[...] + 0.05 * grad * grad
    first_new[...] = m
    second_new[...] = s
    fresh = weights[...] - 0.01 * m / (jnp.sqrt(s) + 1e-08)
    fresh = jnp.concatenate([fresh, line], axis=0)
    for q in range(64):
        new[q * BLOCK : q * BLOCK + BLOCK, :] = fresh


def lay_out(place, blocks, *refs):
    out = refs[-1]
    for q in range(BATCH):
        out[q * OWN : q * OWN + OWN, :] = blocks[q * BLOCK : q * BLOCK + OWN, :]


def lay_out_own(place, blocks, out, lines):
    lay_out(place, blocks, out)
    for q in range(BATCH):
        lines[q : q + 1, :] = blocks[q * BLOCK + OWN : q * BLOCK + BLOCK, :]


def own_half(place, blocks):
    steps = 64 // BATCH
    return pl.pallas_call(
        lay_out_own,
        out_shape=[jax.ShapeDtypeStruct((ROWS, 128), F32), jax.ShapeDtypeStruct((64, 128), F32)],
        grid_spec=pltpu.PrefetchScalarGridSpec(
            num_scalar_prefetch=1,
            grid=(steps,),
            in_specs=[pl.BlockSpec((BATCH * BLOCK, 128), lambda i, spot: (i, 0))],
            out_specs=[
                pl.BlockSpec((BATCH * OWN, 128), lambda i, spot: (spot[0] * steps + i, 0)),
                pl.BlockSpec((BATCH, 128), lambda i, spot: (i, 0)),
            ],
        ),
        compiler_params=PARAMS,
        name="lay_out_own",
    )(place, blocks)


def other_half(place, blocks, so_far):
    steps = 64 // BATCH
    return pl.pallas_call(
        lay_out,
        out_shape=jax.ShapeDtypeStruct((ROWS, 128), F32),
        grid_spec=pltpu.PrefetchScalarGridSpec(
            num_scalar_prefetch=1,
            grid=(steps,),
            in_specs=[
                pl.BlockSpec((BATCH * BLOCK, 128), lambda i, spot: (i, 0)),
                pl.BlockSpec(memory_space=pl.ANY),
            ],
            out_specs=pl.BlockSpec((BATCH * OWN, 128), lambda i, spot: ((1 - spot[0]) * steps + i, 0)),
        ),
        input_output_aliases={2: 0},
        compiler_params=PARAMS,
        name="lay_out_other",
    )(place, blocks, so_far)


def per_device(
    block_input, cotangent, weights, first_moment, second_moment, bias_table, bias_index, region_ids
):
    lat_at, lon_at = lax.axis_index("lat"), lax.axis_index("lon")
    factor = 1.0 / math.sqrt(TOK * 128)
    flat = weights.reshape(ROWS, 128)
    bias = bias_of_pairs(bias_table, bias_index)
    edges = edges_of(block_input, cotangent)
    pairs_of = worker_pairs()
    moments = jnp.stack([first_moment.reshape(OWN, 128), second_moment.reshape(OWN, 128)])
    moments = lax.ppermute(moments, BOTH, pairs_of)
    *edges, moments = lax.optimization_barrier((*edges, moments))
    core = lon_at % 2
    place = jnp.stack([core, (lat_at == 7).astype(jnp.int32)]).astype(jnp.int32)
    keep, send, dscore, x, grad, dqkv = run_block(
        (block_input, cotangent), edges, flat, bias, region_ids, place
    )
    came = lax.ppermute(send, BOTH, core_swap())
    line = table_gradient(dscore, bias_index)
    line_came = lax.ppermute(line, BOTH, core_swap())
    summed = merged(keep, came, line, line_came)
    parts = exchanged(summed.reshape(64, 1, BLOCK * 128), chip_groups())

    _, dqkv = lax.optimization_barrier((summed, dqkv))
    o_l, o_e, o_s, o_c = run_input_grad(x, grad, dqkv, flat)
    from_west = around(o_e, "lon", 1)
    from_north = around(o_s, "lat", 1)
    from_corner = diagonal(o_c, 1)
    parts, from_west, from_north, from_corner = lax.optimization_barrier(
        (parts, from_west, from_north, from_corner)
    )

    shard = core * 64 + lat_at * 8 + lon_at // 2
    own = lax.dynamic_slice_in_dim(flat, shard * OWN, OWN, 0)
    new, first_new, second_new = pl.pallas_call(
        functools.partial(adam, factor=factor),
        out_shape=[jax.ShapeDtypeStruct((n, 128), F32) for n in (64 * BLOCK, OWN, OWN)],
        in_specs=[VMEM] * 4,
        out_specs=[VMEM] * 3,
        compiler_params=PARAMS,
        name="adam",
    )(parts.reshape(64 * BLOCK, 128), own, moments[0], moments[1])
    mine = exchanged(new.reshape(64, 1, BLOCK * 128), chip_groups())
    back = [(b, a) for a, b in pairs_of]
    moments = lax.ppermute(jnp.stack([first_new, second_new]), BOTH, back)
    grad_input = with_edges(o_l, from_west, from_north, from_corner)
    mine, grad_input = lax.optimization_barrier((mine, grad_input))

    mine = mine.reshape(64 * BLOCK, 128)
    theirs = lax.ppermute(mine, BOTH, core_swap())
    weights_new, table = own_half(place, mine)
    table_new = table[: HEADS * 5].reshape(5, HEADS, 128).transpose(1, 0, 2)
    table_new = table_new.reshape(HEADS, 640)[:, :BIAS]
    theirs, moments = lax.optimization_barrier((theirs, moments))
    weights_new = other_half(place, theirs, weights_new)
    return (
        grad_input,
        weights_new.reshape(-1),
        moments[0].reshape(-1),
        moments[1].reshape(-1),
        table_new,
    )


def solution(mesh):
    placed = (
        P("lat", "lon", None),
        P("lat", "lon", None),
        P(),
        P(BOTH),
        P(BOTH),
        P(),
        P(),
        P("lat", "lon"),
    )
    return jax.shard_map(
        per_device,
        mesh=mesh,
        in_specs=placed,
        out_specs=(P("lat", "lon", None), P(), P(BOTH), P(BOTH), P()),
        check_vma=False,
    )
```

```python
import functools
import math

import jax
import jax.numpy as jnp
from jax import lax
from jax.experimental import pallas as pl
from jax.experimental.pallas import tpu as pltpu
from jax.sharding import PartitionSpec as P

D = 384
HEADS = 12
FF = 1536
WIN = 12
SHIFT = 6
WT = WIN * WIN
TILE = 24
TOK = TILE * TILE
WINS = TOK // WT
GROUPS = 3
PER = 4
QKV_ROWS = D * 3 * D // 128
PROJ_ROWS = D * D // 128
MLP_ROWS = D * FF // 128
PROJ_AT = QKV_ROWS
UP_AT = QKV_ROWS + PROJ_ROWS
DOWN_AT = UP_AT + MLP_ROWS
ROWS = DOWN_AT + MLP_ROWS
CHUNK = 256
CHUNKS = FF // CHUNK
HALF = ROWS // 2
OWN = ROWS // 128
BLOCK = OWN + 1
BATCH = 32
BIAS = 529
BOTH = ("lat", "lon")
F32 = jnp.float32
BF16 = jnp.bfloat16
VMEM = pl.BlockSpec(memory_space=pltpu.VMEM)
PARAMS = pltpu.CompilerParams(vmem_limit_bytes=58 * 1024 * 1024)

NN = (((1,), (0,)), ((), ()))
NT = (((1,), (1,)), ((), ()))
TN = (((0,), (0,)), ((), ()))


def split(value):
    high = value.astype(BF16)
    return high, (value - high.astype(F32)).astype(BF16)


def dot(a, b, dims):
    return lax.dot_general(a, b, dims, preferred_element_type=F32)


def dot3(a, b, dims):
    return dot(a[0], b[0], dims) + dot(a[0], b[1], dims) + dot(a[1], b[0], dims)


def dot3_deep(a, b, dims):
    (x,), (y,) = dims[0]
    left = jnp.concatenate([a[0], a[0], a[1]], axis=x)
    right = jnp.concatenate([b[0], b[1], b[0]], axis=y)
    return dot(left, right, dims)


def dot3_wide(a, b, dims):
    wide = dot(a[0], jnp.concatenate([b[0], b[1]], axis=1), dims)
    return wide[:, :128] + wide[:, 128:] + dot(a[1], b[0], dims)


def unit(value):
    center = value - jnp.mean(value, axis=-1, keepdims=True)
    scale = lax.rsqrt(jnp.mean(center * center, axis=-1, keepdims=True) + 1e-05)
    return center * scale, scale


def unit_back(grad, normed, scale):
    mean = jnp.mean(grad, axis=-1, keepdims=True)
    along = jnp.mean(grad * normed, axis=-1, keepdims=True)
    return scale * (grad - mean - normed * along)


STEPS = 6


def prepare(qkv, proj, up, down, table, index, wq_h, wq_l, wp_h, wp_l, wu_h, wu_l, wd_h, wd_l, bias):
    for flat, rows, blocks, high, low in (
        (qkv, D // STEPS, 9, wq_h, wq_l),
        (proj, D // STEPS, 3, wp_h, wp_l),
        (down, FF // STEPS, 3, wd_h.at[0], wd_l.at[0]),
    ):
        for b in range(blocks):
            h, l = split(flat[pl.ds(b, rows, stride=blocks), :])
            high[:, 128 * b : 128 * b + 128] = h
            low[:, 128 * b : 128 * b + 128] = l
    for f in range(CHUNKS):
        for b in range(2):
            h, l = split(up[pl.ds(2 * f + b, D // STEPS, stride=12), :])
            wu_h[f, :, 128 * b : 128 * b + 128] = h
            wu_l[f, :, 128 * b : 128 * b + 128] = l
    lines = jnp.concatenate([table[...], jnp.zeros((HEADS, 640 - BIAS), F32)], axis=1)
    for k in range(WT // 8 // STEPS):
        at = pl.multiple_of((pl.program_id(0) * (WT // 8 // STEPS) + k) * 8, 8)
        columns = index[pl.ds(at, 8), :]
        columns = jnp.concatenate([columns, jnp.zeros((8, 256 - WT), jnp.int32)], axis=1)
        low = columns & 127
        part = columns >> 7
        for h in range(HEADS):
            found = jnp.zeros((8, 256), F32)
            for p in range(5):
                line = jnp.broadcast_to(lines[h : h + 1, 128 * p : 128 * p + 128], (8, 128))
                taken = jnp.concatenate(
                    [
                        jnp.take_along_axis(line, low[:, :128], axis=1),
                        jnp.take_along_axis(line, low[:, 128:], axis=1),
                    ],
                    axis=1,
                )
                found = jnp.where(part == p, taken, found)
            bias[h // PER, pl.ds(pl.multiple_of((h % PER) * WT + at, 8), 8), :] = found[:, :WT]


def prepared(flat, table, index):
    shapes = [(D, 3 * D)] * 2 + [(D, D)] * 2 + [(CHUNKS, D, CHUNK)] * 2 + [(CHUNKS, CHUNK, D)] * 2
    piece = D // STEPS
    outs = [
        *[pl.BlockSpec((piece, 3 * D), lambda i: (i, 0))] * 2,
        *[pl.BlockSpec((piece, D), lambda i: (i, 0))] * 2,
        *[pl.BlockSpec((CHUNKS, piece, CHUNK), lambda i: (0, i, 0))] * 2,
        *[pl.BlockSpec((1, CHUNK, D), lambda i: (i, 0, 0))] * 2,
        pl.BlockSpec((GROUPS, PER * WT, WT), lambda i: (0, 0, 0)),
    ]

    def part(at, rows):
        return pl.BlockSpec((rows // STEPS, 128), lambda i: (at * STEPS // rows + i, 0))

    return pl.pallas_call(
        prepare,
        out_shape=[jax.ShapeDtypeStruct(s, BF16) for s in shapes]
        + [jax.ShapeDtypeStruct((GROUPS, PER * WT, WT), F32)],
        grid=(STEPS,),
        in_specs=[
            part(0, QKV_ROWS),
            part(PROJ_AT, PROJ_ROWS),
            part(UP_AT, MLP_ROWS),
            part(DOWN_AT, MLP_ROWS),
            pl.BlockSpec((HEADS, BIAS), lambda i: (0, 0)),
            pl.BlockSpec((WT, WT), lambda i: (0, 0)),
        ],
        out_specs=outs,
        compiler_params=PARAMS,
        name="prepare",
    )(flat, flat, flat, flat, table, index)


INNER = TILE - SHIFT
EDGE = 112
CORNER = 40


def window_rows():
    for wr in range(2):
        for wc in range(2):
            for r in range(WIN):
                yield (wr * 2 + wc) * WT + r * WIN, wc, wr * WIN + r


def gather_windows(target, local, east, south, corner):
    for at, wc, row in window_rows():
        k, n = row + SHIFT, row - INNER
        if wc == 0:
            target[at : at + WIN, :] = (
                local[k, SHIFT : SHIFT + WIN, :] if n < 0 else south[INNER * n : INNER * n + WIN, :]
            )
        else:
            target[at : at + SHIFT, :] = (
                local[k, SHIFT + WIN : TILE, :] if n < 0 else south[INNER * n + WIN : INNER * n + INNER, :]
            )
            target[at + SHIFT : at + WIN, :] = (
                east[SHIFT * row : SHIFT * row + SHIFT, :] if n < 0 else corner[SHIFT * n : SHIFT * n + SHIFT, :]
            )


def scatter_windows(source, local, east, south, corner):
    for at, wc, row in window_rows():
        k, n = row + SHIFT, row - INNER
        near = source[at : at + (WIN if wc == 0 else SHIFT), :]
        if n < 0:
            first = SHIFT if wc == 0 else SHIFT + WIN
            local[k, first : first + near.shape[0], :] = near
        else:
            first = INNER * n + (0 if wc == 0 else WIN)
            south[first : first + near.shape[0], :] = near
        if wc == 1:
            far = source[at + SHIFT : at + WIN, :]
            if n < 0:
                east[SHIFT * row : SHIFT * row + SHIFT, :] = far
            else:
                corner[SHIFT * n : SHIFT * n + SHIFT, :] = far


def head_lane():
    return lax.broadcasted_iota(jnp.int32, (WT, 128), 1) >> 5


def stacked(value):
    lane = head_lane()
    return jnp.concatenate([jnp.where(lane == h, value, 0.0) for h in range(PER)], axis=0)


def unstacked(value):
    lane = head_lane()
    total = jnp.where(lane == 0, value[:WT], 0.0)
    for h in range(1, PER):
        total = jnp.where(lane == h, value[h * WT : h * WT + WT], total)
    return total


def find_labels(region, last, label_row, label_col):
    eye = lax.broadcasted_iota(jnp.int32, (WT, WT), 0) == lax.broadcasted_iota(jnp.int32, (WT, WT), 1)
    for wr in range(2):
        for wc in range(2):
            w = wr * 2 + wc
            pieces = []
            for r in range(WIN):
                row = wr * WIN + r
                ids = region[row : row + 1, wc * WIN : wc * WIN + WIN]
                pieces.append(ids + (4 * last if row >= TILE - SHIFT else 0))
            line = jnp.concatenate(pieces, axis=1).astype(F32)
            label_row[w] = line
            wide = jnp.where(eye, jnp.broadcast_to(line, (WT, WT)), 0.0)
            label_col[w] = jnp.sum(wide, axis=1, keepdims=True)


SCALE = 1.0 / math.sqrt(32.0)


def block_pass(
    x_l, c_l, east, south, corner, region, place, *rest
):
    stored, rest = rest[:9], rest[9:]
    (
    keep, send, dscore, x_out, grad_out, dqkv_out,
    x, cot, qkv, ctx, prob, n2h, n2l, ch, cl, grad, dqkv, dctx, grads, label_row, label_col, norm2, scale2, sems,
    ) = rest[:-9]
    held = rest[-9:]
    wq_h, wq_l, wp_h, wp_l, wu_h, wu_l, wd_h, wd_l, bias = held
    loads = [pltpu.make_async_copy(a, b, sems.at[i]) for i, (a, b) in enumerate(zip(stored, held))]
    for i in (0, 1, 8, 2, 3, 4, 5, 6, 7):
        loads[i].start()
    core = place[0]

    def piece(i, half, start, rows):
        source = grads.at[pl.ds(start, rows)]
        spot = pl.ds(start - half * HALF, rows)
        for target, here in ((keep, core == half), (send, core != half)):
            yield here, pltpu.make_async_copy(source, target.at[spot], sems.at[9 + i])

    def start(*what):
        for here, copy in piece(*what):
            pl.when(here)(copy.start)

    def finish(*what):
        for here, copy in piece(*what):
            pl.when(here)(copy.wait)

    pieces = (
        (0, 1, HALF, HALF),
        (1, 0, UP_AT, HALF - UP_AT),
        (2, 0, 0, UP_AT),
    )
    find_labels(region, place[1], label_row, label_col)
    gather_windows(x, x_l, east.at[0], south.at[0], corner.at[0])
    kept = [
        pltpu.make_async_copy(a, b, sems.at[12 + i])
        for i, (a, b) in enumerate(((x, x_out), (grad, grad_out), (dqkv, dqkv_out)))
    ]
    kept[0].start()
    gather_windows(cot, c_l, east.at[1], south.at[1], corner.at[1])
    n1 = split(unit(x[...])[0])
    loads[0].wait()
    loads[1].wait()
    qkv[...] = dot3_deep(n1, (wq_h[...], wq_l[...]), NN)

    loads[8].wait()

    def attend(step, carry):
        w, g = step // GROUPS, step % GROUPS
        rows = pl.ds(pl.multiple_of(w * WT, 16), WT)
        lanes = pl.ds(pl.multiple_of(g * 128, 128), 128)
        q = split(stacked(qkv[rows, pl.ds(pl.multiple_of(g * 128, 128), 128)] * SCALE))
        k = split(qkv[rows, pl.ds(pl.multiple_of(D + g * 128, 128), 128)])
        v = split(qkv[rows, pl.ds(pl.multiple_of(2 * D + g * 128, 128), 128)])
        allowed = label_col[w] == label_row[w]
        score = dot3_deep(q, k, NT) + bias[g]
        score = jnp.where(jnp.concatenate([allowed] * PER, axis=0), score, -jnp.inf)
        raised = jnp.exp(score - jnp.max(score, axis=-1, keepdims=True))
        p = raised * (1.0 / jnp.sum(raised, axis=-1, keepdims=True))
        prob[step] = p
        ctx[rows, lanes] = unstacked(dot3_wide(split(p), v, NN))
        return carry

    lax.fori_loop(0, WINS * GROUPS, attend, 0, unroll=12)

    for i in range(2, 8):
        loads[i].wait()
    mixed = x[...] + dot3_deep(split(ctx[...]), (wp_h[...], wp_l[...]), NN)
    norm2[...], scale2[...] = unit(mixed)
    n2h[...], n2l[...] = split(norm2[...])
    ch[...], cl[...] = split(cot[...])
    grad[...] = jnp.zeros_like(grad)

    def feed(f, carry):
        n = (n2h[...], n2l[...])
        c = (ch[...], cl[...])
        up = (wu_h[f], wu_l[f])
        u = dot3_deep(n, up, NN)
        back = dot3_deep(c, (wd_h[f], wd_l[f]), NT)
        inner = 0.7978845608028654 * (u + 0.044715 * u * u * u)
        t = jnp.tanh(inner)
        hidden = split(0.5 * u * (1.0 + t))
        slope = 0.5 * (1.0 + t) + 0.5 * u * (1.0 - t * t) * (
            0.7978845608028654 * (1.0 + 3.0 * 0.044715 * u * u)
        )
        du = split(back * slope)
        gdown = dot3_deep(hidden, c, TN)
        for b in range(3):
            grads[pl.ds(DOWN_AT + 3 * CHUNK * f + b, CHUNK, stride=3), :] = gdown[:, 128 * b : 128 * b + 128]
        gup = dot3_deep(n, du, TN)
        for b in range(2):
            grads[pl.ds(UP_AT + 2 * f + b, D, stride=12), :] = gup[:, 128 * b : 128 * b + 128]
        grad[...] += dot3_deep(du, up, NT)
        return carry

    lax.fori_loop(0, CHUNKS, feed, 0)

    start(*pieces[0])
    start(*pieces[1])
    grad[...] = cot[...] + unit_back(grad[...], norm2[...], scale2[...])
    kept[1].start()
    gm = split(grad[...])
    dctx[...] = dot3_deep(gm, (wp_h[...], wp_l[...]), NT)
    gproj = dot3_deep(split(ctx[...]), gm, TN)
    for b in range(3):
        grads[pl.ds(PROJ_AT + b, D, stride=3), :] = gproj[:, 128 * b : 128 * b + 128]
    dscore[...] = jnp.zeros_like(dscore)

    def attend_back(step, carry):
        w, g = step // GROUPS, step % GROUPS
        rows = pl.ds(pl.multiple_of(w * WT, 16), WT)
        q_at = pl.ds(pl.multiple_of(g * 128, 128), 128)
        k_at = pl.ds(pl.multiple_of(D + g * 128, 128), 128)
        v_at = pl.ds(pl.multiple_of(2 * D + g * 128, 128), 128)
        q = split(stacked(qkv[rows, q_at] * SCALE))
        k = split(qkv[rows, k_at])
        v = split(qkv[rows, v_at])
        d = split(stacked(dctx[rows, q_at]))
        p = prob[step]
        dp = dot3_deep(d, v, NT)
        ds = p * (dp - jnp.sum(dp * p, axis=-1, keepdims=True))
        dscore[g] += ds
        ps, dss = split(p), split(ds)
        dqkv[rows, v_at] = dot3_wide(ps, d, TN)
        dqkv[rows, q_at] = unstacked(dot3_wide(dss, k, NN)) * SCALE
        dqkv[rows, k_at] = dot3_wide(dss, q, TN)
        return carry

    lax.fori_loop(0, WINS * GROUPS, attend_back, 0, unroll=12)

    kept[2].start()
    dq = split(dqkv[...])
    gqkv = dot3_deep(split(unit(x[...])[0]), dq, TN)
    for b in range(9):
        grads[pl.ds(b, D, stride=9), :] = gqkv[:, 128 * b : 128 * b + 128]
    start(*pieces[2])
    for copy in kept:
        copy.wait()
    for what in pieces:
        finish(*what)


def input_grad(x, grad, dqkv, wq_h, wq_l, o_l, o_e, o_s, o_c, total):
    n1, scale1 = unit(x[...])
    back = dot3_deep(split(dqkv[...]), (wq_h[...], wq_l[...]), NT)
    total[...] = grad[...] + unit_back(back, n1, scale1)
    scatter_windows(total, o_l, o_e, o_s, o_c)


def run_input_grad(x, grad, dqkv, wq_h, wq_l):
    halo = [(TILE, TILE, D), (EDGE, D), (EDGE, D), (CORNER, D)]
    return pl.pallas_call(
        input_grad,
        out_shape=[jax.ShapeDtypeStruct(s, F32) for s in halo],
        in_specs=[VMEM] * 5,
        out_specs=[VMEM] * 4,
        scratch_shapes=[pltpu.VMEM((TOK, D), F32)],
        compiler_params=PARAMS,
        name="input_grad",
    )(x, grad, dqkv, wq_h, wq_l)


def run_block(tiles, edges, weights, bias, region, place):
    outs = [(HALF, 128), (HALF, 128), (GROUPS, PER * WT, WT), (TOK, D), (TOK, D), (TOK, 3 * D)]
    whole = pl.BlockSpec(memory_space=pl.ANY)
    scratch = [
        pltpu.VMEM((TOK, D), F32),
        pltpu.VMEM((TOK, D), F32),
        pltpu.VMEM((TOK, 3 * D), F32),
        pltpu.VMEM((TOK, D), F32),
        pltpu.VMEM((WINS * GROUPS, PER * WT, WT), F32),
        pltpu.VMEM((TOK, D), BF16),
        pltpu.VMEM((TOK, D), BF16),
        pltpu.VMEM((TOK, D), BF16),
        pltpu.VMEM((TOK, D), BF16),
        pltpu.VMEM((TOK, D), F32),
        pltpu.VMEM((TOK, 3 * D), F32),
        pltpu.VMEM((TOK, D), F32),
        pltpu.VMEM((ROWS, 128), F32),
        pltpu.VMEM((WINS, 1, WT), F32),
        pltpu.VMEM((WINS, WT, 1), F32),
        pltpu.VMEM((TOK, D), F32),
        pltpu.VMEM((TOK, 1), F32),
        pltpu.SemaphoreType.DMA((15,)),
        *[pltpu.VMEM(a.shape, a.dtype) for a in (*weights, bias)],
    ]
    args = (*tiles, *edges, region, place, *weights, bias)
    return pl.pallas_call(
        block_pass,
        out_shape=[jax.ShapeDtypeStruct(s, F32) for s in outs],
        in_specs=[VMEM] * 6 + [pl.BlockSpec(memory_space=pltpu.SMEM)] + [whole] * 9,
        out_specs=[whole] * 2 + [VMEM] + [whole] * 3,
        scratch_shapes=scratch,
        compiler_params=PARAMS,
        name="block_pass",
    )(*args)


def table_sum(by_head, index, out, sums, scores):
    sums[...] = jnp.zeros_like(sums)
    for h in range(16):
        if h < HEADS:
            scores[:, h, :] = by_head[h // PER, (h % PER) * WT : (h % PER) * WT + WT, :]
        else:
            scores[:, h, :] = jnp.zeros((WT, WT), F32)
    column = lax.broadcasted_iota(jnp.int32, (128, WT), 0)

    def one(i):
        line = index[pl.ds(i, 1), :]
        part = jnp.broadcast_to(line >> 7, (16, WT))
        hot = (column == jnp.broadcast_to(line & 127, (128, WT))).astype(F32).astype(BF16)
        high, low = split(scores[i])
        pieces = []
        for p in range(5):
            here = part == p
            pieces.append(jnp.where(here, high, jnp.zeros_like(high)))
            pieces.append(jnp.where(here, low, jnp.zeros_like(low)))
        return dot(jnp.concatenate(pieces, axis=0), hot, NT)

    def step(k, carry):
        at = 8 * k
        quads = [(one(at + i) + one(at + i + 1)) + (one(at + i + 2) + one(at + i + 3)) for i in (0, 4)]
        sums[...] += quads[0] + quads[1]
        return carry

    lax.fori_loop(0, WT // 8, step, 0)
    out[...] = jnp.zeros_like(out)
    for p in range(5):
        both = sums[32 * p : 32 * p + 16, :] + sums[32 * p + 16 : 32 * p + 32, :]
        out[HEADS * p : HEADS * p + HEADS, :] = both[:HEADS]


def table_gradient(dscore, index):
    return pl.pallas_call(
        table_sum,
        out_shape=jax.ShapeDtypeStruct((64, 128), F32),
        in_specs=[VMEM] * 2,
        out_specs=VMEM,
        scratch_shapes=[pltpu.VMEM((160, 128), F32), pltpu.VMEM((WT, 16, WT), F32)],
        compiler_params=PARAMS,
        name="table_sum",
    )(dscore, index)


def chip_order():
    return [(y_lo * 4 + x) * 16 + zy * 2 for y_lo in range(2) for x in range(4) for zy in range(8)]


def chip_groups():
    return [[d + core for d in chip_order()] for core in range(2)]


def core_swap():
    return [(d, d ^ 1) for d in range(128)]


def worker_pairs():
    return [(core * 64 + q, d + core) for core in range(2) for q, d in enumerate(chip_order())]


def exchanged(value, groups):
    return lax.all_to_all(value, BOTH, 0, 0, axis_index_groups=groups, tiled=True)


def around(value, axis, by):
    size = lax.axis_size(axis)
    return lax.ppermute(value, axis, [(i, (i + by) % size) for i in range(size)])


def diagonal(value, by):
    lat, lon = lax.axis_size("lat"), lax.axis_size("lon")
    return lax.ppermute(
        value,
        BOTH,
        [
            (a * lon + o, ((a + by) % lat) * lon + (o + by) % lon)
            for a in range(lat)
            for o in range(lon)
        ],
    )


def pack(x, c, east, south, corner):
    for i, tile in enumerate((x, c)):
        for k in range(SHIFT, TILE):
            east[i, SHIFT * (k - SHIFT) : SHIFT * (k - SHIFT) + SHIFT, :] = tile[k, 0:SHIFT, :]
        for n in range(SHIFT):
            south[i, INNER * n : INNER * n + INNER, :] = tile[n, SHIFT:TILE, :]
            corner[i, SHIFT * n : SHIFT * n + SHIFT, :] = tile[n, 0:SHIFT, :]


def edges_of(x, c):
    shapes = [(2, EDGE, D), (2, EDGE, D), (2, CORNER, D)]
    east, south, corner = pl.pallas_call(
        pack,
        out_shape=[jax.ShapeDtypeStruct(s, F32) for s in shapes],
        in_specs=[VMEM] * 2,
        out_specs=[VMEM] * 3,
        compiler_params=PARAMS,
        name="pack",
    )(x, c)
    return around(east, "lon", -1), around(south, "lat", -1), diagonal(corner, -1)


def unpack_edges(local, west, north, corner, out):
    out[SHIFT:TILE, SHIFT:TILE, :] = local[SHIFT:TILE, SHIFT:TILE, :]
    for k in range(SHIFT, TILE):
        out[k, 0:SHIFT, :] = west[SHIFT * (k - SHIFT) : SHIFT * (k - SHIFT) + SHIFT, :]
    for n in range(SHIFT):
        out[n, SHIFT:TILE, :] = north[INNER * n : INNER * n + INNER, :]
        out[n, 0:SHIFT, :] = corner[SHIFT * n : SHIFT * n + SHIFT, :]


def with_edges(local, west, north, corner):
    return pl.pallas_call(
        unpack_edges,
        out_shape=jax.ShapeDtypeStruct((TILE, TILE, D), F32),
        in_specs=[VMEM] * 4,
        out_specs=VMEM,
        compiler_params=PARAMS,
        name="unpack_edges",
    )(local, west, north, corner)


def merge(keep, came, line, line_came, out):
    for q in range(BATCH):
        rows = slice(q * OWN, q * OWN + OWN)
        out[q * BLOCK : q * BLOCK + OWN, :] = keep[rows, :] + came[rows, :]
        out[q * BLOCK + OWN : (q + 1) * BLOCK, :] = line[q : q + 1, :] + line_came[q : q + 1, :]


def merged(keep, came, line, line_came):
    halves = pl.BlockSpec((BATCH * OWN, 128), lambda i: (i, 0))
    lines = pl.BlockSpec((BATCH, 128), lambda i: (i, 0))
    return pl.pallas_call(
        merge,
        out_shape=jax.ShapeDtypeStruct((64 * BLOCK, 128), F32),
        grid=(64 // BATCH,),
        in_specs=[halves, halves, lines, lines],
        out_specs=pl.BlockSpec((BATCH * BLOCK, 128), lambda i: (i, 0)),
        compiler_params=PARAMS,
        name="merge",
    )(keep, came, line, line_came)


def adam(parts, weights, first, second, new, first_new, second_new, factor):
    total = parts[0:BLOCK, :]
    for q in range(1, 64):
        total = total + parts[q * BLOCK : q * BLOCK + BLOCK, :]
    total = total * factor
    grad, line = total[:OWN], total[OWN:]
    m = 0.9 * first[...] + 0.1 * grad
    s = 0.95 * second[...] + 0.05 * grad * grad
    first_new[...] = m
    second_new[...] = s
    fresh = weights[...] - 0.01 * m / (jnp.sqrt(s) + 1e-08)
    fresh = jnp.concatenate([fresh, line], axis=0)
    for q in range(64):
        new[q * BLOCK : q * BLOCK + BLOCK, :] = fresh


def lay_out(place, blocks, *refs):
    out = refs[-1]
    for q in range(BATCH):
        out[q * OWN : q * OWN + OWN, :] = blocks[q * BLOCK : q * BLOCK + OWN, :]


def lay_out_own(place, blocks, out, lines):
    lay_out(place, blocks, out)
    for q in range(BATCH):
        lines[q : q + 1, :] = blocks[q * BLOCK + OWN : q * BLOCK + BLOCK, :]


def own_half(place, blocks):
    steps = 64 // BATCH
    return pl.pallas_call(
        lay_out_own,
        out_shape=[jax.ShapeDtypeStruct((ROWS, 128), F32), jax.ShapeDtypeStruct((64, 128), F32)],
        grid_spec=pltpu.PrefetchScalarGridSpec(
            num_scalar_prefetch=1,
            grid=(steps,),
            in_specs=[pl.BlockSpec((BATCH * BLOCK, 128), lambda i, spot: (i, 0))],
            out_specs=[
                pl.BlockSpec((BATCH * OWN, 128), lambda i, spot: (spot[0] * steps + i, 0)),
                pl.BlockSpec((BATCH, 128), lambda i, spot: (i, 0)),
            ],
        ),
        compiler_params=PARAMS,
        name="lay_out_own",
    )(place, blocks)


def other_half(place, blocks, so_far):
    steps = 64 // BATCH
    return pl.pallas_call(
        lay_out,
        out_shape=jax.ShapeDtypeStruct((ROWS, 128), F32),
        grid_spec=pltpu.PrefetchScalarGridSpec(
            num_scalar_prefetch=1,
            grid=(steps,),
            in_specs=[
                pl.BlockSpec((BATCH * BLOCK, 128), lambda i, spot: (i, 0)),
                pl.BlockSpec(memory_space=pl.ANY),
            ],
            out_specs=pl.BlockSpec((BATCH * OWN, 128), lambda i, spot: ((1 - spot[0]) * steps + i, 0)),
        ),
        input_output_aliases={2: 0},
        compiler_params=PARAMS,
        name="lay_out_other",
    )(place, blocks, so_far)


def per_device(
    block_input, cotangent, weights, first_moment, second_moment, bias_table, bias_index, region_ids
):
    lat_at, lon_at = lax.axis_index("lat"), lax.axis_index("lon")
    factor = 1.0 / math.sqrt(TOK * 128)
    flat = weights.reshape(ROWS, 128)
    *pairs, bias = prepared(flat, bias_table, bias_index)
    edges = edges_of(block_input, cotangent)
    core = lon_at % 2
    place = jnp.stack([core, (lat_at == 7).astype(jnp.int32)]).astype(jnp.int32)
    keep, send, dscore, x, grad, dqkv = run_block(
        (block_input, cotangent), edges, pairs, bias, region_ids, place
    )
    came = lax.ppermute(send, BOTH, core_swap())
    line = table_gradient(dscore, bias_index)
    line_came = lax.ppermute(line, BOTH, core_swap())
    summed = merged(keep, came, line, line_came)
    parts = exchanged(summed.reshape(64, 1, BLOCK * 128), chip_groups())

    _, dqkv, first_moment, second_moment = lax.optimization_barrier(
        (summed, dqkv, first_moment, second_moment)
    )
    o_l, o_e, o_s, o_c = run_input_grad(x, grad, dqkv, pairs[0], pairs[1])
    from_west = around(o_e, "lon", 1)
    from_north = around(o_s, "lat", 1)
    from_corner = diagonal(o_c, 1)
    pairs_of = worker_pairs()
    moments = jnp.stack([first_moment.reshape(OWN, 128), second_moment.reshape(OWN, 128)])
    moments = lax.ppermute(moments, BOTH, pairs_of)
    parts, from_west, from_north, from_corner, moments = lax.optimization_barrier(
        (parts, from_west, from_north, from_corner, moments)
    )

    shard = core * 64 + lat_at * 8 + lon_at // 2
    own = lax.dynamic_slice_in_dim(flat, shard * OWN, OWN, 0)
    new, first_new, second_new = pl.pallas_call(
        functools.partial(adam, factor=factor),
        out_shape=[jax.ShapeDtypeStruct((n, 128), F32) for n in (64 * BLOCK, OWN, OWN)],
        in_specs=[VMEM] * 4,
        out_specs=[VMEM] * 3,
        compiler_params=PARAMS,
        name="adam",
    )(parts.reshape(64 * BLOCK, 128), own, moments[0], moments[1])
    mine = exchanged(new.reshape(64, 1, BLOCK * 128), chip_groups())
    back = [(b, a) for a, b in pairs_of]
    moments = lax.ppermute(jnp.stack([first_new, second_new]), BOTH, back)
    grad_input = with_edges(o_l, from_west, from_north, from_corner)
    mine, moments, grad_input = lax.optimization_barrier((mine, moments, grad_input))

    mine = mine.reshape(64 * BLOCK, 128)
    theirs = lax.ppermute(mine, BOTH, core_swap())
    weights_new, table = own_half(place, mine)
    table_new = table[: HEADS * 5].reshape(5, HEADS, 128).transpose(1, 0, 2)
    table_new = table_new.reshape(HEADS, 640)[:, :BIAS]
    weights_new = other_half(place, theirs, weights_new)
    return (
        grad_input,
        weights_new.reshape(-1),
        moments[0].reshape(-1),
        moments[1].reshape(-1),
        table_new,
    )


def solution(mesh):
    placed = (
        P("lat", "lon", None),
        P("lat", "lon", None),
        P(),
        P(BOTH),
        P(BOTH),
        P(),
        P(),
        P("lat", "lon"),
    )
    return jax.shard_map(
        per_device,
        mesh=mesh,
        in_specs=placed,
        out_specs=(P("lat", "lon", None), P(), P(BOTH), P(BOTH), P()),
        check_vma=False,
    )
```
